32 devices in a mesh: groups: 2 (over y), seq: 8 (over z, x), dp: 2 (over core).
Axes of the slice: x: 2, y: 2, z: 4, core: 2. Of those that a mesh axis runs over, the one named last changes fastest.
Arguments:
- x_input: bfloat16 [6144, 4096], P(('groups', 'seq'), 'dp'), parts along dimension 0, may hold values from -6 to 6
- b_input: bfloat16 [6144, 512], P(('groups', 'seq'), 'dp'), parts along dimension 0, may hold values from -6 to 6
- c_input: bfloat16 [6144, 512], P(('groups', 'seq'), 'dp'), parts along dimension 0, may hold values from -6 to 6
- dt_input: float32 [6144, 64], P(('groups', 'seq'), 'dp'), parts along dimension 0, may hold values from -4 to 4
- decay_rate: float32 [64], P('dp'), may hold values from 0 to 1
- gate_input: bfloat16 [6144, 4096], P(('groups', 'seq'), 'dp'), parts along dimension 0, may hold values from -24 to 24
- taps_x: float32 [4, 4096], P(None, 'dp'), may hold values from -3 to 3
- taps_b: float32 [4, 512], P(None, 'dp'), may hold values from -3 to 3
- taps_c: float32 [4, 512], P(None, 'dp'), may hold values from -3 to 3
- norm_gain: float32 [4096], P('dp'), may hold values from 0.5 to 1.5
- doc_lengths: int32 [8], P('groups'), parts along dimension 0, may hold values from 1 to 2304, as said below
Outputs:
- mixed: bfloat16 [6144, 4096], P(('groups', 'seq'), 'dp'), parts along dimension 0
The draws below stay inside these ranges and needn't reach their ends.
There are 2 independent parts, one for each index of `groups`. The reference program is written for one: setup_inputs(seed, part) draws one part's arguments, and reference() takes and returns one part's arrays. A program takes and returns all parts, laid end to end along the dimension named above; an argument that names none is the same for every part. Nothing has to cross between parts.
Inputs may be any that keep to these rules, and one draw needn't show every extreme that they name: `doc_lengths`: the 4 lengths sum to 3072; the second document is the longest, with exactly 2304 tokens.
All inputs are finite; a program needn't handle non-finite values.
Results may differ from the reference program's by a relative error of at most 0.005.
Values may be sent and summed in bfloat16 or wider, within the bound.
No kernel may reach another device: no remote copies, remote signals or barrier semaphores. Data moves between devices by JAX's collectives and lax.ppermute only.
A program may use at most 192 MiB of HBM per device.

```python
import math
import jax
import jax.numpy as jnp
from jax import lax

HEADS = 64
HEAD_DIM = 64
STATE = 128
GROUPS = 4
NORM_HEADS = 16
KW = 4
BLOCK = 384
NDOCS = 4
TOK_DEV = 384
TOKENS = 3072
CHANNELS = 4096
GN = 512


def draw_decay_rate(key, part):
    chooser_key, slow_key, fast_key = jax.random.split(key, 3)
    portion = 0.5
    chooser = jax.random.uniform(chooser_key, (HEADS,))
    slow_rate = jnp.exp(jax.random.uniform(slow_key, (HEADS,), minval=math.log(0.05 / TOKENS), maxval=math.log(1.0 / TOKENS)))
    fast_rate = jnp.exp(jax.random.uniform(fast_key, (HEADS,), minval=math.log(1.0 / 64), maxval=math.log(1.0 / 16)))
    return jnp.where(chooser < portion, slow_rate, fast_rate).astype(jnp.float32)


def draw_gate_input(key, part):
    noise_key, column_key, row_key = jax.random.split(key, 3)
    base_noise = jnp.clip(jax.random.normal(noise_key, (TOKENS, CHANNELS)), -4.0, 4.0)
    column_scale = jnp.exp(jax.random.uniform(column_key, (1, CHANNELS), minval=math.log(0.3), maxval=math.log(3.0)))
    row_scale = jnp.exp(jax.random.uniform(row_key, (TOKENS, 1), minval=math.log(0.5), maxval=math.log(2.0)))
    return (base_noise * column_scale * row_scale).astype(jnp.bfloat16)


def draw_dt_input(key, part):
    noise_key, offset_key = jax.random.split(key, 2)
    region_count = TOKENS // TOK_DEV
    base_noise = 0.7 * jnp.clip(jax.random.normal(noise_key, (TOKENS, HEADS)), -3.0, 3.0)
    offsets = jax.random.uniform(offset_key, (region_count, 1), minval=-3.0, maxval=2.0)
    spread_offsets = jnp.repeat(offsets, TOK_DEV, axis=0)
    return jnp.clip(base_noise + spread_offsets, -4.0, 4.0).astype(jnp.float32)


def draw_doc_lengths(key, part):
    rest = TOKENS // 4
    longest = TOKENS - rest
    picked = jax.random.permutation(jax.random.fold_in(key, 17), rest - 1)[:NDOCS - 2] + 1
    cuts = jnp.sort(picked.astype(jnp.int32))
    bounds = jnp.concatenate([jnp.zeros((1,), jnp.int32), cuts, jnp.full((1,), rest, jnp.int32)])
    short_docs = (bounds[1:] - bounds[:-1]).astype(jnp.int32)
    lengths = jnp.concatenate([short_docs[:1], jnp.full((1,), longest, jnp.int32), short_docs[1:]])
    return lengths.astype(jnp.int32)


def steps_of(key, dims, cuts, least, top_value):
    def one(position, blocks):
        draws = jax.random.uniform(jax.random.fold_in(jax.random.fold_in(key, 6), position), (blocks,), jnp.float32, least / len(cuts), top_value / len(cuts))
        return jnp.repeat(jnp.exp(draws), dims[position] // blocks).reshape((-1,) + (1,) * (len(dims) - position - 1))

    gain = one(*cuts[0])
    for cut in cuts[1:]:
        gain = gain * one(*cut)
    return gain


def centred(stream_key, shape, scale, limit, cuts=(), held_as=jnp.bfloat16):
    gain = steps_of(stream_key, shape, cuts, -0.22, 0.18) if cuts else 1.0
    drawn = jax.random.normal(stream_key, shape, jnp.float32) * scale * gain
    return jnp.minimum(jnp.maximum(drawn, -limit), limit).astype(held_as)


def setup_inputs(seed: int = 0, part: int = 0) -> dict:
    seeds = jax.random.split(jax.random.key(seed), 12)
    part_keys = jax.random.split(jax.random.fold_in(seeds[11], part), 12)
    x_input = centred(part_keys[0], (TOKENS, CHANNELS), 1.0, 6.0, ((0, 8), (1, 2)))
    b_input = centred(part_keys[1], (TOKENS, GN), 1.0, 6.0, ((0, 8), (1, 2)))
    c_input = centred(part_keys[2], (TOKENS, GN), 1.0, 6.0, ((0, 8), (1, 2)))
    dt_input = draw_dt_input(jax.random.fold_in(jax.random.fold_in(seeds[11], part), 71), part)
    decay_rate = draw_decay_rate(jax.random.fold_in(seeds[11], 71), part)
    gate_input = draw_gate_input(jax.random.fold_in(jax.random.fold_in(seeds[11], part), 71), part)
    taps_x = centred(seeds[6], (KW, CHANNELS), KW ** -0.5, 3.0, ((1, 2),), jnp.float32)
    taps_b = centred(seeds[7], (KW, GN), KW ** -0.5, 3.0, ((1, 2),), jnp.float32)
    taps_c = centred(seeds[8], (KW, GN), KW ** -0.5, 3.0, ((1, 2),), jnp.float32)
    norm_gain = jnp.clip(1.0 + 0.1 * jax.random.normal(seeds[9], (CHANNELS,), jnp.float32), 0.5, 1.5)
    doc_lengths = draw_doc_lengths(jax.random.fold_in(jax.random.fold_in(seeds[11], part), 71), part)
    return dict(x_input=x_input, b_input=b_input, c_input=c_input, dt_input=dt_input, decay_rate=decay_rate, gate_input=gate_input, taps_x=taps_x, taps_b=taps_b, taps_c=taps_c, norm_gain=norm_gain, doc_lengths=doc_lengths)


norm_eps = 1e-05

def doc_index(positions, doc_ends):
    return lax.optimization_barrier(jnp.sum((positions[:, None] >= doc_ends[None, :-1]).astype(jnp.int32), axis=1)).astype(jnp.int32)

def causal_conv(extended, doc_ext, doc_ids, weight, margin):
    row_count = doc_ids.shape[0]
    running = jnp.zeros((row_count, extended.shape[1]), jnp.float32)
    for offset in range(margin + 1):
        window = extended[offset:offset + row_count]
        same_doc = (doc_ext[offset:offset + row_count] == doc_ids)[:, None]
        running = running + jnp.where(same_doc, window * weight[offset][None, :], 0.0)
    return jax.nn.silu(running).astype(jnp.bfloat16)

def gated_norm(gated_rows, norm_gain, width):
    row_count = gated_rows.shape[0]
    grouped = gated_rows.reshape(row_count, -1, width)
    mean_sq = lax.optimization_barrier(jnp.mean(grouped * grouped, axis=-1, keepdims=True))
    scaled = (grouped * lax.rsqrt(mean_sq + norm_eps)).reshape(row_count, -1)
    return (scaled * norm_gain[None, :]).astype(jnp.bfloat16)

def reference(x_input, b_input, c_input, dt_input, decay_rate, gate_input, taps_x, taps_b, taps_c, norm_gain, doc_lengths):
    margin = KW - 1
    doc_ends = jnp.cumsum(doc_lengths).astype(jnp.int32)
    positions = jnp.arange(TOKENS, dtype=jnp.int32)
    doc_ids = doc_index(positions, doc_ends)
    doc_ext = jnp.concatenate([jnp.full((margin,), -1, jnp.int32), doc_ids])

    def convolve(values, weight):
        extended = jnp.concatenate([jnp.zeros((margin, values.shape[1]), values.dtype), values], 0).astype(jnp.float32)
        return causal_conv(extended, doc_ext, doc_ids, weight, margin)
    x_conv = convolve(x_input, taps_x)
    b_conv = convolve(b_input, taps_b)
    c_conv = convolve(c_input, taps_c)
    step_size = jax.nn.softplus(dt_input)
    log_decay = -(step_size * decay_rate[None, :])
    block_count = TOKENS // BLOCK
    per_group = HEADS // GROUPS
    prev_docs = jnp.concatenate([jnp.full((1,), -1, jnp.int32), doc_ids[BLOCK - 1::BLOCK][:-1].astype(jnp.int32)])

    def blocks(values):
        return values.reshape((block_count, BLOCK) + values.shape[1:])
    row_order = jnp.arange(BLOCK, dtype=jnp.int32)

    def advance(carry_state, inputs):
        x_blk, b_blk, c_blk, step_blk, log_blk, doc_blk, prev_doc, gate_blk = inputs
        cum_log = jnp.cumsum(log_blk, axis=0)
        b_groups = b_blk.reshape(BLOCK, GROUPS, STATE).astype(jnp.float32)
        c_groups = c_blk.reshape(BLOCK, GROUPS, STATE).astype(jnp.float32)
        b_heads = jnp.repeat(b_groups, per_group, axis=1)
        c_heads = jnp.repeat(c_groups, per_group, axis=1)
        scores = jnp.einsum('tgn,sgn->gts', c_groups, b_groups)
        score_heads = jnp.repeat(scores, per_group, axis=0)
        causal = (row_order[None, :] <= row_order[:, None]) & (doc_blk[:, None] == doc_blk[None, :])
        cum_heads = cum_log.T
        log_gap = cum_heads[:, :, None] - cum_heads[:, None, :]
        weights = (jnp.where(causal[None], jnp.exp(jnp.minimum(log_gap, 0.0)), 0.0) * step_blk.T[:, None, :] * score_heads).astype(jnp.bfloat16)
        weights = lax.optimization_barrier(weights).astype(jnp.float32)
        x_heads = x_blk.reshape(BLOCK, HEADS, HEAD_DIM).astype(jnp.float32)
        intra_out = jnp.einsum('hts,shp->thp', weights, x_heads)
        in_scale = jnp.exp(cum_log) * (doc_blk == prev_doc).astype(jnp.float32)[:, None]
        state_low = lax.optimization_barrier(carry_state.astype(jnp.bfloat16)).astype(jnp.float32)
        carried = jnp.einsum('thn,hnp->thp', c_heads, state_low) * in_scale[:, :, None]
        output = intra_out + carried
        end_weight = jnp.where((doc_blk == doc_blk[-1])[:, None], jnp.exp(cum_log[-1][None, :] - cum_log), 0.0) * step_blk
        x_weighted = (x_heads * end_weight[:, :, None]).astype(jnp.bfloat16)
        x_weighted = lax.optimization_barrier(x_weighted).astype(jnp.float32)
        state_block = jnp.einsum('shn,shp->hnp', b_heads, x_weighted)
        decay_block = jnp.exp(cum_log[-1]) * (doc_blk[-1] == prev_doc).astype(jnp.float32)
        new_state = decay_block[:, None, None] * carry_state + state_block
        gated_rows = output.reshape(BLOCK, CHANNELS) * jax.nn.silu(gate_blk.astype(jnp.float32))
        return (new_state, gated_norm(gated_rows, norm_gain, NORM_HEADS * HEAD_DIM))
    start_state = jnp.zeros((HEADS, STATE, HEAD_DIM), jnp.float32)
    inputs = (blocks(x_conv), blocks(b_conv), blocks(c_conv), blocks(step_size), blocks(log_decay), blocks(doc_ids), prev_docs, blocks(gate_input))
    final_state, normed = lax.scan(advance, start_state, inputs)
    return normed.reshape(TOKENS, CHANNELS)
```

```python
import functools

import jax
import jax.numpy as jnp
from jax import lax
from jax.experimental import pallas as pl
from jax.experimental.pallas import tpu as pltpu
from jax.sharding import PartitionSpec as P

STATE = 128
NORM_HEADS = 16
SUB = 128
CHUNK = 256
LANES = 128
ROWS = 32
LOG2E = 1.4426950408889634
norm_eps = 1e-05

F32 = jnp.float32
BF16 = jnp.bfloat16
VMEM = pl.BlockSpec(memory_space=pltpu.VMEM)
SMEM = pl.BlockSpec(memory_space=pltpu.SMEM)
ANY = pl.BlockSpec(memory_space=pl.ANY)


def params(mib=48):
    return pltpu.CompilerParams(vmem_limit_bytes=mib << 20)


def cost(flops, moved, transcendentals=0):
    return pl.CostEstimate(flops=flops, bytes_accessed=moved, transcendentals=transcendentals)


def doc_edges(dl_ref):
    edges = [0]
    for i in range(dl_ref.shape[0] - 1):
        edges.append(edges[-1] + dl_ref[i])
    return edges


def doc_start(token, edges):
    start = jnp.zeros_like(token)
    for edge in edges[1:]:
        start = jnp.where(token >= edge, jnp.maximum(start, edge), start)
    return start


def split2(value):
    high = value.astype(BF16)
    return high, (value - high.astype(F32)).astype(BF16)


def split3(value):
    high = value.astype(BF16)
    rest = value - high.astype(F32)
    mid = rest.astype(BF16)
    return high, mid, (rest - mid.astype(F32)).astype(BF16)


def mm(a, b):
    return jnp.dot(a, b, preferred_element_type=F32)


def spread(heads, chunk, width, head_dim):
    row = lax.broadcasted_iota(jnp.int32, (2 * heads, width), 0)
    lane = lax.broadcasted_iota(jnp.int32, (2 * heads, width), 1)
    head = jnp.where(row >= heads, row - heads, row)
    low = (head - chunk * (width // head_dim)) * head_dim
    return jnp.where((lane >= low) & (lane < low + head_dim), 1.0, 0.0).astype(BF16)


def prep_kernel(dl_ref, dt_ref, rate_ref, w_ref, u_ref, u0_ref, col_ref, row_ref, d_ref):
    tok, heads = dt_ref.shape
    row0 = lax.axis_index("seq") * tok
    edges = doc_edges(dl_ref)
    tri = jnp.where(
        lax.broadcasted_iota(jnp.int32, (SUB, SUB), 0) >= lax.broadcasted_iota(jnp.int32, (SUB, SUB), 1), 1.0, 0.0
    ).astype(BF16)
    total = jnp.zeros((1, heads), F32)
    decays = []
    for c in range(tok // SUB):
        rows = pl.ds(c * SUB, SUB)
        first = row0 + c * SUB
        dt = dt_ref[rows, :]
        step = jnp.maximum(dt, 0.0) + jnp.log1p(jnp.exp(-jnp.abs(dt)))
        parts = split3(-(step * rate_ref[...]))
        cum = mm(tri, parts[0]) + (mm(tri, parts[1]) + mm(tri, parts[2]))
        last = cum[SUB - 1 :, :]
        token = first + lax.broadcasted_iota(jnp.int32, (SUB, heads), 0)
        start = doc_start(token, edges)
        last_start = doc_start(jnp.int32(first + SUB - 1), edges)
        within = jnp.where(token >= last_start, 1.0, 0.0)
        w_ref[rows, :] = jnp.concatenate(split2(jnp.exp(last - cum) * step * within), 1)
        u_ref[rows, :] = jnp.concatenate(split2(jnp.exp(cum) * jnp.where(start < first, 1.0, 0.0)), 1)
        u0_ref[rows, :] = jnp.concatenate(split2(jnp.exp(cum + total) * jnp.where(start < row0, 1.0, 0.0)), 1)
        col_ref[rows, :] = cum * LOG2E
        row = (jnp.log(step) - cum) * LOG2E
        padded = jnp.concatenate([row, jnp.zeros((SUB, LANES - heads), F32)], 1)
        row_ref[:, c * SUB : (c + 1) * SUB] = padded.T[:heads]
        decays.append(jnp.exp(last) * jnp.where(last_start < first, 1.0, 0.0))
        total = total + last
    end_start = doc_start(jnp.int32(row0 + tok - 1), edges)
    whole = jnp.exp(total) * jnp.where(end_start < row0, 1.0, 0.0)
    high, mid, low = split3(whole)
    none = jnp.zeros((1, heads), BF16)
    table = [jnp.concatenate([part, none], 1) for part in (high, mid, low)]
    table += [jnp.concatenate(split2(decay), 1) for decay in decays[1:]]
    table += [jnp.concatenate([none, none], 1)] * (8 - len(table))
    d_ref[...] = jnp.concatenate([part.astype(F32) for part in table], 0).astype(BF16)


def prep(doc_lengths, dt_input, rate):
    tok, heads = dt_input.shape
    pair = jax.ShapeDtypeStruct((tok, 2 * heads), BF16)
    return pl.pallas_call(
        prep_kernel,
        out_shape=(
            pair,
            pair,
            pair,
            jax.ShapeDtypeStruct((tok, heads), F32),
            jax.ShapeDtypeStruct((heads, tok), F32),
            jax.ShapeDtypeStruct((8, 2 * heads), BF16),
        ),
        in_specs=[SMEM, VMEM, VMEM],
        out_specs=(VMEM,) * 6,
        compiler_params=params(),
        cost_estimate=cost(tok * SUB * heads * 6, tok * 2048, tok * heads * 6),
        name="prep",
    )(doc_lengths, dt_input, rate)


def convolve(ext_ref, mask_ref, taps, tok, width, put):
    for low in range(0, tok, ROWS):
        total = ext_ref[8 + low : 8 + low + ROWS, :] * taps[-1]
        for back in range(1, len(taps)):
            mask = jnp.concatenate([mask_ref[back - 1, low : low + ROWS, :]] * (width // LANES), 1)
            window = ext_ref[8 + low - back : 8 + low - back + ROWS, :]
            total = total + (window * taps[-1 - back]) * mask
        put(low, (total / (1.0 + jnp.exp(-total))).astype(BF16))


def state_kernel(
    owners,
    dl_ref,
    x_ref,
    b_ref,
    c_ref,
    tail_ref,
    taps_x_ref,
    taps_b_ref,
    taps_c_ref,
    w_ref,
    d_ref,
    xc_ref,
    bc_ref,
    cc_ref,
    h_ref,
    *rest,
):
    sends = rest[:owners]
    ext_ref, mask_ref, bt_ref, xw_ref, out_ref, sem = rest[owners:]
    tok, channels = x_ref.shape
    heads = w_ref.shape[1] // 2
    head_dim = channels // heads
    gn = b_ref.shape[1]
    per_group = channels // (gn // STATE) // CHUNK
    me = lax.axis_index("seq") if sends_apart(owners, channels) else 0
    row0 = lax.axis_index("seq") * tok
    edges = doc_edges(dl_ref)
    taps_len = taps_x_ref.shape[0]
    token = row0 + lax.broadcasted_iota(jnp.int32, (tok, LANES), 0)
    age = token - doc_start(token, edges)
    for back in range(1, taps_len):
        mask_ref[back - 1] = jnp.where(age >= back, 1.0, 0.0)

    def load(values, tail, lanes):
        ext_ref[8:, :] = values.astype(F32)
        ext_ref[:8, :] = tail.astype(F32)

    for ref, taps_ref, to_ref, at in ((b_ref, taps_b_ref, bc_ref, channels), (c_ref, taps_c_ref, cc_ref, channels + gn)):
        load(ref[...], tail_ref[:, at : at + gn], None)
        taps = [taps_ref[i : i + 1, :] for i in range(taps_len)]

        def put(low, value, to_ref=to_ref):
            to_ref[low : low + ROWS, :] = value

        convolve(ext_ref, mask_ref, taps, tok, gn, put)
    for group in range(gn // STATE):
        lanes = slice(group * STATE, (group + 1) * STATE)
        bt_ref[group] = bc_ref[:, lanes].astype(F32).T.astype(BF16)

    def body(k, carry):
        chunk = me ^ k
        lanes = pl.ds(pl.multiple_of(chunk * CHUNK, CHUNK), CHUNK)
        load(x_ref[:, lanes], tail_ref[:, lanes], None)
        taps = [taps_x_ref[i : i + 1, lanes] for i in range(taps_len)]
        one_hot = spread(heads, chunk, CHUNK, head_dim)

        def put(low, value):
            xc_ref[low : low + ROWS, lanes] = value
            weight = mm(w_ref[low : low + ROWS, :], one_hot)
            xw_ref[low : low + ROWS, :] = (value.astype(F32) * weight).astype(BF16)

        convolve(ext_ref, mask_ref, taps, tok, CHUNK, put)
        decay = mm(d_ref[...], one_hot)
        group = chunk // per_group
        state = None
        for c in range(tok // SUB):
            rows = slice(c * SUB, (c + 1) * SUB)
            local = mm(bt_ref[group, :, rows], xw_ref[rows, :])
            if state is None:
                state = local
            else:
                h_ref[c - 1, :, lanes] = state.astype(BF16)
                state = local + decay[2 + c : 3 + c, :] * state
        out_ref[k, :STATE, :] = state.astype(BF16)
        out_ref[k, STATE:, :] = decay.astype(BF16)
        return carry

    lax.fori_loop(0, owners, body, 0)
    copies = [pltpu.make_async_copy(out_ref.at[k], sends[k], sem.at[k]) for k in range(owners)]
    for copy in copies:
        copy.start()
    for copy in copies:
        copy.wait()


def sends_apart(owners, channels):
    return owners == lax.axis_size("seq") and owners * CHUNK == channels and owners & (owners - 1) == 0


def states(doc_lengths, x, b, c, tail, taps_x, taps_b, taps_c, w, d):
    tok, channels = x.shape
    gn = b.shape[1]
    owners = channels // CHUNK
    subs = tok // SUB
    piece = jax.ShapeDtypeStruct((STATE + 8, CHUNK), BF16)
    return pl.pallas_call(
        functools.partial(state_kernel, owners),
        out_shape=(
            jax.ShapeDtypeStruct((tok, channels), BF16),
            jax.ShapeDtypeStruct((tok, gn), BF16),
            jax.ShapeDtypeStruct((tok, gn), BF16),
            jax.ShapeDtypeStruct((subs - 1, STATE, channels), BF16),
        )
        + (piece,) * owners,
        in_specs=[SMEM] + [VMEM] * 9,
        out_specs=(VMEM,) * 4 + (ANY,) * owners,
        scratch_shapes=[
            pltpu.VMEM((tok + 8, CHUNK), F32),
            pltpu.VMEM((taps_x.shape[0] - 1, tok, LANES), F32),
            pltpu.VMEM((gn // STATE, STATE, tok), BF16),
            pltpu.VMEM((tok, CHUNK), BF16),
            pltpu.VMEM((owners, STATE + 8, CHUNK), BF16),
            pltpu.SemaphoreType.DMA((owners,)),
        ],
        compiler_params=params(),
        cost_estimate=cost(tok * STATE * channels * 4, tok * channels * 6, tok * channels * 2),
        name="conv_state",
    )(doc_lengths, x, b, c, tail, taps_x, taps_b, taps_c, w, d)


def scan_kernel(owners, *refs):
    pieces, outs = refs[:owners], refs[owners : 2 * owners]
    in_ref, out_ref, sem_in, sem_out = refs[2 * owners :]
    me = lax.axis_index("seq")
    copies = [pltpu.make_async_copy(pieces[k], in_ref.at[me ^ k], sem_in.at[k]) for k in range(owners)]
    for copy in copies:
        copy.start()
    for copy in copies:
        copy.wait()
    state = jnp.zeros((STATE, CHUNK), F32)
    out_ref[0] = state.astype(BF16)
    for i in range(owners - 1):
        row = in_ref[i, STATE:, :].astype(F32)
        decay = row[0:1] + (row[1:2] + row[2:3])
        state = decay * state + in_ref[i, :STATE, :].astype(F32)
        out_ref[i + 1] = state.astype(BF16)
    copies = [pltpu.make_async_copy(out_ref.at[me ^ k], outs[k], sem_out.at[k]) for k in range(owners)]
    for copy in copies:
        copy.start()
    for copy in copies:
        copy.wait()


def scan_blocks(pieces):
    owners = len(pieces)
    return pl.pallas_call(
        functools.partial(scan_kernel, owners),
        out_shape=(jax.ShapeDtypeStruct((STATE, CHUNK), BF16),) * owners,
        in_specs=[ANY] * owners,
        out_specs=(ANY,) * owners,
        scratch_shapes=[
            pltpu.VMEM((owners, STATE + 8, CHUNK), BF16),
            pltpu.VMEM((owners, STATE, CHUNK), BF16),
            pltpu.SemaphoreType.DMA((owners,)),
            pltpu.SemaphoreType.DMA((owners,)),
        ],
        compiler_params=params(),
        cost_estimate=cost(owners * STATE * CHUNK * 2, owners * STATE * CHUNK * 4),
        name="block_scan",
    )(*pieces)


def intra_kernel(group, heads, head_dim, dl_ref, xc_ref, bc_ref, cc_ref, h_ref, u_ref, col_ref, row_ref, out_ref):
    sub = pl.program_id(0)
    per_group = xc_ref.shape[1] // head_dim
    first = lax.axis_index("seq") * (pl.num_programs(0) * SUB) + sub * SUB
    edges = doc_edges(dl_ref)
    token = first + lax.broadcasted_iota(jnp.int32, (SUB, SUB), 0)
    source = first + lax.broadcasted_iota(jnp.int32, (SUB, SUB), 1)
    keep = (source <= token) & (source >= doc_start(token, edges))
    c_blk = cc_ref[...]
    scores = lax.dot_general(c_blk, bc_ref[...], (((1,), (1,)), ((), ())), preferred_element_type=F32)
    scores = jnp.where(keep, scores, 0.0)
    lane = lax.broadcasted_iota(jnp.int32, (SUB, LANES), 1)
    per_tile = LANES // head_dim
    for tile in range(per_group // per_tile):
        lanes = slice(tile * LANES, (tile + 1) * LANES)
        x_tile = xc_ref[:, lanes].astype(F32)
        left, right = [], []
        for i in range(per_tile):
            head = group * per_group + tile * per_tile + i
            gap = col_ref[:, head : head + 1] + row_ref[head : head + 1, :]
            left.append((jnp.exp2(jnp.minimum(gap, 80.0)) * scores).astype(BF16))
            mine = (lane >= i * head_dim) & (lane < (i + 1) * head_dim)
            right.append(jnp.where(mine, x_tile, 0.0).astype(BF16))
        out_ref[:, lanes] = mm(jnp.concatenate(left, 1), jnp.concatenate(right, 0))

    @pl.when(sub > 0)
    def _():
        for chunk in range(xc_ref.shape[1] // CHUNK):
            lanes = slice(chunk * CHUNK, (chunk + 1) * CHUNK)
            one_hot = spread(heads, group * (xc_ref.shape[1] // CHUNK) + chunk, CHUNK, head_dim)
            out_ref[:, lanes] += mm(c_blk, h_ref[0, :, lanes]) * mm(u_ref[...], one_hot)


def intra(group, doc_lengths, xc, bc, cc, h, u, col, row):
    tok, channels = xc.shape
    heads = col.shape[1]
    head_dim = channels // heads
    groups = bc.shape[1] // STATE
    width = channels // groups
    subs = tok // SUB
    return pl.pallas_call(
        functools.partial(intra_kernel, group, heads, head_dim),
        out_shape=jax.ShapeDtypeStruct((tok, width), F32),
        grid=(subs,),
        in_specs=[
            SMEM,
            pl.BlockSpec((SUB, width), lambda i: (i, group)),
            pl.BlockSpec((SUB, STATE), lambda i: (i, group)),
            pl.BlockSpec((SUB, STATE), lambda i: (i, group)),
            pl.BlockSpec((1, STATE, width), lambda i: (jnp.maximum(i - 1, 0), 0, group)),
            pl.BlockSpec((SUB, 2 * heads), lambda i: (i, 0)),
            pl.BlockSpec((SUB, heads), lambda i: (i, 0)),
            pl.BlockSpec((heads, SUB), lambda i: (0, i)),
        ],
        out_specs=pl.BlockSpec((SUB, width), lambda i: (i, 0)),
        compiler_params=params(),
        cost_estimate=cost(tok * SUB * width * 4, tok * width * 8, tok * SUB * width // head_dim),
        name="intra",
    )(doc_lengths, xc, bc, cc, h, u, col, row)


def final_kernel(owners, heads, head_dim, apart, norm_width, *refs):
    cc_ref, u0_ref, gate_ref, gain_ref = refs[:4]
    groups = cc_ref.shape[1] // STATE
    intra_refs = refs[4 : 4 + groups]
    pieces = refs[4 + groups : 4 + groups + owners]
    out_ref, e_ref, y_ref, sem = refs[4 + groups + owners :]
    me = lax.axis_index("seq") if apart else 0

    @pl.when(pl.program_id(0) == 0)
    def _():
        copies = [pltpu.make_async_copy(pieces[k], e_ref.at[me ^ k], sem.at[k]) for k in range(owners)]
        for copy in copies:
            copy.start()
        for copy in copies:
            copy.wait()

    channels = out_ref.shape[1]
    per_group = owners // groups
    per_norm = norm_width // CHUNK
    for norm in range(channels // norm_width):
        squares = None
        for chunk in range(norm * per_norm, (norm + 1) * per_norm):
            group = chunk // per_group
            lanes = slice(chunk * CHUNK, (chunk + 1) * CHUNK)
            inner = slice((chunk % per_group) * CHUNK, (chunk % per_group + 1) * CHUNK)
            scale = mm(u0_ref[...], spread(heads, chunk, CHUNK, head_dim))
            carried = mm(cc_ref[:, group * STATE : (group + 1) * STATE], e_ref[chunk])
            gate = gate_ref[:, lanes].astype(F32)
            value = (intra_refs[group][:, inner] + carried * scale) * (gate / (1.0 + jnp.exp(-gate)))
            y_ref[:, lanes] = value
            square = value * value
            for part in range(CHUNK // LANES):
                piece = square[:, part * LANES : (part + 1) * LANES]
                squares = piece if squares is None else squares + piece
        factor = lax.rsqrt(jnp.sum(squares, axis=1, keepdims=True) * (1.0 / norm_width) + norm_eps)
        lanes = slice(norm * norm_width, (norm + 1) * norm_width)
        out_ref[:, lanes] = (y_ref[:, lanes] * factor * gain_ref[:, lanes]).astype(BF16)


def final(cc, u0, gate, gain, intra_parts, pieces, head_dim, apart):
    tok, channels = gate.shape
    heads = channels // head_dim
    owners = len(pieces)
    rows = 64
    width = channels // len(intra_parts)
    return pl.pallas_call(
        functools.partial(final_kernel, owners, heads, head_dim, apart, NORM_HEADS * head_dim),
        out_shape=jax.ShapeDtypeStruct((tok, channels), BF16),
        grid=(tok // rows,),
        in_specs=[
            pl.BlockSpec((rows, cc.shape[1]), lambda i: (i, 0)),
            pl.BlockSpec((rows, 2 * heads), lambda i: (i, 0)),
            pl.BlockSpec((rows, channels), lambda i: (i, 0)),
            pl.BlockSpec((1, channels), lambda i: (0, 0)),
        ]
        + [pl.BlockSpec((rows, width), lambda i: (i, 0))] * len(intra_parts)
        + [ANY] * owners,
        out_specs=pl.BlockSpec((rows, channels), lambda i: (i, 0)),
        scratch_shapes=[
            pltpu.VMEM((owners, STATE, CHUNK), BF16),
            pltpu.VMEM((rows, channels), F32),
            pltpu.SemaphoreType.DMA((owners,)),
        ],
        compiler_params=params(),
        cost_estimate=cost(tok * STATE * channels * 2, tok * channels * 8, tok * channels * 2),
        name="final",
    )(cc, u0, gate, gain, *intra_parts, *pieces)


def shifted(value, steps):
    count = lax.axis_size("seq")
    return lax.ppermute(value, "seq", [(i, i + steps) for i in range(count - steps)])


def entering_by_doubling(pieces):
    whole = jnp.concatenate(pieces, 1).astype(F32)
    state, decay = whole[:STATE], whole[STATE] + (whole[STATE + 1] + whole[STATE + 2])
    step = 1
    while step < lax.axis_size("seq"):
        earlier, fell = shifted((state, decay), step)
        state, decay = decay[None, :] * earlier + state, decay * fell
        step *= 2
    entering = shifted(state, 1).astype(BF16)
    return [entering[:, k * CHUNK : (k + 1) * CHUNK] for k in range(len(pieces))]


def exchanged(pieces):
    count = len(pieces)
    return [pieces[0]] + [lax.ppermute(pieces[k], "seq", [(i, i ^ k) for i in range(count)]) for k in range(1, count)]


def on_device(
    x_input,
    b_input,
    c_input,
    dt_input,
    decay_rate,
    gate_input,
    taps_x,
    taps_b,
    taps_c,
    norm_gain,
    doc_lengths,
):
    tok, channels = x_input.shape
    heads = dt_input.shape[1]
    head_dim = channels // heads
    groups = b_input.shape[1] // STATE
    count = lax.axis_size("seq")
    apart = sends_apart(channels // CHUNK, channels)
    ends = jnp.concatenate([x_input[tok - 8 :], b_input[tok - 8 :], c_input[tok - 8 :]], 1)
    tail = lax.ppermute(ends, "seq", [(i, (i + 1) % count) for i in range(count)])
    w, u, u0, col, row, d = prep(doc_lengths, dt_input, decay_rate[None, :])
    xc, bc, cc, h, *pieces = states(doc_lengths, x_input, b_input, c_input, tail, taps_x, taps_b, taps_c, w, d)
    parts = [intra(group, doc_lengths, xc, bc, cc, h, u, col, row) for group in range(groups)]
    if apart:
        entering = exchanged(scan_blocks(exchanged(pieces)))
    else:
        entering = entering_by_doubling(pieces)
    return final(cc, u0, gate_input, norm_gain[None, :], parts, entering, head_dim, apart)


def solution(mesh):
    rows = P(("groups", "seq"), "dp")
    placed = (rows, rows, rows, rows, P("dp"), rows, P(None, "dp"), P(None, "dp"), P(None, "dp"), P("dp"), P("groups"))
    return jax.shard_map(on_device, mesh=mesh, in_specs=placed, out_specs=rows, check_vma=False)
```

```python
import functools

import jax
import jax.numpy as jnp
from jax import lax
from jax.experimental import pallas as pl
from jax.experimental.pallas import tpu as pltpu
from jax.sharding import PartitionSpec as P

STATE = 128
NORM_HEADS = 16
SUB = 128
CHUNK = 256
LANES = 128
ROWS = 32
CLUSTER = 4
LOG2E = 1.4426950408889634
norm_eps = 1e-05

F32 = jnp.float32
BF16 = jnp.bfloat16
VMEM = pl.BlockSpec(memory_space=pltpu.VMEM)
SMEM = pl.BlockSpec(memory_space=pltpu.SMEM)
ANY = pl.BlockSpec(memory_space=pl.ANY)
HBM = pl.BlockSpec(memory_space=pltpu.HBM)


def params(mib=48):
    return pltpu.CompilerParams(vmem_limit_bytes=mib << 20)


def cost(flops, moved, transcendentals=0):
    return pl.CostEstimate(flops=flops, bytes_accessed=moved, transcendentals=transcendentals)


def doc_edges(dl_ref):
    edges = [0]
    for i in range(dl_ref.shape[0] - 1):
        edges.append(edges[-1] + dl_ref[i])
    return edges


def doc_start(token, edges):
    start = jnp.zeros_like(token)
    for edge in edges[1:]:
        start = jnp.where(token >= edge, jnp.maximum(start, edge), start)
    return start


def split2(value):
    high = value.astype(BF16)
    return high, (value - high.astype(F32)).astype(BF16)


def split3(value):
    high = value.astype(BF16)
    rest = value - high.astype(F32)
    mid = rest.astype(BF16)
    return high, mid, (rest - mid.astype(F32)).astype(BF16)


def mm(a, b):
    return jnp.dot(a, b, preferred_element_type=F32)


def silu(value):
    half = 0.5 * value
    return half + half * jnp.tanh(half)


def spread(which, first_head, heads, width, head_dim):
    row = lax.broadcasted_iota(jnp.int32, (2 * LANES, width), 0) & (LANES - 1)
    lane = lax.broadcasted_iota(jnp.int32, (2 * LANES, width), 1)
    low = (row - (which * heads + first_head)) * head_dim
    return jnp.where((lane >= low) & (lane < low + head_dim), 1.0, 0.0).astype(BF16)


def start_all(copies):
    for copy in copies:
        copy.start()


def wait_all(copies):
    for copy in copies:
        copy.wait()


def pack_kernel(x_ref, b_ref, c_ref, out_ref, sem):
    copies, low = [], 0
    for i, ref in enumerate((x_ref, b_ref, c_ref)):
        tok, width = ref.shape
        copies.append(
            pltpu.make_async_copy(ref.at[pl.ds(tok - 8, 8), :], out_ref.at[:, pl.ds(low, width)], sem.at[i])
        )
        low += width
    start_all(copies)
    wait_all(copies)


def pack(x, b, c):
    width = x.shape[1] + b.shape[1] + c.shape[1]
    return pl.pallas_call(
        pack_kernel,
        out_shape=jax.ShapeDtypeStruct((8, width), BF16),
        in_specs=[HBM] * 3,
        out_specs=VMEM,
        scratch_shapes=[pltpu.SemaphoreType.DMA((3,))],
        name="pack",
    )(x, b, c)


def tables(row0, edges, dt_ref, rate_ref, tab_ref, tab32_ref, row_ref, d_ref):
    heads, tok = dt_ref.shape
    upto = jnp.where(
        lax.broadcasted_iota(jnp.int32, (SUB, SUB), 0) <= lax.broadcasted_iota(jnp.int32, (SUB, SUB), 1), 1.0, 0.0
    ).astype(BF16)
    rate = jnp.concatenate([rate_ref[...], jnp.zeros((1, LANES - heads), F32)], 1)
    rate = jnp.broadcast_to(rate, (LANES, LANES)).T[:heads]
    total = jnp.zeros((heads, 1), F32)
    decays = []
    for c in range(tok // SUB):
        span = slice(c * SUB, (c + 1) * SUB)
        first = row0 + c * SUB
        dt = dt_ref[:, span]
        step = jnp.maximum(dt, 0.0) + jnp.log1p(jnp.exp(-jnp.abs(dt)))
        parts = split3(-(step * rate))
        cum = mm(parts[0], upto) + (mm(parts[1], upto) + mm(parts[2], upto))
        last = cum[:, SUB - 1 :]
        token = first + lax.broadcasted_iota(jnp.int32, (heads, SUB), 1)
        start = doc_start(token, edges)
        last_start = doc_start(jnp.int32(first + SUB - 1), edges)
        to_end = jnp.exp(last - cum) * step * jnp.where(token >= last_start, 1.0, 0.0)
        since_sub = jnp.exp(cum) * jnp.where(start < first, 1.0, 0.0)
        since_block = jnp.exp(cum + total) * jnp.where(start < row0, 1.0, 0.0)
        table = jnp.concatenate([to_end, since_sub, since_block, cum * LOG2E], 0).T
        tab32_ref[span, :] = table
        tab_ref[span, :] = jnp.concatenate(split2(table), 1)
        row_ref[:, span] = (jnp.log(step) - cum) * LOG2E
        decays.append(jnp.exp(last) * jnp.where(last_start < first, 1.0, 0.0))
        total = total + last
    end_start = doc_start(jnp.int32(row0 + tok - 1), edges)
    whole = jnp.exp(total) * jnp.where(end_start < row0, 1.0, 0.0)
    columns = [part.astype(F32) for part in split3(whole)] + decays[1:]
    columns.append(jnp.zeros((heads, LANES - len(columns)), F32))
    columns = jnp.concatenate([jnp.concatenate(columns, 1), jnp.zeros((LANES - heads, LANES), F32)], 0)
    d_ref[...] = jnp.concatenate(split2(columns.T[:8]), 1)


def conv_kernel(
    dl_hbm,
    dt_hbm,
    rate_hbm,
    x_hbm,
    b_hbm,
    c_hbm,
    taps_x_hbm,
    taps_b_hbm,
    taps_c_hbm,
    tab_ref,
    tab32_ref,
    row_ref,
    d_ref,
    age_ref,
    taps_ref,
    part_ref,
    xc_ref,
    bc_ref,
    cc_ref,
    dl_ref,
    dt_ref,
    rate_ref,
    in_ref,
    ext_ref,
    mask_ref,
    sem,
    in_sem,
):
    tok, channels = x_hbm.shape
    gn = b_hbm.shape[1]
    taps_len = taps_x_hbm.shape[0]
    row0 = lax.axis_index("seq") * tok
    chunks = channels // CHUNK
    small = [pltpu.make_async_copy(dl_hbm, dl_ref, sem.at[0])]
    small.append(pltpu.make_async_copy(dt_hbm, dt_ref, sem.at[1]))
    small.append(pltpu.make_async_copy(rate_hbm, rate_ref, sem.at[2]))
    low = 0
    for i, ref in enumerate((taps_x_hbm, taps_b_hbm, taps_c_hbm)):
        small.append(pltpu.make_async_copy(ref, taps_ref.at[:, pl.ds(low, ref.shape[1])], sem.at[3 + i]))
        low += ref.shape[1]
    start_all(small)

    def chunk_copy(ref, at, place):
        return pltpu.make_async_copy(ref.at[:, pl.ds(at, CHUNK)], in_ref.at[place], in_sem.at[place])

    for k in range(chunks):
        chunk_copy(x_hbm, k * CHUNK, k).start()
    chunk_copy(b_hbm, 0, chunks).start()
    chunk_copy(c_hbm, 0, chunks + 1).start()
    wait_all(small)
    edges = doc_edges(dl_ref)
    tables(row0, edges, dt_ref, rate_ref, tab_ref, tab32_ref, row_ref, d_ref)
    token = row0 + lax.broadcasted_iota(jnp.int32, (tok, LANES), 0)
    age = token - doc_start(token, edges)
    age_ref[...] = age
    for back in range(1, taps_len):
        mask_ref[back - 1] = jnp.where(age >= back, 1.0, 0.0)
    ext_ref[:8, :] = jnp.zeros((8, CHUNK), F32)

    def convolve(place, lanes, to_ref, to_lanes):
        ext_ref[8:, :] = in_ref[place].astype(F32)
        taps = [taps_ref[i : i + 1, lanes] for i in range(taps_len)]
        for low in range(0, tok, ROWS):
            total = ext_ref[8 + low : 8 + low + ROWS, :] * taps[-1]
            for back in range(1, taps_len):
                mask = jnp.concatenate([mask_ref[back - 1, low : low + ROWS, :]] * (CHUNK // LANES), 1)
                window = ext_ref[8 + low - back : 8 + low - back + ROWS, :]
                total = total + (window * taps[-1 - back]) * mask
            if low == 0:
                part_ref[:, lanes] = total[:8]
            to_ref[low : low + ROWS, to_lanes] = silu(total).astype(BF16)

    def body(k, carry):
        chunk_copy(x_hbm, pl.multiple_of(k * CHUNK, CHUNK), k).wait()
        lanes = pl.ds(pl.multiple_of(k * CHUNK, CHUNK), CHUNK)
        convolve(k, lanes, xc_ref, lanes)
        return carry

    lax.fori_loop(0, chunks, body, 0)
    for i, (ref, to_ref) in enumerate(((b_hbm, bc_ref), (c_hbm, cc_ref))):
        chunk_copy(ref, 0, chunks + i).wait()
        convolve(chunks + i, slice(channels + i * gn, channels + (i + 1) * gn), to_ref, slice(0, gn))


def conv(doc_lengths, dt_t, rate, x, b, c, taps_x, taps_b, taps_c):
    heads, tok = dt_t.shape
    channels, gn = x.shape[1], b.shape[1]
    width = channels + 2 * gn
    places = channels // CHUNK + 2
    taps_len = taps_x.shape[0]
    shape = jax.ShapeDtypeStruct
    return pl.pallas_call(
        conv_kernel,
        out_shape=(
            shape((tok, 2 * LANES), BF16),
            shape((tok, LANES), F32),
            shape((heads, tok), F32),
            shape((8, 2 * LANES), BF16),
            shape((tok, LANES), jnp.int32),
            shape((taps_len, width), F32),
            shape((8, width), F32),
            shape((tok, channels), BF16),
            shape((tok, gn), BF16),
            shape((tok, gn), BF16),
        ),
        in_specs=[HBM] * 9,
        out_specs=(VMEM,) * 10,
        scratch_shapes=[
            pltpu.SMEM(doc_lengths.shape, jnp.int32),
            pltpu.VMEM((heads, tok), F32),
            pltpu.VMEM((1, heads), F32),
            pltpu.VMEM((places, tok, CHUNK), BF16),
            pltpu.VMEM((tok + 8, CHUNK), F32),
            pltpu.VMEM((taps_len - 1, tok, LANES), F32),
            pltpu.SemaphoreType.DMA((6,)),
            pltpu.SemaphoreType.DMA((places,)),
        ],
        compiler_params=params(),
        cost_estimate=cost(tok * width * 16, tok * width * 4, tok * width),
        name="conv",
    )(doc_lengths, dt_t, rate, x, b, c, taps_x, taps_b, taps_c)


def state_kernel(
    tail_ref, part_ref, taps_ref, age_ref, tab_ref, d_ref, xc_in, bc_in, cc_in, xc_ref, bc_ref, cc_ref, h_ref, *rest
):
    sends = rest[:CLUSTER]
    ext_ref, head_ref, bt_ref = rest[CLUSTER:]
    tok, channels = xc_in.shape
    gn = bc_in.shape[1]
    heads = LANES // 4
    head_dim = channels // heads
    owned = channels // CLUSTER
    group_width = channels // (gn // STATE)
    mine = lax.axis_index("seq") % CLUSTER
    taps_len = taps_ref.shape[0]
    width = part_ref.shape[1]

    ext_ref[:8, :] = tail_ref[...].astype(F32)
    ext_ref[8:, :] = jnp.zeros((8, width), F32)
    total = part_ref[...]
    age = jnp.concatenate([age_ref[:8, :]] * (width // LANES), 1)
    for back in range(1, taps_len):
        term = ext_ref[8 - back : 16 - back, :] * taps_ref[taps_len - 1 - back : taps_len - back, :]
        total = total + jnp.where(age >= back, term, 0.0)
    head = silu(total).astype(BF16)
    head_ref[...] = head.astype(F32)
    xc_ref[:8, :] = head[:, :channels]
    bc_ref[:8, :] = head[:, channels : channels + gn]
    cc_ref[:8, :] = head[:, channels + gn :]
    for group in range(gn // STATE):
        lanes = slice(group * STATE, (group + 1) * STATE)
        at = slice(channels + group * STATE, channels + (group + 1) * STATE)
        b_blk = jnp.concatenate([head_ref[:, at], bc_in[:, lanes].astype(F32)[8:]], 0)
        bt_ref[group] = b_blk.T.astype(BF16)

    for k in range(CLUSTER):
        owner = mine ^ k
        for part in range(owned // CHUNK):
            at = owner * owned + part * CHUNK
            lanes = pl.ds(pl.multiple_of(at, CHUNK), CHUNK)
            here = slice(part * CHUNK, (part + 1) * CHUNK)
            one_hot = spread(0, at // head_dim, heads, CHUNK, head_dim)
            decay = mm(d_ref[...], one_hot)
            state = None
            for c in range(tok // SUB):
                rows = slice(c * SUB, (c + 1) * SUB)
                weight = mm(tab_ref[rows, :], one_hot)
                value = xc_in[rows, lanes].astype(F32)
                if c == 0:
                    value = jnp.concatenate([head_ref[:, lanes], value[8:]], 0)
                local = mm(bt_ref[at // group_width, :, rows], (value * weight).astype(BF16))
                if state is None:
                    state = local
                else:
                    h_ref[c - 1, :, lanes] = state.astype(BF16)
                    state = local + decay[2 + c : 3 + c, :] * state
            sends[k][:STATE, here] = state.astype(BF16)
            sends[k][STATE:, here] = decay.astype(BF16)


def states(tail, part, taps, age, tab, d, xc, bc, cc):
    tok, channels = xc.shape
    gn = bc.shape[1]
    width = part.shape[1]
    piece = jax.ShapeDtypeStruct((STATE + 8, channels // CLUSTER), BF16)
    same = [jax.ShapeDtypeStruct(value.shape, value.dtype) for value in (xc, bc, cc)]
    return pl.pallas_call(
        state_kernel,
        out_shape=(*same, jax.ShapeDtypeStruct((tok // SUB - 1, STATE, channels), BF16)) + (piece,) * CLUSTER,
        in_specs=[VMEM] * 9,
        out_specs=(VMEM,) * (4 + CLUSTER),
        scratch_shapes=[
            pltpu.VMEM((16, width), F32),
            pltpu.VMEM((8, width), F32),
            pltpu.VMEM((gn // STATE, STATE, tok), BF16),
        ],
        input_output_aliases={6: 0, 7: 1, 8: 2},
        compiler_params=params(),
        cost_estimate=cost(tok * STATE * channels * 4, tok * channels * 4),
        name="state",
    )(tail, part, taps, age, tab, d, xc, bc, cc)


def scan_kernel(*refs):
    pieces = refs[:CLUSTER]
    local_ref, pre_ref, total_ref = refs[CLUSTER:]
    mine = lax.axis_index("seq") % CLUSTER

    def in_order(values):
        bit = 1
        while bit < CLUSTER:
            odd = (mine & bit) != 0
            values = [jnp.where(odd, values[i ^ bit], values[i]) for i in range(CLUSTER)]
            bit *= 2
        return values

    owned = total_ref.shape[1]
    tables = [ref[STATE:, :].astype(F32) for ref in pieces]
    decays = in_order([row[0:1] + (row[1:2] + row[2:3]) for row in tables])
    pre = jnp.ones((1, owned), F32)
    for i in range(CLUSTER):
        pre_ref[i] = jnp.broadcast_to(pre, (8, owned))
        pre = pre * decays[i]
    pre_ref[CLUSTER] = jnp.broadcast_to(pre, (8, owned))
    for at in range(0, owned, LANES):
        lanes = slice(at, at + LANES)
        for low in range(0, STATE, 64):
            rows = slice(low, low + 64)
            values = in_order([ref[rows, lanes].astype(F32) for ref in pieces])
            local_ref[0, rows, lanes] = jnp.zeros((64, LANES), F32)
            state = values[0]
            for i in range(1, CLUSTER):
                local_ref[i, rows, lanes] = state
                state = decays[i][:, lanes] * state + values[i]
            total_ref[rows, lanes] = state.astype(BF16)


def scan_blocks(pieces):
    owned = pieces[0].shape[1]
    return pl.pallas_call(
        scan_kernel,
        out_shape=(
            jax.ShapeDtypeStruct((CLUSTER, STATE, owned), F32),
            jax.ShapeDtypeStruct((CLUSTER + 1, 8, owned), F32),
            jax.ShapeDtypeStruct((STATE, owned), BF16),
        ),
        in_specs=[VMEM] * CLUSTER,
        out_specs=(VMEM,) * 3,
        compiler_params=params(),
        cost_estimate=cost(CLUSTER * STATE * owned * 2, CLUSTER * STATE * owned * 6),
        name="cluster_scan",
    )(*pieces)


def join_kernel(before_ref, local_ref, pre_ref, *outs):
    index = lax.axis_index("seq")
    mine = index % CLUSTER
    before = jnp.where(index >= CLUSTER, before_ref[...].astype(F32), 0.0)
    for k in range(CLUSTER):
        block = mine ^ k
        outs[k][...] = (local_ref[block] + pre_ref[block][0:1] * before).astype(BF16)


def join(before, local, pre):
    owned = local.shape[2]
    return pl.pallas_call(
        join_kernel,
        out_shape=(jax.ShapeDtypeStruct((STATE, owned), BF16),) * CLUSTER,
        in_specs=[VMEM] * 3,
        out_specs=(VMEM,) * CLUSTER,
        compiler_params=params(),
        cost_estimate=cost(CLUSTER * STATE * owned * 2, CLUSTER * STATE * owned * 6),
        name="join",
    )(before, local, pre)


def group_at(turn, groups):
    return (lax.axis_index("seq") % CLUSTER) // (CLUSTER // groups) ^ turn


def intra_kernel(turn, groups, head_dim, xc_ref, bc_ref, cc_ref, h_ref, tab_ref, tab32_ref, row_ref, age_ref, out_ref):
    sub = pl.program_id(0)
    group = group_at(turn, groups)
    width = xc_ref.shape[1]
    per_group = width // head_dim
    heads = per_group * groups
    back = lax.broadcasted_iota(jnp.int32, (SUB, SUB), 0) - lax.broadcasted_iota(jnp.int32, (SUB, SUB), 1)
    keep = (back >= 0) & (back <= age_ref[...])
    c_blk = cc_ref[...]
    scores = lax.dot_general(c_blk, bc_ref[...], (((1,), (1,)), ((), ())), preferred_element_type=F32)
    scores = jnp.where(keep, scores, 0.0)
    col = pltpu.roll(tab32_ref[...], LANES - (3 * heads + group * per_group), 1)
    lane = lax.broadcasted_iota(jnp.int32, (SUB, LANES), 1)
    per_tile = LANES // head_dim
    for tile in range(per_group // per_tile):
        lanes = slice(tile * LANES, (tile + 1) * LANES)
        x_tile = xc_ref[:, lanes].astype(F32)
        left, right = [], []
        for i in range(per_tile):
            head = tile * per_tile + i
            gap = col[:, head : head + 1] + row_ref[head : head + 1, :]
            left.append((jnp.exp2(jnp.minimum(gap, 80.0)) * scores).astype(BF16))
            mine = (lane >= i * head_dim) & (lane < (i + 1) * head_dim)
            right.append(jnp.where(mine, x_tile, 0.0).astype(BF16))
        out_ref[:, lanes] = mm(jnp.concatenate(left, 1), jnp.concatenate(right, 0))

    @pl.when(sub > 0)
    def _():
        for chunk in range(width // CHUNK):
            lanes = slice(chunk * CHUNK, (chunk + 1) * CHUNK)
            first_head = group * per_group + chunk * (CHUNK // head_dim)
            one_hot = spread(1, first_head, heads, CHUNK, head_dim)
            out_ref[:, lanes] += mm(c_blk, h_ref[0, :, lanes]) * mm(tab_ref[...], one_hot)


def intra(turn, xc, bc, cc, h, tab, tab32, row, age):
    tok, channels = xc.shape
    heads = row.shape[0]
    head_dim = channels // heads
    groups = bc.shape[1] // STATE
    width = channels // groups
    return pl.pallas_call(
        functools.partial(intra_kernel, turn, groups, head_dim),
        out_shape=jax.ShapeDtypeStruct((tok, width), F32),
        grid=(tok // SUB,),
        in_specs=[
            pl.BlockSpec((SUB, width), lambda i: (i, group_at(turn, groups))),
            pl.BlockSpec((SUB, STATE), lambda i: (i, group_at(turn, groups))),
            pl.BlockSpec((SUB, STATE), lambda i: (i, group_at(turn, groups))),
            pl.BlockSpec((1, STATE, width), lambda i: (jnp.maximum(i - 1, 0), 0, group_at(turn, groups))),
            pl.BlockSpec((SUB, 2 * LANES), lambda i: (i, 0)),
            pl.BlockSpec((SUB, LANES), lambda i: (i, 0)),
            pl.BlockSpec((heads // groups, SUB), lambda i: (group_at(turn, groups), i)),
            pl.BlockSpec((SUB, LANES), lambda i: (i, 0)),
        ],
        out_specs=pl.BlockSpec((SUB, width), lambda i: (i, 0)),
        compiler_params=params(),
        cost_estimate=cost(tok * SUB * width * 4, tok * width * 8, tok * SUB * width // head_dim),
        name="intra",
    )(xc, bc, cc, h, tab, tab32, row, age)


def final_kernel(turn, groups, head_dim, *refs):
    cc_ref, tab_ref, gate_ref, gain_ref, part_ref = refs[:5]
    per_group = CLUSTER // groups
    pieces = refs[5 : 5 + per_group]
    out_ref, y_ref = refs[-2:]
    width = gate_ref.shape[1]
    heads = groups * width // head_dim
    group = group_at(turn, groups)
    mine = lax.axis_index("seq") % CLUSTER
    owned = width // per_group
    squares = None
    for k in range(per_group):
        for part in range(owned // CHUNK):
            at = ((mine ^ k) % per_group) * owned + part * CHUNK
            lanes = pl.ds(pl.multiple_of(at, CHUNK), CHUNK)
            scale = mm(tab_ref[...], spread(2, group * (width // head_dim) + at // head_dim, heads, CHUNK, head_dim))
            carried = mm(cc_ref[...], pieces[k][:, part * CHUNK : (part + 1) * CHUNK])
            value = (part_ref[:, lanes] + carried * scale) * silu(gate_ref[:, lanes].astype(F32))
            y_ref[:, lanes] = value
            square = value * value
            for i in range(CHUNK // LANES):
                piece = square[:, i * LANES : (i + 1) * LANES]
                squares = piece if squares is None else squares + piece
    factor = lax.rsqrt(jnp.sum(squares, axis=1, keepdims=True) * (1.0 / width) + norm_eps)
    out_ref[...] = (y_ref[...] * factor * gain_ref[...]).astype(BF16)


def final(turn, cc, tab, gate, gain, part, pieces, head_dim, so_far=None):
    tok, channels = gate.shape
    groups = CLUSTER // len(pieces)
    rows = 64
    width = channels // groups
    operands = (cc, tab, gate, gain, part, *pieces) + (() if so_far is None else (so_far,))
    return pl.pallas_call(
        functools.partial(final_kernel, turn, groups, head_dim),
        out_shape=jax.ShapeDtypeStruct((tok, channels), BF16),
        grid=(tok // rows,),
        in_specs=[
            pl.BlockSpec((rows, STATE), lambda i: (i, group_at(turn, groups))),
            pl.BlockSpec((rows, 2 * LANES), lambda i: (i, 0)),
            pl.BlockSpec((rows, width), lambda i: (i, group_at(turn, groups))),
            pl.BlockSpec((1, width), lambda i: (0, group_at(turn, groups))),
            pl.BlockSpec((rows, width), lambda i: (i, 0)),
        ]
        + [VMEM] * len(pieces)
        + ([] if so_far is None else [ANY]),
        out_specs=pl.BlockSpec((rows, width), lambda i: (i, group_at(turn, groups))),
        scratch_shapes=[pltpu.VMEM((rows, width), F32)],
        input_output_aliases={} if so_far is None else {len(operands) - 1: 0},
        compiler_params=params(),
        cost_estimate=cost(tok * STATE * width * 2, tok * width * 8, tok * width),
        name="final",
    )(*operands)


def moved(value, hop):
    count = lax.axis_size("seq")
    return lax.ppermute(value, "seq", [(i, hop(i)) for i in range(count) if 0 <= hop(i) < count])


def exchanged(pieces, order):
    arrived = {0: pieces[0]}
    for k in order:
        arrived[k] = moved(pieces[k], lambda i, k=k: i ^ k)
    return [arrived[k] for k in range(CLUSTER)]


def before_cluster(total, pre):
    clusters = lax.axis_size("seq") // CLUSTER
    if clusters == 1:
        return jnp.zeros_like(total)
    if clusters == 2:
        return moved(total, lambda i: i ^ CLUSTER)
    shift = lambda value, steps: moved(value, lambda i: i + steps * CLUSTER)
    state, decay = shift((total.astype(F32), pre[CLUSTER, 0]), 1)
    step = 1
    while step < clusters - 1:
        earlier, fell = shift((state, decay), step)
        state, decay = state + decay[None, :] * earlier, decay * fell
        step *= 2
    return state


def tied(values, other):
    *values, _ = lax.optimization_barrier((*values, other))
    return values


def on_device(
    x_input,
    b_input,
    c_input,
    dt_input,
    decay_rate,
    gate_input,
    taps_x,
    taps_b,
    taps_c,
    norm_gain,
    doc_lengths,
):
    channels = x_input.shape[1]
    head_dim = channels // dt_input.shape[1]
    groups = b_input.shape[1] // STATE
    count = lax.axis_size("seq")
    tail = lax.ppermute(pack(x_input, b_input, c_input), "seq", [(i, (i + 1) % count) for i in range(count)])
    tab, tab32, row, d, age, taps, part, xc, bc, cc = conv(
        doc_lengths, dt_input.T, decay_rate[None, :], x_input, b_input, c_input, taps_x, taps_b, taps_c
    )
    xc, bc, cc, h, *pieces = states(tail, part, taps, age, tab, d, xc, bc, cc)
    first = intra(0, xc, bc, cc, h, tab, tab32, row, age)
    local, pre, total = scan_blocks(tied(exchanged(pieces, (3, 2, 1)), first))
    second = intra(1, xc, bc, cc, h, tab, tab32, row, age)
    (before,) = tied([before_cluster(total, pre)], second)
    entering = exchanged(join(before, local, pre), (1, 3, 2))
    share = CLUSTER // groups
    output = None
    for turn, inner in enumerate((first, second)):
        mine = entering[turn * share : (turn + 1) * share]
        output = final(turn, cc, tab, gate_input, norm_gain[None, :], inner, mine, head_dim, output)
    return output


def solution(mesh):
    rows = P(("groups", "seq"), "dp")
    placed = (rows, rows, rows, rows, P("dp"), rows, P(None, "dp"), P(None, "dp"), P(None, "dp"), P("dp"), P("groups"))
    return jax.shard_map(on_device, mesh=mesh, in_specs=placed, out_specs=rows, check_vma=False)
```

```python
import functools

import jax
import jax.numpy as jnp
from jax import lax
from jax.experimental import pallas as pl
from jax.experimental.pallas import tpu as pltpu
from jax.sharding import PartitionSpec as P

STATE = 128
SUB = 128
CHUNK = 256
LANES = 128
ROWS = 32
CLUSTER = 4
LOG2E = 1.4426950408889634
norm_eps = 1e-05

F32 = jnp.float32
BF16 = jnp.bfloat16
VMEM = pl.BlockSpec(memory_space=pltpu.VMEM)
ANY = pl.BlockSpec(memory_space=pl.ANY)
HBM = pl.BlockSpec(memory_space=pltpu.HBM)


def params(mib=24):
    return pltpu.CompilerParams(vmem_limit_bytes=mib << 20)


def cost(flops, moved, transcendentals=0):
    return pl.CostEstimate(flops=flops, bytes_accessed=moved, transcendentals=transcendentals)


def doc_edges(dl_ref):
    edges = [0]
    for i in range(dl_ref.shape[0] - 1):
        edges.append(edges[-1] + dl_ref[i])
    return edges


def doc_start(token, edges):
    start = jnp.zeros_like(token)
    for edge in edges[1:]:
        start = jnp.where(token >= edge, jnp.maximum(start, edge), start)
    return start


def split2(value):
    high = value.astype(BF16)
    return high, (value - high.astype(F32)).astype(BF16)


def split3(value):
    high = value.astype(BF16)
    rest = value - high.astype(F32)
    mid = rest.astype(BF16)
    return high, mid, (rest - mid.astype(F32)).astype(BF16)


def mm(a, b):
    return jnp.dot(a, b, preferred_element_type=F32)


def silu(value):
    half = 0.5 * value
    return half + half * jnp.tanh(half)


def spread(base, rows, first_head, heads, width, head_dim):
    row = lax.broadcasted_iota(jnp.int32, (rows, width), 0) - (base + first_head)
    head = lax.broadcasted_iota(jnp.int32, (rows, width), 1) // head_dim
    return jnp.where((row == head) | (row == head + heads), 1.0, 0.0).astype(BF16)


def start_all(copies):
    for copy in copies:
        copy.start()


def wait_all(copies):
    for copy in copies:
        copy.wait()


def tables(row0, edges, dt_ref, rate_ref, tab_ref, tab0_ref, col_ref, row_ref, d_ref):
    heads, tok = dt_ref.shape
    upto = jnp.where(
        lax.broadcasted_iota(jnp.int32, (SUB, SUB), 0) <= lax.broadcasted_iota(jnp.int32, (SUB, SUB), 1), 1.0, 0.0
    ).astype(BF16)
    rate = jnp.concatenate([rate_ref[...], jnp.zeros((1, LANES - heads), F32)], 1)
    rate = jnp.broadcast_to(rate, (LANES, LANES)).T[:heads]
    total = jnp.zeros((heads, 1), F32)
    decays = []
    for c in range(tok // SUB):
        span = slice(c * SUB, (c + 1) * SUB)
        first = row0 + c * SUB
        dt = dt_ref[:, span]
        step = jnp.maximum(dt, 0.0) + jnp.log1p(jnp.exp(-jnp.abs(dt)))
        parts = split3(-(step * rate))
        cum = mm(parts[0], upto) + (mm(parts[1], upto) + mm(parts[2], upto))
        last = cum[:, SUB - 1 :]
        token = first + lax.broadcasted_iota(jnp.int32, (heads, SUB), 1)
        start = doc_start(token, edges)
        last_start = doc_start(jnp.int32(first + SUB - 1), edges)
        to_end = jnp.exp(last - cum) * step * jnp.where(token >= last_start, 1.0, 0.0)
        since_sub = jnp.exp(cum) * jnp.where((start < first) & (c > 0), 1.0, 0.0)
        since_block = jnp.exp(cum + total) * jnp.where(start < row0, 1.0, 0.0)
        first_pair = [part.astype(F32) for part in (*split2(to_end), *split2(since_sub))]
        second_pair = [part.astype(F32) for part in split2(since_block)] + [cum * LOG2E, jnp.zeros_like(cum)]
        tab_ref[span, :] = jnp.concatenate(first_pair, 0).T.astype(BF16)
        second = jnp.concatenate(second_pair, 0).T
        tab0_ref[span, :] = second[:, : 2 * heads].astype(BF16)
        col_ref[span, :] = second
        row_ref[:, span] = (jnp.log(step) - cum) * LOG2E
        decays.append(jnp.exp(last) * jnp.where(last_start < first, 1.0, 0.0))
        total = total + last
    end_start = doc_start(jnp.int32(row0 + tok - 1), edges)
    whole = jnp.exp(total) * jnp.where(end_start < row0, 1.0, 0.0)
    columns = [part.astype(F32) for part in split3(whole)] + decays[1:]
    columns.append(jnp.zeros((heads, LANES - len(columns)), F32))
    columns = jnp.concatenate([jnp.concatenate(columns, 1), jnp.zeros((LANES - heads, LANES), F32)], 0)
    halves = [part.astype(F32)[:, :heads] for part in split2(columns.T[:8])]
    d_ref[...] = jnp.concatenate(halves, 1).astype(BF16)


def prep_kernel(
    dl_hbm,
    dt_hbm,
    rate_hbm,
    x_hbm,
    b_hbm,
    c_hbm,
    ends_ref,
    tab_ref,
    tab0_ref,
    col_ref,
    row_ref,
    d_ref,
    age_ref,
    dl_ref,
    dt_ref,
    rate_ref,
    sem,
):
    tok = x_hbm.shape[0]
    small = [
        pltpu.make_async_copy(hbm, ref, sem.at[i])
        for i, (hbm, ref) in enumerate(((dl_hbm, dl_ref), (dt_hbm, dt_ref), (rate_hbm, rate_ref)))
    ]
    start_all(small)
    ends, low = [], 0
    for i, ref in enumerate((x_hbm, b_hbm, c_hbm)):
        width = ref.shape[1]
        ends.append(
            pltpu.make_async_copy(ref.at[pl.ds(tok - 8, 8), :], ends_ref.at[:, pl.ds(low, width)], sem.at[3 + i])
        )
        low += width
    start_all(ends)
    wait_all(small)
    row0 = lax.axis_index("seq") * tok
    edges = doc_edges(dl_ref)
    tables(row0, edges, dt_ref, rate_ref, tab_ref, tab0_ref, col_ref, row_ref, d_ref)
    token = row0 + lax.broadcasted_iota(jnp.int32, (tok, LANES), 0)
    age_ref[...] = token - doc_start(token, edges)
    wait_all(ends)


def prep(doc_lengths, dt_t, rate, x, b, c):
    heads, tok = dt_t.shape
    shape = jax.ShapeDtypeStruct
    return pl.pallas_call(
        prep_kernel,
        out_shape=(
            shape((8, x.shape[1] + b.shape[1] + c.shape[1]), BF16),
            shape((tok, LANES), BF16),
            shape((tok, 2 * heads), BF16),
            shape((tok, LANES), F32),
            shape((heads, tok), F32),
            shape((8, 2 * heads), BF16),
            shape((tok, LANES), jnp.int32),
        ),
        in_specs=[HBM] * 6,
        out_specs=(VMEM,) * 7,
        scratch_shapes=[
            pltpu.SMEM(doc_lengths.shape, jnp.int32),
            pltpu.VMEM((heads, tok), F32),
            pltpu.VMEM((1, heads), F32),
            pltpu.SemaphoreType.DMA((6,)),
        ],
        compiler_params=params(16),
        name="prep",
    )(doc_lengths, dt_t, rate, x, b, c)


def conv_kernel(
    age_ref,
    x_hbm,
    b_hbm,
    c_hbm,
    taps_x_hbm,
    taps_b_hbm,
    taps_c_hbm,
    taps_ref,
    part_ref,
    xc_ref,
    bc_ref,
    cc_ref,
    in_ref,
    ext_ref,
    mask_ref,
    sem,
    in_sem,
):
    tok, channels = x_hbm.shape
    gn = b_hbm.shape[1]
    taps_len = taps_x_hbm.shape[0]
    chunks = channels // CHUNK
    small = []
    low = 0
    for i, ref in enumerate((taps_x_hbm, taps_b_hbm, taps_c_hbm)):
        small.append(pltpu.make_async_copy(ref, taps_ref.at[:, pl.ds(low, ref.shape[1])], sem.at[i]))
        low += ref.shape[1]
    start_all(small)

    def chunk_copy(ref, at, place):
        return pltpu.make_async_copy(ref.at[:, pl.ds(at, CHUNK)], in_ref.at[place], in_sem.at[place])

    for k in range(chunks):
        chunk_copy(x_hbm, k * CHUNK, k).start()
    chunk_copy(b_hbm, 0, chunks).start()
    chunk_copy(c_hbm, 0, chunks + 1).start()
    for back in range(1, taps_len):
        mask_ref[back - 1] = jnp.where(age_ref[...] >= back, 1.0, 0.0)
    ext_ref[:8, :] = jnp.zeros((8, CHUNK), F32)
    wait_all(small)

    def convolve(place, lanes, to_ref, to_lanes):
        ext_ref[8:, :] = in_ref[place].astype(F32)
        taps = [taps_ref[i : i + 1, lanes] for i in range(taps_len)]
        for low in range(0, tok, ROWS):
            total = ext_ref[8 + low : 8 + low + ROWS, :] * taps[-1]
            for back in range(1, taps_len):
                mask = jnp.concatenate([mask_ref[back - 1, low : low + ROWS, :]] * (CHUNK // LANES), 1)
                window = ext_ref[8 + low - back : 8 + low - back + ROWS, :]
                total = total + (window * taps[-1 - back]) * mask
            if low == 0:
                part_ref[:, lanes] = total[:8]
            to_ref[low : low + ROWS, to_lanes] = silu(total).astype(BF16)

    def body(k, carry):
        chunk_copy(x_hbm, pl.multiple_of(k * CHUNK, CHUNK), k).wait()
        lanes = pl.ds(pl.multiple_of(k * CHUNK, CHUNK), CHUNK)
        convolve(k, lanes, xc_ref, lanes)
        return carry

    lax.fori_loop(0, chunks, body, 0)
    for i, (ref, to_ref) in enumerate(((b_hbm, bc_ref), (c_hbm, cc_ref))):
        chunk_copy(ref, 0, chunks + i).wait()
        convolve(chunks + i, slice(channels + i * gn, channels + (i + 1) * gn), to_ref, slice(0, gn))


def conv(age, x, b, c, taps_x, taps_b, taps_c):
    tok, channels = x.shape
    gn = b.shape[1]
    width = channels + 2 * gn
    places = channels // CHUNK + 2
    taps_len = taps_x.shape[0]
    shape = jax.ShapeDtypeStruct
    return pl.pallas_call(
        conv_kernel,
        out_shape=(
            shape((taps_len, width), F32),
            shape((8, width), F32),
            shape((tok, channels), BF16),
            shape((tok, gn), BF16),
            shape((tok, gn), BF16),
        ),
        in_specs=[VMEM] + [HBM] * 6,
        out_specs=(VMEM,) * 5,
        scratch_shapes=[
            pltpu.VMEM((places, tok, CHUNK), BF16),
            pltpu.VMEM((tok + 8, CHUNK), F32),
            pltpu.VMEM((taps_len - 1, tok, LANES), F32),
            pltpu.SemaphoreType.DMA((3,)),
            pltpu.SemaphoreType.DMA((places,)),
        ],
        compiler_params=params(16),
        cost_estimate=cost(tok * width * 16, tok * width * 4, tok * width),
        name="conv",
    )(age, x, b, c, taps_x, taps_b, taps_c)


def state_kernel(
    tail_ref, part_ref, taps_ref, age_ref, tab_ref, d_ref, xc_in, bc_in, cc_in, xc_ref, bc_ref, cc_ref, h_ref, *rest
):
    sends = rest[:CLUSTER]
    ext_ref, head_ref, bt_ref = rest[CLUSTER:]
    tok, channels = xc_in.shape
    gn = bc_in.shape[1]
    heads = d_ref.shape[1] // 2
    head_dim = channels // heads
    owned = channels // CLUSTER
    group_width = channels // (gn // STATE)
    mine = lax.axis_index("seq") % CLUSTER
    taps_len = taps_ref.shape[0]
    width = part_ref.shape[1]

    ext_ref[:8, :] = tail_ref[...].astype(F32)
    ext_ref[8:, :] = jnp.zeros((8, width), F32)
    total = part_ref[...]
    age = jnp.concatenate([age_ref[:8, :]] * (width // LANES), 1)
    for back in range(1, taps_len):
        term = ext_ref[8 - back : 16 - back, :] * taps_ref[taps_len - 1 - back : taps_len - back, :]
        total = total + jnp.where(age >= back, term, 0.0)
    head = silu(total).astype(BF16)
    head_ref[...] = head.astype(F32)
    xc_ref[:8, :] = head[:, :channels]
    bc_ref[:8, :] = head[:, channels : channels + gn]
    cc_ref[:8, :] = head[:, channels + gn :]
    for group in range(gn // STATE):
        lanes = slice(group * STATE, (group + 1) * STATE)
        at = slice(channels + group * STATE, channels + (group + 1) * STATE)
        b_blk = jnp.concatenate([head_ref[:, at], bc_in[:, lanes].astype(F32)[8:]], 0)
        bt_ref[group] = b_blk.T.astype(BF16)

    for k in range(CLUSTER):
        owner = mine ^ k
        for part in range(owned // CHUNK):
            at = owner * owned + part * CHUNK
            lanes = pl.ds(pl.multiple_of(at, CHUNK), CHUNK)
            here = slice(part * CHUNK, (part + 1) * CHUNK)
            one_hot = spread(0, 2 * heads, at // head_dim, heads, CHUNK, head_dim)
            decay = mm(d_ref[...], one_hot)
            state = None
            for c in range(tok // SUB):
                rows = slice(c * SUB, (c + 1) * SUB)
                weight = mm(tab_ref[rows, : 2 * heads], one_hot)
                value = xc_in[rows, lanes].astype(F32)
                if c == 0:
                    value = jnp.concatenate([head_ref[:, lanes], value[8:]], 0)
                local = mm(bt_ref[at // group_width, :, rows], (value * weight).astype(BF16))
                if state is None:
                    state = local
                else:
                    h_ref[c - 1, :, lanes] = state.astype(BF16)
                    state = local + decay[2 + c : 3 + c, :] * state
            sends[k][:STATE, here] = state.astype(BF16)
            sends[k][STATE:, here] = decay.astype(BF16)


def states(tail, part, taps, age, tab, d, xc, bc, cc):
    tok, channels = xc.shape
    gn = bc.shape[1]
    width = part.shape[1]
    piece = jax.ShapeDtypeStruct((STATE + 8, channels // CLUSTER), BF16)
    same = [jax.ShapeDtypeStruct(value.shape, value.dtype) for value in (xc, bc, cc)]
    return pl.pallas_call(
        state_kernel,
        out_shape=(*same, jax.ShapeDtypeStruct((tok // SUB - 1, STATE, channels), BF16)) + (piece,) * CLUSTER,
        in_specs=[VMEM] * 9,
        out_specs=(VMEM,) * (4 + CLUSTER),
        scratch_shapes=[
            pltpu.VMEM((16, width), F32),
            pltpu.VMEM((8, width), F32),
            pltpu.VMEM((gn // STATE, STATE, tok), BF16),
        ],
        input_output_aliases={6: 0, 7: 1, 8: 2},
        compiler_params=params(),
        cost_estimate=cost(tok * STATE * channels * 4, tok * channels * 4),
        name="state",
    )(tail, part, taps, age, tab, d, xc, bc, cc)


def scan_kernel(*refs):
    pieces = refs[:CLUSTER]
    local_ref, pre_ref, total_ref = refs[CLUSTER:]
    mine = lax.axis_index("seq") % CLUSTER

    def in_order(values):
        bit = 1
        while bit < CLUSTER:
            odd = (mine & bit) != 0
            values = [jnp.where(odd, values[i ^ bit], values[i]) for i in range(CLUSTER)]
            bit *= 2
        return values

    owned = total_ref.shape[1]
    tables = [ref[STATE:, :].astype(F32) for ref in pieces]
    decays = in_order([row[0:1] + (row[1:2] + row[2:3]) for row in tables])
    pre = jnp.ones((1, owned), F32)
    for i in range(CLUSTER):
        pre_ref[i] = jnp.broadcast_to(pre, (8, owned))
        pre = pre * decays[i]
    pre_ref[CLUSTER] = jnp.broadcast_to(pre, (8, owned))
    for at in range(0, owned, LANES):
        lanes = slice(at, at + LANES)
        for low in range(0, STATE, 64):
            rows = slice(low, low + 64)
            values = in_order([ref[rows, lanes].astype(F32) for ref in pieces])
            local_ref[0, rows, lanes] = jnp.zeros((64, LANES), F32)
            state = values[0]
            for i in range(1, CLUSTER):
                local_ref[i, rows, lanes] = state
                state = decays[i][:, lanes] * state + values[i]
            total_ref[rows, lanes] = state.astype(BF16)


def scan_blocks(pieces):
    owned = pieces[0].shape[1]
    return pl.pallas_call(
        scan_kernel,
        out_shape=(
            jax.ShapeDtypeStruct((CLUSTER, STATE, owned), F32),
            jax.ShapeDtypeStruct((CLUSTER + 1, 8, owned), F32),
            jax.ShapeDtypeStruct((STATE, owned), BF16),
        ),
        in_specs=[VMEM] * CLUSTER,
        out_specs=(VMEM,) * 3,
        compiler_params=params(),
        cost_estimate=cost(CLUSTER * STATE * owned * 2, CLUSTER * STATE * owned * 6),
        name="cluster_scan",
    )(*pieces)


def join_kernel(before_ref, local_ref, pre_ref, *outs):
    index = lax.axis_index("seq")
    mine = index % CLUSTER
    before = jnp.where(index >= CLUSTER, before_ref[...].astype(F32), 0.0)
    for k in range(CLUSTER):
        block = mine ^ k
        outs[k][...] = (local_ref[block] + pre_ref[block][0:1] * before).astype(BF16)


def join(before, local, pre):
    owned = local.shape[2]
    return pl.pallas_call(
        join_kernel,
        out_shape=(jax.ShapeDtypeStruct((STATE, owned), BF16),) * CLUSTER,
        in_specs=[VMEM] * 3,
        out_specs=(VMEM,) * CLUSTER,
        compiler_params=params(),
        cost_estimate=cost(CLUSTER * STATE * owned * 2, CLUSTER * STATE * owned * 6),
        name="join",
    )(before, local, pre)


def group_at(turn, groups):
    return (lax.axis_index("seq") % CLUSTER) // (CLUSTER // groups) ^ turn


def intra_kernel(
    turn,
    groups,
    head_dim,
    xc_ref,
    bc_ref,
    cc_ref,
    h_ref,
    tab_ref,
    tab0_ref,
    col_ref,
    row_ref,
    age_ref,
    gate_ref,
    part_ref,
    scale_ref,
    hot_ref,
    hot0_ref,
):
    sub = pl.program_id(0)
    group = group_at(turn, groups)
    width = xc_ref.shape[1]
    per_group = width // head_dim
    heads = per_group * groups

    @pl.when(sub == 0)
    def _():
        hot_ref[...] = spread(2 * heads, 4 * heads, group * per_group, heads, width, head_dim)
        hot0_ref[...] = spread(0, 2 * heads, group * per_group, heads, width, head_dim)

    back = lax.broadcasted_iota(jnp.int32, (SUB, SUB), 0) - lax.broadcasted_iota(jnp.int32, (SUB, SUB), 1)
    keep = (back >= 0) & (back <= age_ref[...])
    c_blk = cc_ref[...]
    scores = lax.dot_general(c_blk, bc_ref[...], (((1,), (1,)), ((), ())), preferred_element_type=F32)
    scores = jnp.where(keep, scores, 0.0)
    col = pltpu.roll(col_ref[...], LANES - (2 * heads + group * per_group), 1)
    lane = lax.broadcasted_iota(jnp.int32, (SUB, LANES), 1)
    per_tile = LANES // head_dim
    for tile in range(per_group // per_tile):
        lanes = slice(tile * LANES, (tile + 1) * LANES)
        x_tile = xc_ref[:, lanes].astype(F32)
        left, right = [], []
        for i in range(per_tile):
            head = tile * per_tile + i
            gap = col[:, head : head + 1] + row_ref[head : head + 1, :]
            left.append((jnp.exp2(jnp.minimum(gap, 80.0)) * scores).astype(BF16))
            mine = (lane >= i * head_dim) & (lane < (i + 1) * head_dim)
            right.append(jnp.where(mine, x_tile, 0.0).astype(BF16))
        inner = mm(jnp.concatenate(left, 1), jnp.concatenate(right, 0))
        inner = inner + mm(c_blk, h_ref[0, :, lanes]) * mm(tab_ref[...], hot_ref[:, lanes])
        gate = silu(gate_ref[:, lanes].astype(F32))
        part_ref[:, lanes] = inner * gate
        scale_ref[:, lanes] = mm(tab0_ref[...], hot0_ref[:, lanes]) * gate


def intra(turn, xc, bc, cc, h, tab, tab0, col, row, age, gate):
    tok, channels = xc.shape
    heads = row.shape[0]
    head_dim = channels // heads
    groups = bc.shape[1] // STATE
    width = channels // groups
    out = jax.ShapeDtypeStruct((tok, width), F32)
    return pl.pallas_call(
        functools.partial(intra_kernel, turn, groups, head_dim),
        out_shape=(out, out),
        grid=(tok // SUB,),
        in_specs=[
            pl.BlockSpec((SUB, width), lambda i: (i, group_at(turn, groups))),
            pl.BlockSpec((SUB, STATE), lambda i: (i, group_at(turn, groups))),
            pl.BlockSpec((SUB, STATE), lambda i: (i, group_at(turn, groups))),
            pl.BlockSpec((1, STATE, width), lambda i: (jnp.maximum(i - 1, 0), 0, group_at(turn, groups))),
            pl.BlockSpec((SUB, LANES), lambda i: (i, 0)),
            pl.BlockSpec((SUB, 2 * heads), lambda i: (i, 0)),
            pl.BlockSpec((SUB, LANES), lambda i: (i, 0)),
            pl.BlockSpec((heads // groups, SUB), lambda i: (group_at(turn, groups), i)),
            pl.BlockSpec((SUB, LANES), lambda i: (i, 0)),
            pl.BlockSpec((SUB, width), lambda i: (i, group_at(turn, groups))),
        ],
        out_specs=(pl.BlockSpec((SUB, width), lambda i: (i, 0)),) * 2,
        scratch_shapes=[pltpu.VMEM((4 * heads, width), BF16), pltpu.VMEM((2 * heads, width), BF16)],
        compiler_params=params(16),
        cost_estimate=cost(tok * SUB * width * 4, tok * width * 12, tok * SUB * width // head_dim),
        name="intra",
    )(xc, bc, cc, h, tab, tab0, col, row, age, gate)


def final_kernel(turn, groups, *refs):
    cc_ref, gain_ref, part_ref, scale_ref = refs[:4]
    per_group = CLUSTER // groups
    pieces = refs[4 : 4 + per_group]
    out_ref, y_ref = refs[-2:]
    width = part_ref.shape[1]
    mine = lax.axis_index("seq") % CLUSTER
    owned = width // per_group
    squares = None
    for k in range(per_group):
        for part in range(owned // CHUNK):
            at = ((mine ^ k) % per_group) * owned + part * CHUNK
            lanes = pl.ds(pl.multiple_of(at, CHUNK), CHUNK)
            carried = mm(cc_ref[...], pieces[k][:, part * CHUNK : (part + 1) * CHUNK])
            value = part_ref[:, lanes] + carried * scale_ref[:, lanes]
            y_ref[:, lanes] = value
            square = value * value
            for i in range(CHUNK // LANES):
                piece = square[:, i * LANES : (i + 1) * LANES]
                squares = piece if squares is None else squares + piece
    factor = lax.rsqrt(jnp.sum(squares, axis=1, keepdims=True) * (1.0 / width) + norm_eps)
    out_ref[...] = (y_ref[...] * factor * gain_ref[...]).astype(BF16)


def final(turn, cc, gain, part, scale, pieces, so_far=None):
    tok, width = part.shape
    groups = CLUSTER // len(pieces)
    channels = width * groups
    rows = 128
    operands = (cc, gain, part, scale, *pieces) + (() if so_far is None else (so_far,))
    return pl.pallas_call(
        functools.partial(final_kernel, turn, groups),
        out_shape=jax.ShapeDtypeStruct((tok, channels), BF16),
        grid=(tok // rows,),
        in_specs=[
            pl.BlockSpec((rows, STATE), lambda i: (i, group_at(turn, groups))),
            pl.BlockSpec((1, width), lambda i: (0, group_at(turn, groups))),
            pl.BlockSpec((rows, width), lambda i: (i, 0)),
            pl.BlockSpec((rows, width), lambda i: (i, 0)),
        ]
        + [VMEM] * len(pieces)
        + ([] if so_far is None else [ANY]),
        out_specs=pl.BlockSpec((rows, width), lambda i: (i, group_at(turn, groups))),
        scratch_shapes=[pltpu.VMEM((rows, width), F32)],
        input_output_aliases={} if so_far is None else {len(operands) - 1: 0},
        compiler_params=params(16),
        cost_estimate=cost(tok * STATE * width * 2, tok * width * 8),
        name="final",
    )(*operands)


def moved(value, hop):
    count = lax.axis_size("seq")
    return lax.ppermute(value, "seq", [(i, hop(i)) for i in range(count) if 0 <= hop(i) < count])


def exchanged(pieces, order):
    arrived = {0: pieces[0]}
    for k in order:
        arrived[k] = moved(pieces[k], lambda i, k=k: i ^ k)
    return [arrived[k] for k in range(CLUSTER)]


def before_cluster(total, pre):
    clusters = lax.axis_size("seq") // CLUSTER
    if clusters == 1:
        return jnp.zeros_like(total)
    if clusters == 2:
        return moved(total, lambda i: i ^ CLUSTER)
    shift = lambda value, steps: moved(value, lambda i: i + steps * CLUSTER)
    state, decay = shift((total.astype(F32), pre[CLUSTER, 0]), 1)
    step = 1
    while step < clusters - 1:
        earlier, fell = shift((state, decay), step)
        state, decay = state + decay[None, :] * earlier, decay * fell
        step *= 2
    return state


def tied(values, other):
    *values, _ = lax.optimization_barrier((*values, other))
    return values


def on_device(
    x_input,
    b_input,
    c_input,
    dt_input,
    decay_rate,
    gate_input,
    taps_x,
    taps_b,
    taps_c,
    norm_gain,
    doc_lengths,
):
    groups = b_input.shape[1] // STATE
    count = lax.axis_size("seq")
    pin = lambda value: pltpu.with_memory_space_constraint(value, pltpu.HBM)
    x_input, b_input, c_input, doc_lengths = pin(x_input), pin(b_input), pin(c_input), pin(doc_lengths)
    taps_x, taps_b, taps_c = pin(taps_x), pin(taps_b), pin(taps_c)
    ends, tab, tab0, col, row, d, age = prep(
        doc_lengths, pin(dt_input.T), pin(decay_rate[None, :]), x_input, b_input, c_input
    )
    tail = lax.ppermute(ends, "seq", [(i, (i + 1) % count) for i in range(count)])
    taps, part, xc, bc, cc = conv(age, x_input, b_input, c_input, taps_x, taps_b, taps_c)
    xc, bc, cc, h, *pieces = states(tail, part, taps, age, tab, d, xc, bc, cc)
    first = intra(0, xc, bc, cc, h, tab, tab0, col, row, age, gate_input)
    local, pre, total = scan_blocks(tied(exchanged(pieces, (3, 2, 1)), first[0]))
    second = intra(1, xc, bc, cc, h, tab, tab0, col, row, age, gate_input)
    (before,) = tied([before_cluster(total, pre)], second[0])
    entering = exchanged(join(before, local, pre), (1, 3, 2))
    share = CLUSTER // groups
    output = None
    for turn, inner in enumerate((first, second)):
        mine = entering[turn * share : (turn + 1) * share]
        output = final(turn, cc, norm_gain[None, :], *inner, mine, output)
    return output


def solution(mesh):
    rows = P(("groups", "seq"), "dp")
    placed = (rows, rows, rows, rows, P("dp"), rows, P(None, "dp"), P(None, "dp"), P(None, "dp"), P("dp"), P("groups"))
    return jax.shard_map(on_device, mesh=mesh, in_specs=placed, out_specs=rows, check_vma=False)
```

```python
import functools

import jax
import jax.numpy as jnp
from jax import lax
from jax.experimental import pallas as pl
from jax.experimental.pallas import tpu as pltpu
from jax.sharding import PartitionSpec as P

STATE = 128
SUB = 128
CHUNK = 256
LANES = 128
ROWS = 32
CLUSTER = 4
LOG2E = 1.4426950408889634
norm_eps = 1e-05

F32 = jnp.float32
BF16 = jnp.bfloat16
VMEM = pl.BlockSpec(memory_space=pltpu.VMEM)
ANY = pl.BlockSpec(memory_space=pl.ANY)
HBM = pl.BlockSpec(memory_space=pltpu.HBM)


def params(mib=24):
    return pltpu.CompilerParams(vmem_limit_bytes=mib << 20)


def cost(flops, moved, transcendentals=0):
    return pl.CostEstimate(flops=flops, bytes_accessed=moved, transcendentals=transcendentals)


def doc_edges(dl_ref):
    edges = [0]
    for i in range(dl_ref.shape[0] - 1):
        edges.append(edges[-1] + dl_ref[i])
    return edges


def doc_start(token, edges):
    start = jnp.zeros_like(token)
    for edge in edges[1:]:
        start = jnp.where(token >= edge, jnp.maximum(start, edge), start)
    return start


def split2(value):
    high = value.astype(BF16)
    return high, (value - high.astype(F32)).astype(BF16)


def split3(value):
    high = value.astype(BF16)
    rest = value - high.astype(F32)
    mid = rest.astype(BF16)
    return high, mid, (rest - mid.astype(F32)).astype(BF16)


def mm(a, b):
    return jnp.dot(a, b, preferred_element_type=F32)


def silu(value):
    half = 0.5 * value
    return half + half * jnp.tanh(half)


def spread(base, rows, first_head, heads, width, head_dim):
    row = lax.broadcasted_iota(jnp.int32, (rows, width), 0) - (base + first_head)
    head = lax.broadcasted_iota(jnp.int32, (rows, width), 1) // head_dim
    return jnp.where((row == head) | (row == head + heads), 1.0, 0.0).astype(BF16)


def start_all(copies):
    for copy in copies:
        copy.start()


def wait_all(copies):
    for copy in copies:
        copy.wait()


def tables(row0, edges, dt_ref, rate_ref, tab_ref, tab0_ref, col_ref, row_ref, d_ref):
    heads, tok = dt_ref.shape
    upto = jnp.where(
        lax.broadcasted_iota(jnp.int32, (SUB, SUB), 0) <= lax.broadcasted_iota(jnp.int32, (SUB, SUB), 1), 1.0, 0.0
    ).astype(BF16)
    rate = jnp.concatenate([rate_ref[...], jnp.zeros((1, LANES - heads), F32)], 1)
    rate = jnp.broadcast_to(rate, (LANES, LANES)).T[:heads]
    total = jnp.zeros((heads, 1), F32)
    decays = []
    for c in range(tok // SUB):
        span = slice(c * SUB, (c + 1) * SUB)
        first = row0 + c * SUB
        dt = dt_ref[:, span]
        step = jnp.maximum(dt, 0.0) + jnp.log1p(jnp.exp(-jnp.abs(dt)))
        parts = split3(-(step * rate))
        cum = mm(parts[0], upto) + (mm(parts[1], upto) + mm(parts[2], upto))
        last = cum[:, SUB - 1 :]
        token = first + lax.broadcasted_iota(jnp.int32, (heads, SUB), 1)
        start = doc_start(token, edges)
        last_start = doc_start(jnp.int32(first + SUB - 1), edges)
        to_end = jnp.exp(last - cum) * step * jnp.where(token >= last_start, 1.0, 0.0)
        since_sub = jnp.exp(cum) * jnp.where((start < first) & (c > 0), 1.0, 0.0)
        since_block = jnp.exp(cum + total) * jnp.where(start < row0, 1.0, 0.0)
        first_pair = [part.astype(F32) for part in (*split2(to_end), *split2(since_sub))]
        second_pair = [part.astype(F32) for part in split2(since_block)] + [cum * LOG2E, jnp.zeros_like(cum)]
        tab_ref[span, :] = jnp.concatenate(first_pair, 0).T.astype(BF16)
        second = jnp.concatenate(second_pair, 0).T
        tab0_ref[span, :] = second[:, : 2 * heads].astype(BF16)
        col_ref[span, :] = second
        row_ref[:, span] = (jnp.log(step) - cum) * LOG2E
        decays.append(jnp.exp(last) * jnp.where(last_start < first, 1.0, 0.0))
        total = total + last
    end_start = doc_start(jnp.int32(row0 + tok - 1), edges)
    whole = jnp.exp(total) * jnp.where(end_start < row0, 1.0, 0.0)
    columns = [part.astype(F32) for part in split3(whole)] + decays[1:]
    columns.append(jnp.zeros((heads, LANES - len(columns)), F32))
    columns = jnp.concatenate([jnp.concatenate(columns, 1), jnp.zeros((LANES - heads, LANES), F32)], 0)
    halves = [part.astype(F32)[:, :heads] for part in split2(columns.T[:8])]
    d_ref[...] = jnp.concatenate(halves, 1).astype(BF16)


def prep_kernel(
    dl_hbm,
    dt_hbm,
    rate_hbm,
    x_hbm,
    b_hbm,
    c_hbm,
    ends_ref,
    tab_ref,
    tab0_ref,
    col_ref,
    row_ref,
    d_ref,
    age_ref,
    dl_ref,
    dt_ref,
    rate_ref,
    sem,
):
    tok = x_hbm.shape[0]
    small = [
        pltpu.make_async_copy(hbm, ref, sem.at[i])
        for i, (hbm, ref) in enumerate(((dl_hbm, dl_ref), (dt_hbm, dt_ref), (rate_hbm, rate_ref)))
    ]
    start_all(small)
    ends, low = [], 0
    for i, ref in enumerate((x_hbm, b_hbm, c_hbm)):
        width = ref.shape[1]
        ends.append(
            pltpu.make_async_copy(ref.at[pl.ds(tok - 8, 8), :], ends_ref.at[:, pl.ds(low, width)], sem.at[3 + i])
        )
        low += width
    start_all(ends)
    wait_all(small)
    row0 = lax.axis_index("seq") * tok
    edges = doc_edges(dl_ref)
    tables(row0, edges, dt_ref, rate_ref, tab_ref, tab0_ref, col_ref, row_ref, d_ref)
    token = row0 + lax.broadcasted_iota(jnp.int32, (tok, LANES), 0)
    age_ref[...] = token - doc_start(token, edges)
    wait_all(ends)


def prep(doc_lengths, dt_t, rate, x, b, c):
    heads, tok = dt_t.shape
    shape = jax.ShapeDtypeStruct
    return pl.pallas_call(
        prep_kernel,
        out_shape=(
            shape((8, x.shape[1] + b.shape[1] + c.shape[1]), BF16),
            shape((tok, LANES), BF16),
            shape((tok, 2 * heads), BF16),
            shape((tok, LANES), F32),
            shape((heads, tok), F32),
            shape((8, 2 * heads), BF16),
            shape((tok, LANES), jnp.int32),
        ),
        in_specs=[HBM] * 6,
        out_specs=(VMEM,) * 7,
        scratch_shapes=[
            pltpu.SMEM(doc_lengths.shape, jnp.int32),
            pltpu.VMEM((heads, tok), F32),
            pltpu.VMEM((1, heads), F32),
            pltpu.SemaphoreType.DMA((6,)),
        ],
        compiler_params=params(16),
        name="prep",
    )(doc_lengths, dt_t, rate, x, b, c)


def place_of(k, owned):
    return pl.multiple_of((lax.axis_index("seq") % CLUSTER ^ k) * owned, owned)


def fill_masks(age_ref, mask_ref):
    for back in range(1, mask_ref.shape[0] + 1):
        mask_ref[back - 1] = jnp.where(age_ref[...] >= back, 1.0, 0.0)


def convolve(ext_ref, mask_ref, taps, emit):
    tok = ext_ref.shape[0] - 8
    repeats = ext_ref.shape[1] // LANES
    for low in range(0, tok, ROWS):
        total = ext_ref[8 + low : 8 + low + ROWS, :] * taps[-1]
        for back in range(1, len(taps)):
            mask = jnp.concatenate([mask_ref[back - 1, low : low + ROWS, :]] * repeats, 1)
            window = ext_ref[8 + low - back : 8 + low - back + ROWS, :]
            total = total + (window * taps[-1 - back]) * mask
        emit(low, total)


def state_of(at, heads, head_dim, bt_ref, tab_ref, d_ref, x_rows, h_put):
    one_hot = spread(0, 2 * heads, at // head_dim, heads, CHUNK, head_dim)
    decay = mm(d_ref[...], one_hot)
    tok = tab_ref.shape[0]
    state = None
    for c in range(tok // SUB):
        rows = slice(c * SUB, (c + 1) * SUB)
        weight = mm(tab_ref[rows, : 2 * heads], one_hot)
        local = mm(bt_ref[:, rows], (x_rows(c) * weight).astype(BF16))
        if state is None:
            state = local
        else:
            h_put(c - 1, state.astype(BF16))
            state = local + decay[2 + c : 3 + c, :] * state
    return state.astype(BF16), decay.astype(BF16)


def conv_kernel(
    age_ref,
    x_hbm,
    b_hbm,
    taps_x_hbm,
    taps_b_hbm,
    taps_x_ref,
    taps_b_ref,
    part_x_ref,
    part_b_ref,
    xc_ref,
    bc_ref,
    in_ref,
    ext_ref,
    mask_ref,
    sem,
    in_sem,
):
    channels = x_hbm.shape[1]
    owned = channels // CLUSTER
    per = owned // CHUNK
    chunks = (CLUSTER - 1) * per
    small = [
        pltpu.make_async_copy(taps_x_hbm, taps_x_ref, sem.at[0]),
        pltpu.make_async_copy(taps_b_hbm, taps_b_ref, sem.at[1]),
    ]
    start_all(small)

    def place(i):
        return pl.multiple_of(place_of(i // per + 1, owned) + (i % per) * CHUNK, CHUNK)

    def fetch(i):
        return pltpu.make_async_copy(x_hbm.at[:, pl.ds(place(i), CHUNK)], in_ref.at[i], in_sem.at[i])

    for i in range(chunks):
        fetch(i).start()
    fetch_b = pltpu.make_async_copy(b_hbm, in_ref.at[chunks], in_sem.at[chunks])
    fetch_b.start()
    fill_masks(age_ref, mask_ref)
    ext_ref[:8, :] = jnp.zeros((8, CHUNK), F32)
    wait_all(small)
    taps_len = taps_x_ref.shape[0]

    def body(i, carry):
        fetch(i).wait()
        k = i // per
        inner = pl.ds(pl.multiple_of((i % per) * CHUNK, CHUNK), CHUNK)
        ext_ref[8:, :] = in_ref[i].astype(F32)

        def emit(low, total):
            if low == 0:
                part_x_ref[k, :, inner] = total[:8]
            xc_ref[k, low : low + ROWS, inner] = silu(total).astype(BF16)

        convolve(ext_ref, mask_ref, [taps_x_ref[j : j + 1, pl.ds(place(i), CHUNK)] for j in range(taps_len)], emit)
        return carry

    lax.fori_loop(0, chunks, body, 0)
    fetch_b.wait()
    ext_ref[8:, :] = in_ref[chunks].astype(F32)

    def emit_b(low, total):
        if low == 0:
            part_b_ref[...] = total[:8]
        bc_ref[low : low + ROWS, :] = silu(total).astype(BF16)

    convolve(ext_ref, mask_ref, [taps_b_ref[j : j + 1, :] for j in range(taps_len)], emit_b)


def conv(age, x, b, taps_x, taps_b):
    tok, channels = x.shape
    gn = b.shape[1]
    owned = channels // CLUSTER
    places = (CLUSTER - 1) * (owned // CHUNK) + 1
    shape = jax.ShapeDtypeStruct
    return pl.pallas_call(
        conv_kernel,
        out_shape=(
            shape(taps_x.shape, F32),
            shape(taps_b.shape, F32),
            shape((CLUSTER - 1, 8, owned), F32),
            shape((8, gn), F32),
            shape((CLUSTER - 1, tok, owned), BF16),
            shape((tok, gn), BF16),
        ),
        in_specs=[VMEM] + [HBM] * 4,
        out_specs=(VMEM,) * 6,
        scratch_shapes=[
            pltpu.VMEM((places, tok, CHUNK), BF16),
            pltpu.VMEM((tok + 8, CHUNK), F32),
            pltpu.VMEM((taps_x.shape[0] - 1, tok, LANES), F32),
            pltpu.SemaphoreType.DMA((2,)),
            pltpu.SemaphoreType.DMA((places,)),
        ],
        compiler_params=params(16),
        cost_estimate=cost(tok * channels * 16, tok * channels * 4, tok * channels),
        name="conv",
    )(age, x, b, taps_x, taps_b)


def state_kernel(
    tail_ref,
    part_x_ref,
    part_b_ref,
    taps_x_ref,
    taps_b_ref,
    age_ref,
    tab_ref,
    d_ref,
    xc_in,
    bc_in,
    xc_ref,
    bc_ref,
    bt_ref,
    h_ref,
    *rest,
):
    sends = rest[: CLUSTER - 1]
    ext_ref, head_ref, head_b_ref = rest[CLUSTER - 1 :]
    pieces, tok, owned = xc_in.shape
    gn = bc_in.shape[1]
    channels = owned * CLUSTER
    heads = d_ref.shape[1] // 2
    head_dim = channels // heads
    taps_len = taps_x_ref.shape[0]
    ext_ref[:8, :] = tail_ref[...].astype(F32)
    ext_ref[8:, :] = jnp.zeros_like(ext_ref[8:, :])

    def head_of(part, lanes, taps, width):
        total = part
        age = jnp.concatenate([age_ref[:8, :]] * (width // LANES), 1)
        for back in range(1, taps_len):
            total = total + jnp.where(age >= back, ext_ref[8 - back : 16 - back, lanes] * taps[-1 - back], 0.0)
        return silu(total).astype(BF16)

    head = head_of(
        part_b_ref[...], slice(channels, channels + gn), [taps_b_ref[j : j + 1, :] for j in range(taps_len)], gn
    )
    bc_ref[:8, :] = head
    head_b_ref[...] = head.astype(F32)
    for group in range(gn // STATE):
        lanes = slice(group * STATE, (group + 1) * STATE)
        b_blk = jnp.concatenate([head_b_ref[:, lanes], bc_in[:, lanes].astype(F32)[8:]], 0)
        bt_ref[group] = b_blk.T.astype(BF16)
    for k in range(pieces):
        at = place_of(k + 1, owned)
        lanes = pl.ds(at, owned)
        head = head_of(part_x_ref[k], lanes, [taps_x_ref[j : j + 1, lanes] for j in range(taps_len)], owned)
        xc_ref[k, :8, :] = head
        head_ref[k] = head.astype(F32)
        for part in range(owned // CHUNK):
            here = slice(part * CHUNK, (part + 1) * CHUNK)

            def x_rows(c):
                value = xc_in[k, c * SUB : (c + 1) * SUB, here].astype(F32)
                return jnp.concatenate([head_ref[k, :, here], value[8:]], 0) if c == 0 else value

            def h_put(c, value):
                h_ref[k, c, :, here] = value

            group = at // (channels // (gn // STATE))
            state, decay = state_of(
                at + part * CHUNK, heads, head_dim, bt_ref.at[group], tab_ref, d_ref, x_rows, h_put
            )
            sends[k][:STATE, here] = state
            sends[k][STATE:, here] = decay


def states(tail, part_x, part_b, taps_x, taps_b, age, tab, d, xc, bc):
    pieces, tok, owned = xc.shape
    gn = bc.shape[1]
    shape = jax.ShapeDtypeStruct
    return pl.pallas_call(
        state_kernel,
        out_shape=(
            shape(xc.shape, BF16),
            shape(bc.shape, BF16),
            shape((gn // STATE, STATE, tok), BF16),
            shape((pieces, tok // SUB - 1, STATE, owned), BF16),
        )
        + (shape((STATE + 8, owned), BF16),) * pieces,
        in_specs=[VMEM] * 10,
        out_specs=(VMEM,) * (4 + pieces),
        scratch_shapes=[
            pltpu.VMEM((16, tail.shape[1]), F32),
            pltpu.VMEM((pieces, 8, owned), F32),
            pltpu.VMEM((8, gn), F32),
        ],
        input_output_aliases={8: 0, 9: 1},
        compiler_params=params(16),
        cost_estimate=cost(tok * STATE * owned * pieces * 4, tok * owned * pieces * 4),
        name="state",
    )(tail, part_x, part_b, taps_x, taps_b, age, tab, d, xc, bc)


def own_kernel(
    tail_ref,
    age_ref,
    tab_ref,
    d_ref,
    bt_ref,
    taps_x_ref,
    x_hbm,
    c_hbm,
    taps_c_hbm,
    xc_ref,
    cc_ref,
    h_ref,
    send_ref,
    in_ref,
    taps_c_ref,
    ext_ref,
    mask_ref,
    sem,
):
    tok, channels = x_hbm.shape
    gn = c_hbm.shape[1]
    owned = channels // CLUSTER
    per = owned // CHUNK
    heads = d_ref.shape[1] // 2
    head_dim = channels // heads
    taps_len = taps_x_ref.shape[0]
    at = place_of(0, owned)
    copies = [
        pltpu.make_async_copy(
            x_hbm.at[:, pl.ds(pl.multiple_of(at + part * CHUNK, CHUNK), CHUNK)], in_ref.at[part], sem.at[part]
        )
        for part in range(per)
    ]
    copies.append(pltpu.make_async_copy(c_hbm, in_ref.at[per], sem.at[per]))
    copies.append(pltpu.make_async_copy(taps_c_hbm, taps_c_ref, sem.at[per + 1]))
    start_all(copies)
    fill_masks(age_ref, mask_ref)
    wait_all(copies)
    for part in range(per + 1):
        here = slice(part * CHUNK, (part + 1) * CHUNK)
        if part < per:
            lanes = pl.ds(pl.multiple_of(at + part * CHUNK, CHUNK), CHUNK)
            taps = [taps_x_ref[j : j + 1, lanes] for j in range(taps_len)]
        else:
            lanes = slice(channels + gn, channels + 2 * gn)
            taps = [taps_c_ref[j : j + 1, :] for j in range(taps_len)]
        ext_ref[:8, :] = tail_ref[:, lanes].astype(F32)
        ext_ref[8:, :] = in_ref[part].astype(F32)

        def emit(low, total):
            value = silu(total).astype(BF16)
            if part < per:
                xc_ref[0, low : low + ROWS, here] = value
            else:
                cc_ref[low : low + ROWS, :] = value

        convolve(ext_ref, mask_ref, taps, emit)
        if part < per:

            def h_put(c, value):
                h_ref[0, c, :, here] = value

            group = at // (channels // (gn // STATE))
            state, decay = state_of(
                at + part * CHUNK,
                heads,
                head_dim,
                bt_ref.at[group],
                tab_ref,
                d_ref,
                lambda c: xc_ref[0, c * SUB : (c + 1) * SUB, here].astype(F32),
                h_put,
            )
            send_ref[:STATE, here] = state
            send_ref[STATE:, here] = decay


def own(tail, age, tab, d, bt, taps_x, x, c, taps_c):
    tok, channels = x.shape
    gn = c.shape[1]
    owned = channels // CLUSTER
    places = owned // CHUNK + 1
    shape = jax.ShapeDtypeStruct
    return pl.pallas_call(
        own_kernel,
        out_shape=(
            shape((1, tok, owned), BF16),
            shape((tok, gn), BF16),
            shape((1, tok // SUB - 1, STATE, owned), BF16),
            shape((STATE + 8, owned), BF16),
        ),
        in_specs=[VMEM] * 6 + [HBM] * 3,
        out_specs=(VMEM,) * 4,
        scratch_shapes=[
            pltpu.VMEM((places, tok, CHUNK), BF16),
            pltpu.VMEM(taps_c.shape, F32),
            pltpu.VMEM((tok + 8, CHUNK), F32),
            pltpu.VMEM((taps_c.shape[0] - 1, tok, LANES), F32),
            pltpu.SemaphoreType.DMA((places + 1,)),
        ],
        compiler_params=params(16),
        cost_estimate=cost(tok * owned * 16 + tok * STATE * owned * 4, tok * owned * 8, tok * owned),
        name="own",
    )(tail, age, tab, d, bt, taps_x, x, c, taps_c)


def scan_kernel(*refs):
    pieces = refs[:CLUSTER]
    local_ref, pre_ref, total_ref = refs[CLUSTER:]
    mine = lax.axis_index("seq") % CLUSTER

    def in_order(values):
        bit = 1
        while bit < CLUSTER:
            odd = (mine & bit) != 0
            values = [jnp.where(odd, values[i ^ bit], values[i]) for i in range(CLUSTER)]
            bit *= 2
        return values

    owned = total_ref.shape[1]
    tables = [ref[STATE:, :].astype(F32) for ref in pieces]
    decays = in_order([row[0:1] + (row[1:2] + row[2:3]) for row in tables])
    pre = jnp.ones((1, owned), F32)
    for i in range(CLUSTER):
        pre_ref[i] = jnp.broadcast_to(pre, (8, owned))
        pre = pre * decays[i]
    pre_ref[CLUSTER] = jnp.broadcast_to(pre, (8, owned))
    for at in range(0, owned, LANES):
        lanes = slice(at, at + LANES)
        for low in range(0, STATE, 64):
            rows = slice(low, low + 64)
            values = in_order([ref[rows, lanes].astype(F32) for ref in pieces])
            local_ref[0, rows, lanes] = jnp.zeros((64, LANES), F32)
            state = values[0]
            for i in range(1, CLUSTER):
                local_ref[i, rows, lanes] = state
                state = decays[i][:, lanes] * state + values[i]
            total_ref[rows, lanes] = state.astype(BF16)


def scan_blocks(pieces):
    owned = pieces[0].shape[1]
    return pl.pallas_call(
        scan_kernel,
        out_shape=(
            jax.ShapeDtypeStruct((CLUSTER, STATE, owned), F32),
            jax.ShapeDtypeStruct((CLUSTER + 1, 8, owned), F32),
            jax.ShapeDtypeStruct((STATE, owned), BF16),
        ),
        in_specs=[VMEM] * CLUSTER,
        out_specs=(VMEM,) * 3,
        compiler_params=params(),
        cost_estimate=cost(CLUSTER * STATE * owned * 2, CLUSTER * STATE * owned * 6),
        name="cluster_scan",
    )(*pieces)


def join_kernel(before_ref, local_ref, pre_ref, *outs):
    index = lax.axis_index("seq")
    mine = index % CLUSTER
    before = jnp.where(index >= CLUSTER, before_ref[...].astype(F32), 0.0)
    for k in range(CLUSTER):
        block = mine ^ k
        outs[k][...] = (local_ref[block] + pre_ref[block][0:1] * before).astype(BF16)


def join(before, local, pre):
    owned = local.shape[2]
    return pl.pallas_call(
        join_kernel,
        out_shape=(jax.ShapeDtypeStruct((STATE, owned), BF16),) * CLUSTER,
        in_specs=[VMEM] * 3,
        out_specs=(VMEM,) * CLUSTER,
        compiler_params=params(),
        cost_estimate=cost(CLUSTER * STATE * owned * 2, CLUSTER * STATE * owned * 6),
        name="join",
    )(before, local, pre)


def group_at(turn, groups):
    return (lax.axis_index("seq") % CLUSTER) // (CLUSTER // groups) ^ turn


def intra_kernel(pieces, heads, head_dim, *refs):
    bc_ref, cc_ref, tab_ref, tab0_ref, col_ref, row_ref, age_ref = refs[:7]
    count = len(pieces)
    xs, hs, gates = refs[7 : 7 + count], refs[7 + count : 7 + 2 * count], refs[7 + 2 * count : 7 + 3 * count]
    parts, scales = refs[7 + 3 * count : 7 + 4 * count], refs[7 + 4 * count : 7 + 5 * count]
    hot_ref, hot0_ref = refs[7 + 5 * count :]
    owned = parts[0].shape[1]
    per_piece = owned // head_dim
    mine = lax.axis_index("seq") % CLUSTER

    @pl.when(pl.program_id(0) == 0)
    def _():
        for p, k in enumerate(pieces):
            hot_ref[p] = spread(2 * heads, 4 * heads, (mine ^ k) * per_piece, heads, owned, head_dim)
            hot0_ref[p] = spread(0, 2 * heads, (mine ^ k) * per_piece, heads, owned, head_dim)

    back = lax.broadcasted_iota(jnp.int32, (SUB, SUB), 0) - lax.broadcasted_iota(jnp.int32, (SUB, SUB), 1)
    keep = (back >= 0) & (back <= age_ref[...])
    c_blk = cc_ref[...]
    scores = lax.dot_general(c_blk, bc_ref[...], (((1,), (1,)), ((), ())), preferred_element_type=F32)
    scores = jnp.where(keep, scores, 0.0)
    lane = lax.broadcasted_iota(jnp.int32, (SUB, LANES), 1)
    per_tile = LANES // head_dim
    for p, k in enumerate(pieces):
        first = (mine ^ k) * per_piece
        col = pltpu.roll(col_ref[...], LANES - (2 * heads + first), 1)
        row = row_ref[pl.ds(pl.multiple_of(first, per_piece), per_piece), :]
        for tile in range(owned // LANES):
            lanes = slice(tile * LANES, (tile + 1) * LANES)
            x_tile = xs[p][0, :, lanes].astype(F32)
            left, right = [], []
            for i in range(per_tile):
                head = tile * per_tile + i
                gap = col[:, head : head + 1] + row[head : head + 1, :]
                left.append((jnp.exp2(jnp.minimum(gap, 80.0)) * scores).astype(BF16))
                here = (lane >= i * head_dim) & (lane < (i + 1) * head_dim)
                right.append(jnp.where(here, x_tile, 0.0).astype(BF16))
            inner = mm(jnp.concatenate(left, 1), jnp.concatenate(right, 0))
            inner = inner + mm(c_blk, hs[p][0, 0, :, lanes]) * mm(tab_ref[...], hot_ref[p, :, lanes])
            gate = silu(gates[p][:, lanes].astype(F32))
            parts[p][:, lanes] = inner * gate
            scales[p][:, lanes] = mm(tab0_ref[...], hot0_ref[p, :, lanes]) * gate


def intra(turn, pieces, bc, cc, tab, tab0, col, row, age, xs, hs, gate):
    tok, gn = bc.shape
    heads = row.shape[0]
    channels = gate.shape[1]
    head_dim = channels // heads
    groups = gn // STATE
    owned = channels // CLUSTER
    count = len(pieces)
    out = jax.ShapeDtypeStruct((tok, owned), F32)

    def piece_spec(block, index):
        return [pl.BlockSpec(block, functools.partial(index, k)) for k in pieces]

    return pl.pallas_call(
        functools.partial(intra_kernel, pieces, heads, head_dim),
        out_shape=(out,) * (2 * count),
        grid=(tok // SUB,),
        in_specs=[
            pl.BlockSpec((SUB, STATE), lambda i: (i, group_at(turn, groups))),
            pl.BlockSpec((SUB, STATE), lambda i: (i, group_at(turn, groups))),
            pl.BlockSpec((SUB, tab.shape[1]), lambda i: (i, 0)),
            pl.BlockSpec((SUB, tab0.shape[1]), lambda i: (i, 0)),
            pl.BlockSpec((SUB, LANES), lambda i: (i, 0)),
            pl.BlockSpec((heads, SUB), lambda i: (0, i)),
            pl.BlockSpec((SUB, LANES), lambda i: (i, 0)),
        ]
        + piece_spec((1, SUB, owned), lambda k, i: (max(k - 1, 0), i, 0))
        + piece_spec((1, 1, STATE, owned), lambda k, i: (max(k - 1, 0), jnp.maximum(i - 1, 0), 0, 0))
        + piece_spec((SUB, owned), lambda k, i: (i, lax.axis_index("seq") % CLUSTER ^ k)),
        out_specs=(pl.BlockSpec((SUB, owned), lambda i: (i, 0)),) * (2 * count),
        scratch_shapes=[pltpu.VMEM((count, 4 * heads, owned), BF16), pltpu.VMEM((count, 2 * heads, owned), BF16)],
        compiler_params=params(16),
        cost_estimate=cost(tok * SUB * owned * count * 4, tok * owned * count * 12, tok * SUB * owned * count // head_dim),
        name="intra",
    )(bc, cc, tab, tab0, col, row, age, *xs, *hs, *([gate] * count))


def final_kernel(groups, *refs):
    cc_ref, gain_ref = refs[:2]
    parts, scales, pieces = (refs[2 + i * CLUSTER : 2 + (i + 1) * CLUSTER] for i in range(3))
    out_hbm, y_ref, put_ref, sem = refs[2 + 3 * CLUSTER :]
    tok, owned = parts[0].shape
    share = CLUSTER // groups
    rows = y_ref.shape[1]
    copies = []
    for turn in range(groups):
        group = group_at(turn, groups)
        c_lanes = pl.ds(pl.multiple_of(group * STATE, STATE), STATE)
        for low in range(0, tok, rows):
            span = slice(low, low + rows)
            c_blk = cc_ref[span, c_lanes]
            squares = None
            for i in range(share):
                k = turn * share + i
                for at in range(0, owned, CHUNK):
                    lanes = slice(at, at + CHUNK)
                    value = parts[k][span, lanes] + mm(c_blk, pieces[k][:, lanes]) * scales[k][span, lanes]
                    y_ref[i, :, lanes] = value
                    square = value * value
                    for j in range(0, CHUNK, LANES):
                        piece = square[:, j : j + LANES]
                        squares = piece if squares is None else squares + piece
            factor = lax.rsqrt(jnp.sum(squares, axis=1, keepdims=True) * (1.0 / (share * owned)) + norm_eps)
            for i in range(share):
                k = turn * share + i
                columns = pl.ds(place_of(k, owned), owned)
                put_ref[k, span, :] = (y_ref[i] * factor * gain_ref[:, columns]).astype(BF16)
                copy = pltpu.make_async_copy(
                    put_ref.at[k, span, :], out_hbm.at[span, columns], sem.at[k, low // rows]
                )
                copy.start()
                copies.append(copy)
    wait_all(copies)


def final(cc, gain, parts, scales, pieces):
    tok, owned = parts[0].shape
    groups = cc.shape[1] // STATE
    rows = 64
    return pl.pallas_call(
        functools.partial(final_kernel, groups),
        out_shape=jax.ShapeDtypeStruct((tok, owned * CLUSTER), BF16),
        in_specs=[VMEM] * (2 + 3 * CLUSTER),
        out_specs=ANY,
        scratch_shapes=[
            pltpu.VMEM((CLUSTER // groups, rows, owned), F32),
            pltpu.VMEM((CLUSTER, tok, owned), BF16),
            pltpu.SemaphoreType.DMA((CLUSTER, tok // rows)),
        ],
        compiler_params=params(16),
        cost_estimate=cost(tok * STATE * owned * CLUSTER * 2, tok * owned * CLUSTER * 8),
        name="final",
    )(cc, gain, *parts, *scales, *pieces)


def moved(value, hop):
    count = lax.axis_size("seq")
    return lax.ppermute(value, "seq", [(i, hop(i)) for i in range(count) if 0 <= hop(i) < count])


def exchanged(pieces, order):
    arrived = {0: pieces[0]}
    for k in order:
        arrived[k] = moved(pieces[k], lambda i, k=k: i ^ k)
    return [arrived[k] for k in range(CLUSTER)]


def before_cluster(total, pre):
    clusters = lax.axis_size("seq") // CLUSTER
    if clusters == 1:
        return jnp.zeros_like(total)
    if clusters == 2:
        return moved(total, lambda i: i ^ CLUSTER)
    shift = lambda value, steps: moved(value, lambda i: i + steps * CLUSTER)
    state, decay = shift((total.astype(F32), pre[CLUSTER, 0]), 1)
    step = 1
    while step < clusters - 1:
        earlier, fell = shift((state, decay), step)
        state, decay = state + decay[None, :] * earlier, decay * fell
        step *= 2
    return state


def tied(values, other):
    *values, _ = lax.optimization_barrier((*values, other))
    return values


def on_device(
    x_input,
    b_input,
    c_input,
    dt_input,
    decay_rate,
    gate_input,
    taps_x,
    taps_b,
    taps_c,
    norm_gain,
    doc_lengths,
):
    groups = b_input.shape[1] // STATE
    count = lax.axis_size("seq")
    pin = lambda value: pltpu.with_memory_space_constraint(value, pltpu.HBM)
    x_input, b_input, c_input, doc_lengths = pin(x_input), pin(b_input), pin(c_input), pin(doc_lengths)
    taps_x, taps_b, taps_c = pin(taps_x), pin(taps_b), pin(taps_c)
    ends, tab, tab0, col, row, d, age = prep(
        doc_lengths, pin(dt_input.T), pin(decay_rate[None, :]), x_input, b_input, c_input
    )
    tail = lax.ppermute(ends, "seq", [(i, (i + 1) % count) for i in range(count)])
    taps_x, taps_b, part_x, part_b, xc, bc = conv(age, x_input, b_input, taps_x, taps_b)
    xc, bc, bt, h, *sends = states(tail, part_x, part_b, taps_x, taps_b, age, tab, d, xc, bc)
    own_x, cc, own_h, own_send = own(tail, age, tab, d, bt, taps_x, x_input, c_input, taps_c)
    shared = (bc, cc, tab, tab0, col, row, age)
    share = CLUSTER // groups

    def inner(turn):
        pieces = tuple(range(turn * share, (turn + 1) * share))
        xs, hs = ([mine if k == 0 else other for k in pieces] for mine, other in ((own_x, xc), (own_h, h)))
        return intra(turn, pieces, *shared, xs, hs, gate_input)

    first = inner(0)
    arrived = tied(exchanged([own_send, *sends], (3, 2, 1)), first[0])
    local, pre, total = scan_blocks(arrived)
    later = [inner(turn) for turn in range(1, groups)]
    (before,) = tied([before_cluster(total, pre)], later[-1][0])
    entering = exchanged(join(before, local, pre), (3, 2, 1))
    parts = [part for turn in (first, *later) for part in turn[:share]]
    scales = [part for turn in (first, *later) for part in turn[share:]]
    return final(cc, norm_gain[None, :], parts, scales, entering)


def solution(mesh):
    rows = P(("groups", "seq"), "dp")
    placed = (rows, rows, rows, rows, P("dp"), rows, P(None, "dp"), P(None, "dp"), P(None, "dp"), P("dp"), P("groups"))
    return jax.shard_map(on_device, mesh=mesh, in_specs=placed, out_specs=rows, check_vma=False)
```

```python
import functools

import jax
import jax.numpy as jnp
from jax import lax
from jax.experimental import pallas as pl
from jax.experimental.pallas import tpu as pltpu
from jax.sharding import PartitionSpec as P

STATE = 128
SUB = 128
CHUNK = 256
LANES = 128
ROWS = 32
CLUSTER = 4
EARLY = 2
LOG2E = 1.4426950408889634
norm_eps = 1e-05

F32 = jnp.float32
BF16 = jnp.bfloat16
VMEM = pl.BlockSpec(memory_space=pltpu.VMEM)
ANY = pl.BlockSpec(memory_space=pl.ANY)
HBM = pl.BlockSpec(memory_space=pltpu.HBM)


def params(mib=24):
    return pltpu.CompilerParams(vmem_limit_bytes=mib << 20)


def cost(flops, moved, transcendentals=0):
    return pl.CostEstimate(flops=flops, bytes_accessed=moved, transcendentals=transcendentals)


def doc_edges(dl_ref):
    edges = [0]
    for i in range(dl_ref.shape[0] - 1):
        edges.append(edges[-1] + dl_ref[i])
    return edges


def doc_start(token, edges):
    start = jnp.zeros_like(token)
    for edge in edges[1:]:
        start = jnp.where(token >= edge, jnp.maximum(start, edge), start)
    return start


def split2(value):
    high = value.astype(BF16)
    return high, (value - high.astype(F32)).astype(BF16)


def split3(value):
    high = value.astype(BF16)
    rest = value - high.astype(F32)
    mid = rest.astype(BF16)
    return high, mid, (rest - mid.astype(F32)).astype(BF16)


def mm(a, b):
    return jnp.dot(a, b, preferred_element_type=F32)


def silu(value):
    half = 0.5 * value
    return half + half * jnp.tanh(half)


def spread(base, rows, first_head, heads, width, head_dim):
    row = lax.broadcasted_iota(jnp.int32, (rows, width), 0) - (base + first_head)
    head = lax.broadcasted_iota(jnp.int32, (rows, width), 1) // head_dim
    return jnp.where((row == head) | (row == head + heads), 1.0, 0.0).astype(BF16)


def start_all(copies):
    for copy in copies:
        copy.start()


def wait_all(copies):
    for copy in copies:
        copy.wait()


def tables(row0, edges, dt_ref, rate_ref, tab_ref, tab0_ref, col_ref, row_ref, d_ref):
    heads, tok = dt_ref.shape
    upto = jnp.where(
        lax.broadcasted_iota(jnp.int32, (SUB, SUB), 0) <= lax.broadcasted_iota(jnp.int32, (SUB, SUB), 1), 1.0, 0.0
    ).astype(BF16)
    rate = jnp.concatenate([rate_ref[...], jnp.zeros((1, LANES - heads), F32)], 1)
    rate = jnp.broadcast_to(rate, (LANES, LANES)).T[:heads]
    total = jnp.zeros((heads, 1), F32)
    decays = []
    for c in range(tok // SUB):
        span = slice(c * SUB, (c + 1) * SUB)
        first = row0 + c * SUB
        dt = dt_ref[:, span]
        step = jnp.maximum(dt, 0.0) + jnp.log1p(jnp.exp(-jnp.abs(dt)))
        parts = split3(-(step * rate))
        cum = mm(parts[0], upto) + (mm(parts[1], upto) + mm(parts[2], upto))
        last = cum[:, SUB - 1 :]
        token = first + lax.broadcasted_iota(jnp.int32, (heads, SUB), 1)
        start = doc_start(token, edges)
        last_start = doc_start(jnp.int32(first + SUB - 1), edges)
        to_end = jnp.exp(last - cum) * step * jnp.where(token >= last_start, 1.0, 0.0)
        since_sub = jnp.exp(cum) * jnp.where((start < first) & (c > 0), 1.0, 0.0)
        since_block = jnp.exp(cum + total) * jnp.where(start < row0, 1.0, 0.0)
        first_pair = [part.astype(F32) for part in (*split2(to_end), *split2(since_sub))]
        second_pair = [part.astype(F32) for part in split2(since_block)] + [cum * LOG2E, jnp.zeros_like(cum)]
        tab_ref[span, :] = jnp.concatenate(first_pair, 0).T.astype(BF16)
        second = jnp.concatenate(second_pair, 0).T
        tab0_ref[span, :] = second[:, : 2 * heads].astype(BF16)
        col_ref[span, :] = second
        row_ref[:, span] = (jnp.log(step) - cum) * LOG2E
        decays.append(jnp.exp(last) * jnp.where(last_start < first, 1.0, 0.0))
        total = total + last
    end_start = doc_start(jnp.int32(row0 + tok - 1), edges)
    whole = jnp.exp(total) * jnp.where(end_start < row0, 1.0, 0.0)
    columns = [part.astype(F32) for part in split3(whole)] + decays[1:]
    columns.append(jnp.zeros((heads, LANES - len(columns)), F32))
    columns = jnp.concatenate([jnp.concatenate(columns, 1), jnp.zeros((LANES - heads, LANES), F32)], 0)
    halves = [part.astype(F32)[:, :heads] for part in split2(columns.T[:8])]
    d_ref[...] = jnp.concatenate(halves, 1).astype(BF16)


def pack_kernel(x_ref, b_ref, c_ref, out_ref):
    out_ref[...] = jnp.concatenate([x_ref[...], b_ref[...], c_ref[...]], 1)


def pack(x, b, c):
    tiles = x.shape[0] // 8
    widths = [value.shape[1] for value in (x, b, c)]
    return pl.pallas_call(
        pack_kernel,
        out_shape=jax.ShapeDtypeStruct((8, sum(widths)), BF16),
        grid=(1,),
        in_specs=[pl.BlockSpec((8, width), lambda i: (tiles - 1, 0)) for width in widths],
        out_specs=pl.BlockSpec((8, sum(widths)), lambda i: (0, 0)),
        compiler_params=params(16),
        name="pack",
    )(x, b, c)


def place_of(k, owned):
    return pl.multiple_of((lax.axis_index("seq") % CLUSTER ^ k) * owned, owned)


def fill_masks(age_ref, mask_ref):
    for back in range(1, mask_ref.shape[0] + 1):
        mask_ref[back - 1] = jnp.where(age_ref[...] >= back, 1.0, 0.0)


def convolve(ext_ref, mask_ref, taps, emit):
    tok = ext_ref.shape[0] - 8
    repeats = ext_ref.shape[1] // LANES
    for low in range(0, tok, ROWS):
        total = ext_ref[8 + low : 8 + low + ROWS, :] * taps[-1]
        for back in range(1, len(taps)):
            mask = jnp.concatenate([mask_ref[back - 1, low : low + ROWS, :]] * repeats, 1)
            window = ext_ref[8 + low - back : 8 + low - back + ROWS, :]
            total = total + (window * taps[-1 - back]) * mask
        emit(low, total)


def state_of(at, heads, head_dim, bt_ref, tab_ref, d_ref, x_rows, h_put):
    one_hot = spread(0, 2 * heads, at // head_dim, heads, CHUNK, head_dim)
    decay = mm(d_ref[...], one_hot)
    tok = tab_ref.shape[0]
    state = None
    for c in range(tok // SUB):
        rows = slice(c * SUB, (c + 1) * SUB)
        weight = mm(tab_ref[rows, : 2 * heads], one_hot)
        if c == 0:
            head_weight = weight[:8]
        local = mm(bt_ref[:, rows], (x_rows(c) * weight).astype(BF16))
        if state is None:
            state = local
        else:
            h_put(c - 1, state)
            state = local + decay[2 + c : 3 + c, :] * state
    return state, decay, head_weight


def conv_kernel(
    dl_hbm,
    dt_hbm,
    rate_hbm,
    x_hbm,
    b_hbm,
    taps_x_hbm,
    taps_b_hbm,
    tab_ref,
    tab0_ref,
    col_ref,
    row_ref,
    d_ref,
    age_ref,
    taps_x_ref,
    taps_b_ref,
    part_x_ref,
    part_b_ref,
    xc_ref,
    bc_ref,
    dl_ref,
    dt_ref,
    rate_ref,
    in_ref,
    ext_ref,
    mask_ref,
    sem,
    in_sem,
):
    tok, channels = x_hbm.shape
    owned = channels // CLUSTER
    per = owned // CHUNK
    chunks = EARLY * per
    small = [
        pltpu.make_async_copy(dl_hbm, dl_ref, sem.at[0]),
        pltpu.make_async_copy(dt_hbm, dt_ref, sem.at[1]),
        pltpu.make_async_copy(rate_hbm, rate_ref, sem.at[2]),
        pltpu.make_async_copy(taps_x_hbm, taps_x_ref, sem.at[3]),
        pltpu.make_async_copy(taps_b_hbm, taps_b_ref, sem.at[4]),
    ]
    start_all(small)

    def place(i):
        return pl.multiple_of(place_of(i // per + 1, owned) + (i % per) * CHUNK, CHUNK)

    def fetch(i):
        return pltpu.make_async_copy(x_hbm.at[:, pl.ds(place(i), CHUNK)], in_ref.at[i], in_sem.at[i])

    for i in range(chunks):
        fetch(i).start()
    fetch_b = pltpu.make_async_copy(b_hbm, in_ref.at[chunks], in_sem.at[chunks])
    fetch_b.start()
    ext_ref[:8, :] = jnp.zeros((8, CHUNK), F32)
    wait_all(small)
    row0 = lax.axis_index("seq") * tok
    edges = doc_edges(dl_ref)
    tables(row0, edges, dt_ref, rate_ref, tab_ref, tab0_ref, col_ref, row_ref, d_ref)
    token = row0 + lax.broadcasted_iota(jnp.int32, (tok, LANES), 0)
    age_ref[...] = token - doc_start(token, edges)
    fill_masks(age_ref, mask_ref)
    taps_len = taps_x_ref.shape[0]

    def body(i, carry):
        fetch(i).wait()
        k = i // per
        inner = pl.ds(pl.multiple_of((i % per) * CHUNK, CHUNK), CHUNK)
        ext_ref[8:, :] = in_ref[i].astype(F32)

        def emit(low, total):
            if low == 0:
                part_x_ref[k, :, inner] = total[:8]
            xc_ref[k, low : low + ROWS, inner] = silu(total).astype(BF16)

        convolve(ext_ref, mask_ref, [taps_x_ref[j : j + 1, pl.ds(place(i), CHUNK)] for j in range(taps_len)], emit)
        return carry

    lax.fori_loop(0, chunks, body, 0)
    fetch_b.wait()
    ext_ref[8:, :] = in_ref[chunks].astype(F32)

    def emit_b(low, total):
        if low == 0:
            part_b_ref[...] = total[:8]
        bc_ref[low : low + ROWS, :] = silu(total).astype(BF16)

    convolve(ext_ref, mask_ref, [taps_b_ref[j : j + 1, :] for j in range(taps_len)], emit_b)


def conv(doc_lengths, dt_t, rate, x, b, taps_x, taps_b):
    heads = dt_t.shape[0]
    tok, channels = x.shape
    gn = b.shape[1]
    owned = channels // CLUSTER
    places = EARLY * (owned // CHUNK) + 1
    shape = jax.ShapeDtypeStruct
    return pl.pallas_call(
        conv_kernel,
        out_shape=(
            shape((tok, LANES), BF16),
            shape((tok, 2 * heads), BF16),
            shape((tok, LANES), F32),
            shape((heads, tok), F32),
            shape((8, 2 * heads), BF16),
            shape((tok, LANES), jnp.int32),
            shape(taps_x.shape, F32),
            shape(taps_b.shape, F32),
            shape((EARLY, 8, owned), F32),
            shape((8, gn), F32),
            shape((EARLY, tok, owned), BF16),
            shape((tok, gn), BF16),
        ),
        in_specs=[HBM] * 7,
        out_specs=(VMEM,) * 12,
        scratch_shapes=[
            pltpu.SMEM(doc_lengths.shape, jnp.int32),
            pltpu.VMEM((heads, tok), F32),
            pltpu.VMEM((1, heads), F32),
            pltpu.VMEM((places, tok, CHUNK), BF16),
            pltpu.VMEM((tok + 8, CHUNK), F32),
            pltpu.VMEM((taps_x.shape[0] - 1, tok, LANES), F32),
            pltpu.SemaphoreType.DMA((5,)),
            pltpu.SemaphoreType.DMA((places,)),
        ],
        compiler_params=params(16),
        cost_estimate=cost(tok * channels * 16, tok * channels * 4, tok * channels),
        name="conv",
    )(doc_lengths, dt_t, rate, x, b, taps_x, taps_b)


def state_kernel(tab_ref, d_ref, xc_ref, bc_ref, s_ref, h_ref, decay_ref, weight_ref, bt_ref):
    pieces, tok, owned = xc_ref.shape
    gn = bc_ref.shape[1]
    channels = owned * CLUSTER
    heads = d_ref.shape[1] // 2
    for group in range(gn // STATE):
        b_blk = bc_ref[:, group * STATE : (group + 1) * STATE].astype(F32)[8:]
        bt_ref[group] = jnp.concatenate([jnp.zeros((8, STATE), F32), b_blk], 0).T.astype(BF16)
    for k in range(pieces):
        at = place_of(k + 1, owned)
        group = at // (channels // (gn // STATE))
        for part in range(owned // CHUNK):
            here = slice(part * CHUNK, (part + 1) * CHUNK)

            def h_put(c, value):
                h_ref[k, c, :, here] = value

            state, decay, weight = state_of(
                at + part * CHUNK,
                heads,
                channels // heads,
                bt_ref.at[group],
                tab_ref,
                d_ref,
                lambda c: xc_ref[k, c * SUB : (c + 1) * SUB, here].astype(F32),
                h_put,
            )
            s_ref[k, :, here] = state
            decay_ref[k, :, here] = decay
            weight_ref[k, :, here] = weight


def states(tab, d, xc, bc):
    pieces, tok, owned = xc.shape
    gn = bc.shape[1]
    row = jax.ShapeDtypeStruct((pieces, 8, owned), F32)
    return pl.pallas_call(
        state_kernel,
        out_shape=(
            jax.ShapeDtypeStruct((pieces, STATE, owned), F32),
            jax.ShapeDtypeStruct((pieces, tok // SUB - 1, STATE, owned), F32),
            row,
            row,
        ),
        in_specs=[VMEM] * 4,
        out_specs=(VMEM,) * 4,
        scratch_shapes=[pltpu.VMEM((gn // STATE, STATE, tok), BF16)],
        compiler_params=params(16),
        cost_estimate=cost(tok * STATE * owned * pieces * 4, tok * owned * pieces * 4),
        name="state",
    )(tab, d, xc, bc)


def head_kernel(
    tail_ref,
    part_x_ref,
    part_b_ref,
    taps_x_ref,
    taps_b_ref,
    age_ref,
    s_ref,
    decay_ref,
    weight_ref,
    xc_in,
    bc_in,
    xc_ref,
    bc_ref,
    extra_ref,
    *rest,
):
    pieces, _, owned = s_ref.shape
    sends = rest[:pieces]
    ext_ref, bt_ref, xw_ref = rest[pieces:]
    gn = bc_in.shape[1]
    channels = owned * CLUSTER
    taps_len = taps_x_ref.shape[0]
    ext_ref[:8, :] = tail_ref[...].astype(F32)
    ext_ref[8:, :] = jnp.zeros_like(ext_ref[8:, :])

    def head_of(part, lanes, taps, width):
        total = part
        age = jnp.concatenate([age_ref[:8, :]] * (width // LANES), 1)
        for back in range(1, taps_len):
            total = total + jnp.where(age >= back, ext_ref[8 - back : 16 - back, lanes] * taps[-1 - back], 0.0)
        return silu(total).astype(BF16)

    head = head_of(
        part_b_ref[...], slice(channels, channels + gn), [taps_b_ref[j : j + 1, :] for j in range(taps_len)], gn
    )
    bc_ref[:8, :] = head
    for group in range(gn // STATE):
        rows = head[:, group * STATE : (group + 1) * STATE].astype(F32)
        bt_ref[group] = jnp.concatenate([rows, jnp.zeros((LANES - 8, STATE), F32)], 0).T.astype(BF16)
    xw_ref[...] = jnp.zeros_like(xw_ref)
    for k in range(pieces):
        at = place_of(k + 1, owned)
        lanes = pl.ds(at, owned)
        head = head_of(part_x_ref[k], lanes, [taps_x_ref[j : j + 1, lanes] for j in range(taps_len)], owned)
        xc_ref[k, :8, :] = head
        xw_ref[:8, :] = head.astype(F32) * weight_ref[k]
        extra = mm(bt_ref[at // (channels // (gn // STATE))], xw_ref[...].astype(BF16))
        extra_ref[k] = extra
        decay = decay_ref[k]
        rest_of_block = decay[3:4, :]
        for c in range(4, 3 + xc_in.shape[1] // SUB - 1):
            rest_of_block = rest_of_block * decay[c : c + 1, :]
        sends[k][:STATE, :] = (s_ref[k] + rest_of_block * extra).astype(BF16)
        sends[k][STATE:, :] = decay.astype(BF16)


def with_head(tail, part_x, part_b, taps_x, taps_b, age, state, decay, weight, xc, bc):
    pieces, _, owned = xc.shape
    gn = bc.shape[1]
    shape = jax.ShapeDtypeStruct
    return pl.pallas_call(
        head_kernel,
        out_shape=(shape(xc.shape, BF16), shape(bc.shape, BF16), shape(state.shape, F32))
        + (shape((STATE + 8, owned), BF16),) * pieces,
        in_specs=[VMEM] * 11,
        out_specs=(VMEM,) * (3 + pieces),
        scratch_shapes=[
            pltpu.VMEM((16, tail.shape[1]), F32),
            pltpu.VMEM((gn // STATE, STATE, LANES), BF16),
            pltpu.VMEM((LANES, owned), F32),
        ],
        input_output_aliases={9: 0, 10: 1},
        compiler_params=params(16),
        cost_estimate=cost(STATE * LANES * owned * pieces * 2, STATE * owned * pieces * 10),
        name="head",
    )(tail, part_x, part_b, taps_x, taps_b, age, state, decay, weight, xc, bc)


def late_kernel(k, with_c, *refs):
    tail_ref, age_ref, tab_ref, d_ref, bc_ref, taps_x_ref, x_ref = refs[:7]
    refs = refs[7:]
    if with_c:
        c_ref, taps_c_ref, others_ref, extra_ref, decay_ref, cc_ref, early_ref = refs[:7]
        refs = refs[7:]
    xc_ref, h_ref, send_ref, bt_ref, ext_ref, mask_ref = refs
    tok, channels = x_ref.shape
    owned = channels // CLUSTER
    gn = bc_ref.shape[1]
    per = owned // CHUNK
    heads = d_ref.shape[1] // 2
    head_dim = channels // heads
    taps_len = taps_x_ref.shape[0]
    at = place_of(k, owned)
    fill_masks(age_ref, mask_ref)
    group = at // (channels // (gn // STATE))
    b_blk = bc_ref[:, pl.ds(pl.multiple_of(group * STATE, STATE), STATE)]
    bt_ref[...] = b_blk.astype(F32).T.astype(BF16)
    if with_c:
        for i in range(EARLY):
            extra = extra_ref[i]
            for c in range(tok // SUB - 1):
                if c > 0:
                    extra = extra * decay_ref[i, 2 + c : 3 + c, :]
                early_ref[i, c] = (others_ref[i, c] + extra).astype(BF16)
    for part in range(per + with_c):
        here = slice(part * CHUNK, (part + 1) * CHUNK)
        if part < per:
            lanes = pl.ds(pl.multiple_of(at + part * CHUNK, CHUNK), CHUNK)
            taps = [taps_x_ref[j : j + 1, lanes] for j in range(taps_len)]
        else:
            lanes = slice(channels + gn, channels + 2 * gn)
            taps = [taps_c_ref[j : j + 1, :] for j in range(taps_len)]
        ext_ref[:8, :] = tail_ref[:, lanes].astype(F32)
        ext_ref[8:, :] = (x_ref[:, lanes] if part < per else c_ref[...]).astype(F32)

        def emit(low, total):
            value = silu(total).astype(BF16)
            if part < per:
                xc_ref[0, low : low + ROWS, here] = value
            else:
                cc_ref[low : low + ROWS, :] = value

        convolve(ext_ref, mask_ref, taps, emit)
        if part < per:

            def h_put(c, value):
                h_ref[0, c, :, here] = value.astype(BF16)

            state, decay, _ = state_of(
                at + part * CHUNK,
                heads,
                head_dim,
                bt_ref,
                tab_ref,
                d_ref,
                lambda c: xc_ref[0, c * SUB : (c + 1) * SUB, here].astype(F32),
                h_put,
            )
            send_ref[:STATE, here] = state.astype(BF16)
            send_ref[STATE:, here] = decay.astype(BF16)


def late(k, tail, age, tab, d, bc, taps_x, x, with_c=()):
    tok, channels = x.shape
    owned = channels // CLUSTER
    gn = bc.shape[1]
    subs = tok // SUB - 1
    shape = jax.ShapeDtypeStruct
    extra_out = (shape((tok, gn), BF16), shape((EARLY, subs, STATE, owned), BF16)) if with_c else ()
    return pl.pallas_call(
        functools.partial(late_kernel, k, bool(with_c)),
        out_shape=(
            *extra_out,
            shape((1, tok, owned), BF16),
            shape((1, subs, STATE, owned), BF16),
            shape((STATE + 8, owned), BF16),
        ),
        in_specs=[VMEM] * (7 + len(with_c)),
        out_specs=(VMEM,) * (3 + len(extra_out)),
        scratch_shapes=[
            pltpu.VMEM((STATE, tok), BF16),
            pltpu.VMEM((tok + 8, CHUNK), F32),
            pltpu.VMEM((taps_x.shape[0] - 1, tok, LANES), F32),
        ],
        compiler_params=params(16),
        cost_estimate=cost(tok * owned * 16 + tok * STATE * owned * 4, tok * owned * 8, tok * owned),
        name="own" if with_c else "late",
    )(tail, age, tab, d, bc, taps_x, x, *with_c)


def collect_kernel(*refs):
    *pieces, out_ref = refs
    for k, ref in enumerate(pieces):
        out_ref[k] = ref[...]


def collect(pieces):
    return pl.pallas_call(
        collect_kernel,
        out_shape=jax.ShapeDtypeStruct((len(pieces), *pieces[0].shape), BF16),
        in_specs=[VMEM] * len(pieces),
        out_specs=VMEM,
        compiler_params=params(16),
        cost_estimate=cost(0, 4 * len(pieces) * pieces[0].size),
        name="collect",
    )(*pieces)


def scan_kernel(*refs):
    first_ref, *last, local_ref, pre_ref, total_ref = refs
    pieces = [first_ref.at[k] for k in range(first_ref.shape[0])] + last
    mine = lax.axis_index("seq") % CLUSTER

    def in_order(values):
        bit = 1
        while bit < CLUSTER:
            odd = (mine & bit) != 0
            values = [jnp.where(odd, values[i ^ bit], values[i]) for i in range(CLUSTER)]
            bit *= 2
        return values

    owned = total_ref.shape[1]
    tables = [ref[STATE:, :].astype(F32) for ref in pieces]
    decays = in_order([row[0:1] + (row[1:2] + row[2:3]) for row in tables])
    pre = jnp.ones((1, owned), F32)
    for i in range(CLUSTER):
        pre_ref[i] = jnp.broadcast_to(pre, (8, owned))
        pre = pre * decays[i]
    pre_ref[CLUSTER] = jnp.broadcast_to(pre, (8, owned))
    for at in range(0, owned, LANES):
        lanes = slice(at, at + LANES)
        for low in range(0, STATE, 64):
            rows = slice(low, low + 64)
            values = in_order([ref[rows, lanes].astype(F32) for ref in pieces])
            local_ref[0, rows, lanes] = jnp.zeros((64, LANES), F32)
            state = values[0]
            for i in range(1, CLUSTER):
                local_ref[i, rows, lanes] = state
                state = decays[i][:, lanes] * state + values[i]
            total_ref[rows, lanes] = state.astype(BF16)


def scan_blocks(pieces):
    operands = (collect(pieces[: 1 + EARLY]), *pieces[1 + EARLY :])
    owned = pieces[0].shape[1]
    return pl.pallas_call(
        scan_kernel,
        out_shape=(
            jax.ShapeDtypeStruct((CLUSTER, STATE, owned), F32),
            jax.ShapeDtypeStruct((CLUSTER + 1, 8, owned), F32),
            jax.ShapeDtypeStruct((STATE, owned), BF16),
        ),
        in_specs=[VMEM] * len(operands),
        out_specs=(VMEM,) * 3,
        compiler_params=params(),
        cost_estimate=cost(CLUSTER * STATE * owned * 2, CLUSTER * STATE * owned * 6),
        name="cluster_scan",
    )(*operands)


def join_kernel(before_ref, local_ref, pre_ref, *outs):
    index = lax.axis_index("seq")
    mine = index % CLUSTER
    before = jnp.where(index >= CLUSTER, before_ref[...].astype(F32), 0.0)
    for k in range(CLUSTER):
        block = mine ^ k
        outs[k][...] = (local_ref[block] + pre_ref[block][0:1] * before).astype(BF16)


def join(before, local, pre):
    owned = local.shape[2]
    return pl.pallas_call(
        join_kernel,
        out_shape=(jax.ShapeDtypeStruct((STATE, owned), BF16),) * CLUSTER,
        in_specs=[VMEM] * 3,
        out_specs=(VMEM,) * CLUSTER,
        compiler_params=params(),
        cost_estimate=cost(CLUSTER * STATE * owned * 2, CLUSTER * STATE * owned * 6),
        name="join",
    )(before, local, pre)


def group_at(turn, groups):
    return (lax.axis_index("seq") % CLUSTER) // (CLUSTER // groups) ^ turn


def intra_kernel(pieces, heads, head_dim, *refs):
    bc_ref, cc_ref, tab_ref, tab0_ref, col_ref, row_ref, age_ref = refs[:7]
    count = len(pieces)
    xs, hs, gates = refs[7 : 7 + count], refs[7 + count : 7 + 2 * count], refs[7 + 2 * count : 7 + 3 * count]
    parts, scales = refs[7 + 3 * count : 7 + 4 * count], refs[7 + 4 * count : 7 + 5 * count]
    hot_ref, hot0_ref = refs[7 + 5 * count :]
    owned = parts[0].shape[1]
    per_piece = owned // head_dim
    mine = lax.axis_index("seq") % CLUSTER

    @pl.when(pl.program_id(0) == 0)
    def _():
        for p, k in enumerate(pieces):
            hot_ref[p] = spread(2 * heads, 4 * heads, (mine ^ k) * per_piece, heads, owned, head_dim)
            hot0_ref[p] = spread(0, 2 * heads, (mine ^ k) * per_piece, heads, owned, head_dim)

    back = lax.broadcasted_iota(jnp.int32, (SUB, SUB), 0) - lax.broadcasted_iota(jnp.int32, (SUB, SUB), 1)
    keep = (back >= 0) & (back <= age_ref[...])
    c_blk = cc_ref[...]
    scores = lax.dot_general(c_blk, bc_ref[...], (((1,), (1,)), ((), ())), preferred_element_type=F32)
    scores = jnp.where(keep, scores, 0.0)
    lane = lax.broadcasted_iota(jnp.int32, (SUB, LANES), 1)
    per_tile = LANES // head_dim
    for p, k in enumerate(pieces):
        first = (mine ^ k) * per_piece
        col = pltpu.roll(col_ref[...], LANES - (2 * heads + first), 1)
        row = row_ref[pl.ds(pl.multiple_of(first, per_piece), per_piece), :]
        for tile in range(owned // LANES):
            lanes = slice(tile * LANES, (tile + 1) * LANES)
            x_tile = xs[p][0, :, lanes].astype(F32)
            left, right = [], []
            for i in range(per_tile):
                head = tile * per_tile + i
                gap = col[:, head : head + 1] + row[head : head + 1, :]
                left.append((jnp.exp2(jnp.minimum(gap, 80.0)) * scores).astype(BF16))
                here = (lane >= i * head_dim) & (lane < (i + 1) * head_dim)
                right.append(jnp.where(here, x_tile, 0.0).astype(BF16))
            inner = mm(jnp.concatenate(left, 1), jnp.concatenate(right, 0))
            inner = inner + mm(c_blk, hs[p][0, 0, :, lanes]) * mm(tab_ref[...], hot_ref[p, :, lanes])
            gate = silu(gates[p][:, lanes].astype(F32))
            parts[p][:, lanes] = inner * gate
            scales[p][:, lanes] = mm(tab0_ref[...], hot0_ref[p, :, lanes]) * gate


def early_index(k):
    return k - 1 if 1 <= k <= EARLY else 0


def intra(turn, pieces, bc, cc, tab, tab0, col, row, age, xs, hs, gate):
    tok, gn = bc.shape
    heads = row.shape[0]
    channels = gate.shape[1]
    head_dim = channels // heads
    groups = gn // STATE
    owned = channels // CLUSTER
    count = len(pieces)
    out = jax.ShapeDtypeStruct((tok, owned), F32)

    def piece_spec(block, index):
        return [pl.BlockSpec(block, functools.partial(index, k)) for k in pieces]

    return pl.pallas_call(
        functools.partial(intra_kernel, pieces, heads, head_dim),
        out_shape=(out,) * (2 * count),
        grid=(tok // SUB,),
        in_specs=[
            pl.BlockSpec((SUB, STATE), lambda i: (i, group_at(turn, groups))),
            pl.BlockSpec((SUB, STATE), lambda i: (i, group_at(turn, groups))),
            pl.BlockSpec((SUB, tab.shape[1]), lambda i: (i, 0)),
            pl.BlockSpec((SUB, tab0.shape[1]), lambda i: (i, 0)),
            pl.BlockSpec((SUB, LANES), lambda i: (i, 0)),
            pl.BlockSpec((heads, SUB), lambda i: (0, i)),
            pl.BlockSpec((SUB, LANES), lambda i: (i, 0)),
        ]
        + piece_spec((1, SUB, owned), lambda k, i: (early_index(k), i, 0))
        + piece_spec((1, 1, STATE, owned), lambda k, i: (early_index(k), jnp.maximum(i - 1, 0), 0, 0))
        + piece_spec((SUB, owned), lambda k, i: (i, lax.axis_index("seq") % CLUSTER ^ k)),
        out_specs=(pl.BlockSpec((SUB, owned), lambda i: (i, 0)),) * (2 * count),
        scratch_shapes=[pltpu.VMEM((count, 4 * heads, owned), BF16), pltpu.VMEM((count, 2 * heads, owned), BF16)],
        compiler_params=params(16),
        cost_estimate=cost(tok * SUB * owned * count * 4, tok * owned * count * 12, tok * SUB * owned * count // head_dim),
        name="intra",
    )(bc, cc, tab, tab0, col, row, age, *xs, *hs, *([gate] * count))


def final_kernel(turn, groups, *refs):
    cc_ref, gain_ref = refs[:2]
    share = CLUSTER // groups
    parts, scales, pieces = (refs[2 + i * share : 2 + (i + 1) * share] for i in range(3))
    out_hbm, y_ref, put_ref, sem = refs[-4:]
    tok, owned = parts[0].shape
    rows = y_ref.shape[1]
    copies = []
    c_lanes = pl.ds(pl.multiple_of(group_at(turn, groups) * STATE, STATE), STATE)
    columns = [pl.ds(place_of(turn * share + i, owned), owned) for i in range(share)]
    for low in range(0, tok, rows):
        span = slice(low, low + rows)
        c_blk = cc_ref[span, c_lanes]
        squares = None
        for i in range(share):
            for at in range(0, owned, CHUNK):
                lanes = slice(at, at + CHUNK)
                value = parts[i][span, lanes] + mm(c_blk, pieces[i][:, lanes]) * scales[i][span, lanes]
                y_ref[i, :, lanes] = value
                square = value * value
                for j in range(0, CHUNK, LANES):
                    piece = square[:, j : j + LANES]
                    squares = piece if squares is None else squares + piece
        factor = lax.rsqrt(jnp.sum(squares, axis=1, keepdims=True) * (1.0 / (share * owned)) + norm_eps)
        for i in range(share):
            put_ref[i, span, :] = (y_ref[i] * factor * gain_ref[:, columns[i]]).astype(BF16)
            copies.append(
                pltpu.make_async_copy(put_ref.at[i, span, :], out_hbm.at[span, columns[i]], sem.at[i, low // rows])
            )
            copies[-1].start()
    wait_all(copies)


def final(turn, cc, gain, parts, scales, pieces, so_far):
    tok, owned = parts[0].shape
    groups = cc.shape[1] // STATE
    share = CLUSTER // groups
    rows = 64
    operands = (cc, gain, *parts, *scales, *pieces) + (() if so_far is None else (so_far,))
    return pl.pallas_call(
        functools.partial(final_kernel, turn, groups),
        out_shape=jax.ShapeDtypeStruct((tok, owned * CLUSTER), BF16),
        in_specs=[VMEM] * (2 + 3 * share) + ([] if so_far is None else [ANY]),
        out_specs=ANY,
        scratch_shapes=[
            pltpu.VMEM((share, rows, owned), F32),
            pltpu.VMEM((share, tok, owned), BF16),
            pltpu.SemaphoreType.DMA((share, tok // rows)),
        ],
        input_output_aliases={} if so_far is None else {len(operands) - 1: 0},
        compiler_params=params(16),
        cost_estimate=cost(tok * STATE * owned * share * 2, tok * owned * share * 8),
        name="final",
    )(*operands)


def moved(value, hop):
    count = lax.axis_size("seq")
    return lax.ppermute(value, "seq", [(i, hop(i)) for i in range(count) if 0 <= hop(i) < count])


def exchanged(pieces, order):
    arrived = {0: pieces[0]}
    for k in order:
        arrived[k] = moved(pieces[k], lambda i, k=k: i ^ k)
    return [arrived[k] for k in range(CLUSTER)]


def before_cluster(total, pre):
    clusters = lax.axis_size("seq") // CLUSTER
    if clusters == 1:
        return jnp.zeros_like(total)
    if clusters == 2:
        return moved(total, lambda i: i ^ CLUSTER)
    shift = lambda value, steps: moved(value, lambda i: i + steps * CLUSTER)
    state, decay = shift((total.astype(F32), pre[CLUSTER, 0]), 1)
    step = 1
    while step < clusters - 1:
        earlier, fell = shift((state, decay), step)
        state, decay = state + decay[None, :] * earlier, decay * fell
        step *= 2
    return state


def tied(values, other):
    *values, _ = lax.optimization_barrier((*values, other))
    return values


def on_device(
    x_input,
    b_input,
    c_input,
    dt_input,
    decay_rate,
    gate_input,
    taps_x,
    taps_b,
    taps_c,
    norm_gain,
    doc_lengths,
):
    groups = b_input.shape[1] // STATE
    count = lax.axis_size("seq")
    pin = lambda value: pltpu.with_memory_space_constraint(value, pltpu.HBM)
    raw_x, raw_c, raw_taps_c = x_input, c_input, taps_c
    x_input, b_input, c_input, doc_lengths = pin(x_input), pin(b_input), pin(c_input), pin(doc_lengths)
    taps_x, taps_b = pin(taps_x), pin(taps_b)
    tail = lax.ppermute(pack(x_input, b_input, c_input), "seq", [(i, (i + 1) % count) for i in range(count)])
    tab, tab0, col, row, d, age, taps_x, taps_b, part_x, part_b, xc, bc = conv(
        doc_lengths, pin(dt_input.T), pin(decay_rate[None, :]), x_input, b_input, taps_x, taps_b
    )
    state, others, decay, weight = states(tab, d, xc, bc)
    xc, bc, extra, *sends = with_head(tail, part_x, part_b, taps_x, taps_b, age, state, decay, weight, xc, bc)
    known = (tail, age, tab, d, bc, taps_x, raw_x)
    xs, hs = [None] + [xc] * EARLY, [None] * (1 + EARLY)
    for k in range(1 + EARLY, CLUSTER):
        late_x, late_h, late_send = late(k, *known)
        xs.append(late_x)
        hs.append(late_h)
        sends.append(late_send)
    cc, early_h, xs[0], hs[0], own_send = late(0, *known, (raw_c, raw_taps_c, others, extra, decay))
    hs[1 : 1 + EARLY] = [early_h] * EARLY
    shared = (bc, cc, tab, tab0, col, row)
    share = CLUSTER // groups

    def inner(turn, age):
        pieces = tuple(range(turn * share, (turn + 1) * share))
        return intra(turn, pieces, *shared, age, [xs[k] for k in pieces], [hs[k] for k in pieces], gate_input)

    local, pre, total = scan_blocks(exchanged([own_send, *sends], (1, 2, 3)))
    first = inner(0, *tied([age], total))
    joined = join(*tied([before_cluster(total, pre)], first[0]), local, pre)
    later = [inner(turn, *tied([age], joined[0])) for turn in range(1, groups)]
    entering = exchanged(joined, (1, 2, 3))
    output = None
    for turn, found in enumerate((first, *later)):
        mine = entering[turn * share : (turn + 1) * share]
        output = final(turn, cc, norm_gain[None, :], found[:share], found[share:], mine, output)
    return output


def solution(mesh):
    rows = P(("groups", "seq"), "dp")
    placed = (rows, rows, rows, rows, P("dp"), rows, P(None, "dp"), P(None, "dp"), P(None, "dp"), P("dp"), P("groups"))
    return jax.shard_map(on_device, mesh=mesh, in_specs=placed, out_specs=rows, check_vma=False)
```

```python
import functools

import jax
import jax.numpy as jnp
from jax import lax
from jax.experimental import pallas as pl
from jax.experimental.pallas import tpu as pltpu
from jax.sharding import PartitionSpec as P

STATE = 128
SUB = 128
CHUNK = 256
LANES = 128
ROWS = 32
CLUSTER = 4
EARLY = 2
LOG2E = 1.4426950408889634
norm_eps = 1e-05

F32 = jnp.float32
BF16 = jnp.bfloat16
VMEM = pl.BlockSpec(memory_space=pltpu.VMEM)
ANY = pl.BlockSpec(memory_space=pl.ANY)
HBM = pl.BlockSpec(memory_space=pltpu.HBM)


def params(mib=24):
    return pltpu.CompilerParams(vmem_limit_bytes=mib << 20)


def cost(flops, moved, transcendentals=0):
    return pl.CostEstimate(flops=flops, bytes_accessed=moved, transcendentals=transcendentals)


def doc_edges(dl_ref):
    edges = [0]
    for i in range(dl_ref.shape[0] - 1):
        edges.append(edges[-1] + dl_ref[i])
    return edges


def doc_start(token, edges):
    start = jnp.zeros_like(token)
    for edge in edges[1:]:
        start = jnp.where(token >= edge, jnp.maximum(start, edge), start)
    return start


def split2(value):
    high = value.astype(BF16)
    return high, (value - high.astype(F32)).astype(BF16)


def split3(value):
    high = value.astype(BF16)
    rest = value - high.astype(F32)
    mid = rest.astype(BF16)
    return high, mid, (rest - mid.astype(F32)).astype(BF16)


def mm(a, b):
    return jnp.dot(a, b, preferred_element_type=F32)


def silu(value):
    half = 0.5 * value
    return half + half * jnp.tanh(half)


def spread(base, rows, first_head, heads, width, head_dim):
    row = lax.broadcasted_iota(jnp.int32, (rows, width), 0) - (base + first_head)
    head = lax.broadcasted_iota(jnp.int32, (rows, width), 1) // head_dim
    return jnp.where((row == head) | (row == head + heads), 1.0, 0.0).astype(BF16)


def start_all(copies):
    for copy in copies:
        copy.start()


def wait_all(copies):
    for copy in copies:
        copy.wait()


def tables(row0, edges, dt_ref, rate_ref, tab_ref, tab0_ref, col_ref, row_ref, d_ref):
    heads, tok = dt_ref.shape
    upto = jnp.where(
        lax.broadcasted_iota(jnp.int32, (SUB, SUB), 0) <= lax.broadcasted_iota(jnp.int32, (SUB, SUB), 1), 1.0, 0.0
    ).astype(BF16)
    rate = jnp.concatenate([rate_ref[...], jnp.zeros((1, LANES - heads), F32)], 1)
    rate = jnp.broadcast_to(rate, (LANES, LANES)).T[:heads]
    total = jnp.zeros((heads, 1), F32)
    decays = []
    for c in range(tok // SUB):
        span = slice(c * SUB, (c + 1) * SUB)
        first = row0 + c * SUB
        dt = dt_ref[:, span]
        step = jnp.maximum(dt, 0.0) + jnp.log1p(jnp.exp(-jnp.abs(dt)))
        parts = split3(-(step * rate))
        cum = mm(parts[0], upto) + (mm(parts[1], upto) + mm(parts[2], upto))
        last = cum[:, SUB - 1 :]
        token = first + lax.broadcasted_iota(jnp.int32, (heads, SUB), 1)
        start = doc_start(token, edges)
        last_start = doc_start(jnp.int32(first + SUB - 1), edges)
        to_end = jnp.exp(last - cum) * step * jnp.where(token >= last_start, 1.0, 0.0)
        since_sub = jnp.exp(cum) * jnp.where((start < first) & (c > 0), 1.0, 0.0)
        since_block = jnp.exp(cum + total) * jnp.where(start < row0, 1.0, 0.0)
        first_pair = [part.astype(F32) for part in (*split2(to_end), *split2(since_sub))]
        second_pair = [part.astype(F32) for part in split2(since_block)] + [cum * LOG2E, jnp.zeros_like(cum)]
        tab_ref[span, :] = jnp.concatenate(first_pair, 0).T.astype(BF16)
        second = jnp.concatenate(second_pair, 0).T
        tab0_ref[span, :] = second[:, : 2 * heads].astype(BF16)
        col_ref[span, :] = second
        row_ref[:, span] = (jnp.log(step) - cum) * LOG2E
        decays.append(jnp.exp(last) * jnp.where(last_start < first, 1.0, 0.0))
        total = total + last
    end_start = doc_start(jnp.int32(row0 + tok - 1), edges)
    whole = jnp.exp(total) * jnp.where(end_start < row0, 1.0, 0.0)
    columns = [part.astype(F32) for part in split3(whole)] + decays[1:]
    columns.append(jnp.zeros((heads, LANES - len(columns)), F32))
    columns = jnp.concatenate([jnp.concatenate(columns, 1), jnp.zeros((LANES - heads, LANES), F32)], 0)
    halves = [part.astype(F32)[:, :heads] for part in split2(columns.T[:8])]
    d_ref[...] = jnp.concatenate(halves, 1).astype(BF16)


def pack_kernel(x_ref, b_ref, c_ref, out_ref):
    rows = [ref[...].astype(F32)[4:] for ref in (x_ref, b_ref, c_ref)]
    out_ref[...] = jnp.concatenate(rows, 1).astype(BF16)


def pack(x, b, c):
    tiles = x.shape[0] // 8
    widths = [value.shape[1] for value in (x, b, c)]
    return pl.pallas_call(
        pack_kernel,
        out_shape=jax.ShapeDtypeStruct((4, sum(widths)), BF16),
        grid=(1,),
        in_specs=[pl.BlockSpec((8, width), lambda i: (tiles - 1, 0)) for width in widths],
        out_specs=pl.BlockSpec((4, sum(widths)), lambda i: (0, 0)),
        compiler_params=params(16),
        name="pack",
    )(x, b, c)


def place_of(k, owned):
    return pl.multiple_of((lax.axis_index("seq") % CLUSTER ^ k) * owned, owned)


def fill_masks(age_ref, mask_ref):
    for back in range(1, mask_ref.shape[0] + 1):
        mask_ref[back - 1] = jnp.where(age_ref[...] >= back, 1.0, 0.0)


def convolve(ext_ref, mask_ref, taps, emit):
    tok = ext_ref.shape[0] - 8
    repeats = ext_ref.shape[1] // LANES
    for low in range(0, tok, ROWS):
        total = ext_ref[8 + low : 8 + low + ROWS, :] * taps[-1]
        for back in range(1, len(taps)):
            mask = jnp.concatenate([mask_ref[back - 1, low : low + ROWS, :]] * repeats, 1)
            window = ext_ref[8 + low - back : 8 + low - back + ROWS, :]
            total = total + (window * taps[-1 - back]) * mask
        emit(low, total)


def state_of(at, heads, head_dim, bt_ref, tab_ref, d_ref, x_rows, h_put):
    one_hot = spread(0, 2 * heads, at // head_dim, heads, CHUNK, head_dim)
    decay = mm(d_ref[...], one_hot)
    tok = tab_ref.shape[0]
    state = None
    for c in range(tok // SUB):
        rows = slice(c * SUB, (c + 1) * SUB)
        weight = mm(tab_ref[rows, : 2 * heads], one_hot)
        if c == 0:
            head_weight = weight[:8]
        local = mm(bt_ref[:, rows], (x_rows(c) * weight).astype(BF16))
        if state is None:
            state = local
        else:
            h_put(c - 1, state)
            state = local + decay[2 + c : 3 + c, :] * state
    return state, decay, head_weight


def put_piece(send_ref, low, state):
    for tile in range(state.shape[1] // LANES):
        at = low * STATE + tile * STATE
        send_ref[at : at + STATE, :] = state[:, tile * LANES : (tile + 1) * LANES].astype(BF16)


def put_decay(send_ref, decay):
    tiles = decay.shape[1] // LANES
    rows = [decay[:2, tile * LANES : (tile + 1) * LANES] for tile in range(tiles)]
    send_ref[tiles * STATE :, :] = jnp.concatenate(rows, 0).astype(BF16)


def piece_shape(owned):
    return jax.ShapeDtypeStruct((owned // LANES * (STATE + 2), LANES), BF16)


def conv_kernel(
    dl_ref,
    dt_ref,
    rate_ref,
    x_ref,
    b_ref,
    taps_x_ref,
    taps_b_ref,
    tab_ref,
    tab0_ref,
    col_ref,
    row_ref,
    d_ref,
    age_ref,
    part_x_ref,
    part_b_ref,
    xc_ref,
    bc_ref,
    ext_ref,
    mask_ref,
):
    tok, channels = x_ref.shape
    owned = channels // CLUSTER
    per = owned // CHUNK
    row0 = lax.axis_index("seq") * tok
    edges = doc_edges(dl_ref)
    tables(row0, edges, dt_ref, rate_ref, tab_ref, tab0_ref, col_ref, row_ref, d_ref)
    token = row0 + lax.broadcasted_iota(jnp.int32, (tok, LANES), 0)
    age_ref[...] = token - doc_start(token, edges)
    fill_masks(age_ref, mask_ref)
    ext_ref[:8, :] = jnp.zeros((8, CHUNK), F32)
    taps_len = taps_x_ref.shape[0]

    def body(i, carry):
        k = i // per
        lanes = pl.ds(pl.multiple_of(place_of(k + 1, owned) + (i % per) * CHUNK, CHUNK), CHUNK)
        inner = pl.ds(pl.multiple_of((i % per) * CHUNK, CHUNK), CHUNK)
        ext_ref[8:, :] = x_ref[:, lanes].astype(F32)

        def emit(low, total):
            if low == 0:
                part_x_ref[k, :, inner] = total[:8]
            xc_ref[k, low : low + ROWS, inner] = silu(total).astype(BF16)

        convolve(ext_ref, mask_ref, [taps_x_ref[j : j + 1, lanes] for j in range(taps_len)], emit)
        return carry

    lax.fori_loop(0, EARLY * per, body, 0)
    ext_ref[8:, :] = b_ref[...].astype(F32)

    def emit_b(low, total):
        if low == 0:
            part_b_ref[...] = total[:8]
        bc_ref[low : low + ROWS, :] = silu(total).astype(BF16)

    convolve(ext_ref, mask_ref, [taps_b_ref[j : j + 1, :] for j in range(taps_len)], emit_b)


def conv(doc_lengths, dt_t, rate, x, b, taps_x, taps_b):
    heads = dt_t.shape[0]
    tok, channels = x.shape
    gn = b.shape[1]
    owned = channels // CLUSTER
    shape = jax.ShapeDtypeStruct
    return pl.pallas_call(
        conv_kernel,
        out_shape=(
            shape((tok, LANES), BF16),
            shape((tok, 2 * heads), BF16),
            shape((tok, LANES), F32),
            shape((heads, tok), F32),
            shape((8, 2 * heads), BF16),
            shape((tok, LANES), jnp.int32),
            shape((EARLY, 8, owned), F32),
            shape((8, gn), F32),
            shape((EARLY, tok, owned), BF16),
            shape((tok, gn), BF16),
        ),
        in_specs=[pl.BlockSpec(memory_space=pltpu.SMEM)] + [VMEM] * 6,
        out_specs=(VMEM,) * 10,
        scratch_shapes=[
            pltpu.VMEM((tok + 8, CHUNK), F32),
            pltpu.VMEM((taps_x.shape[0] - 1, tok, LANES), F32),
        ],
        compiler_params=params(16),
        cost_estimate=cost(tok * channels * 16, tok * channels * 4, tok * channels),
        name="conv",
    )(doc_lengths, dt_t, rate, x, b, taps_x, taps_b)


def state_kernel(tab_ref, d_ref, xc_ref, bc_ref, s_ref, h_ref, decay_ref, weight_ref, bt_ref):
    pieces, tok, owned = xc_ref.shape
    gn = bc_ref.shape[1]
    channels = owned * CLUSTER
    heads = d_ref.shape[1] // 2
    for group in range(gn // STATE):
        b_blk = bc_ref[:, group * STATE : (group + 1) * STATE].astype(F32)[8:]
        bt_ref[group] = jnp.concatenate([jnp.zeros((8, STATE), F32), b_blk], 0).T.astype(BF16)
    for k in range(pieces):
        at = place_of(k + 1, owned)
        group = at // (channels // (gn // STATE))
        for part in range(owned // CHUNK):
            here = slice(part * CHUNK, (part + 1) * CHUNK)

            def h_put(c, value):
                h_ref[k, c, :, here] = value

            state, decay, weight = state_of(
                at + part * CHUNK,
                heads,
                channels // heads,
                bt_ref.at[group],
                tab_ref,
                d_ref,
                lambda c: xc_ref[k, c * SUB : (c + 1) * SUB, here].astype(F32),
                h_put,
            )
            s_ref[k, :, here] = state
            decay_ref[k, :, here] = decay
            weight_ref[k, :, here] = weight


def states(tab, d, xc, bc):
    pieces, tok, owned = xc.shape
    gn = bc.shape[1]
    row = jax.ShapeDtypeStruct((pieces, 8, owned), F32)
    return pl.pallas_call(
        state_kernel,
        out_shape=(
            jax.ShapeDtypeStruct((pieces, STATE, owned), F32),
            jax.ShapeDtypeStruct((pieces, tok // SUB - 1, STATE, owned), F32),
            row,
            row,
        ),
        in_specs=[VMEM] * 4,
        out_specs=(VMEM,) * 4,
        scratch_shapes=[pltpu.VMEM((gn // STATE, STATE, tok), BF16)],
        compiler_params=params(16),
        cost_estimate=cost(tok * STATE * owned * pieces * 4, tok * owned * pieces * 4),
        name="state",
    )(tab, d, xc, bc)


def head_kernel(
    tail_ref,
    part_x_ref,
    part_b_ref,
    taps_x_ref,
    taps_b_ref,
    age_ref,
    s_ref,
    decay_ref,
    weight_ref,
    xc_in,
    bc_in,
    xc_ref,
    bc_ref,
    extra_ref,
    *rest,
):
    pieces, _, owned = s_ref.shape
    sends = rest[:pieces]
    ext_ref, bt_ref, xw_ref = rest[pieces:]
    gn = bc_in.shape[1]
    channels = owned * CLUSTER
    taps_len = taps_x_ref.shape[0]
    ext_ref[4:8, :] = tail_ref[...].astype(F32)
    ext_ref[8:, :] = jnp.zeros_like(ext_ref[8:, :])

    def head_of(part, lanes, taps, width):
        total = part
        age = jnp.concatenate([age_ref[:8, :]] * (width // LANES), 1)
        for back in range(1, taps_len):
            total = total + jnp.where(age >= back, ext_ref[8 - back : 16 - back, lanes] * taps[-1 - back], 0.0)
        return silu(total).astype(BF16)

    head = head_of(
        part_b_ref[...], slice(channels, channels + gn), [taps_b_ref[j : j + 1, :] for j in range(taps_len)], gn
    )
    bc_ref[:8, :] = head
    for group in range(gn // STATE):
        rows = head[:, group * STATE : (group + 1) * STATE].astype(F32)
        bt_ref[group] = jnp.concatenate([rows, jnp.zeros((LANES - 8, STATE), F32)], 0).T.astype(BF16)
    xw_ref[...] = jnp.zeros_like(xw_ref)
    for k in range(pieces):
        at = place_of(k + 1, owned)
        lanes = pl.ds(at, owned)
        head = head_of(part_x_ref[k], lanes, [taps_x_ref[j : j + 1, lanes] for j in range(taps_len)], owned)
        xc_ref[k, :8, :] = head
        xw_ref[:8, :] = head.astype(F32) * weight_ref[k]
        extra = mm(bt_ref[at // (channels // (gn // STATE))], xw_ref[...].astype(BF16))
        extra_ref[k] = extra
        decay = decay_ref[k]
        rest_of_block = decay[3:4, :]
        for c in range(4, 3 + xc_in.shape[1] // SUB - 1):
            rest_of_block = rest_of_block * decay[c : c + 1, :]
        put_piece(sends[k], 0, s_ref[k] + rest_of_block * extra)
        put_decay(sends[k], decay)


def with_head(tail, part_x, part_b, taps_x, taps_b, age, state, decay, weight, xc, bc):
    pieces, _, owned = xc.shape
    gn = bc.shape[1]
    shape = jax.ShapeDtypeStruct
    return pl.pallas_call(
        head_kernel,
        out_shape=(shape(xc.shape, BF16), shape(bc.shape, BF16), shape(state.shape, F32))
        + (piece_shape(owned),) * pieces,
        in_specs=[VMEM] * 11,
        out_specs=(VMEM,) * (3 + pieces),
        scratch_shapes=[
            pltpu.VMEM((16, tail.shape[1]), F32),
            pltpu.VMEM((gn // STATE, STATE, LANES), BF16),
            pltpu.VMEM((LANES, owned), F32),
        ],
        input_output_aliases={9: 0, 10: 1},
        compiler_params=params(16),
        cost_estimate=cost(STATE * LANES * owned * pieces * 2, STATE * owned * pieces * 10),
        name="head",
    )(tail, part_x, part_b, taps_x, taps_b, age, state, decay, weight, xc, bc)


def late_kernel(k, with_c, *refs):
    tail_ref, age_ref, tab_ref, d_ref, bc_ref, taps_x_ref, x_ref = refs[:7]
    refs = refs[7:]
    if with_c:
        c_ref, taps_c_ref, others_ref, extra_ref, decay_ref, cc_ref, early_ref = refs[:7]
        refs = refs[7:]
    xc_ref, h_ref, send_ref, bt_ref, ext_ref, mask_ref = refs
    tok, channels = x_ref.shape
    owned = channels // CLUSTER
    gn = bc_ref.shape[1]
    per = owned // CHUNK
    heads = d_ref.shape[1] // 2
    head_dim = channels // heads
    taps_len = taps_x_ref.shape[0]
    at = place_of(k, owned)
    fill_masks(age_ref, mask_ref)
    group = at // (channels // (gn // STATE))
    b_blk = bc_ref[:, pl.ds(pl.multiple_of(group * STATE, STATE), STATE)]
    bt_ref[...] = b_blk.astype(F32).T.astype(BF16)
    if with_c:
        for i in range(EARLY):
            extra = extra_ref[i]
            for c in range(tok // SUB - 1):
                if c > 0:
                    extra = extra * decay_ref[i, 2 + c : 3 + c, :]
                early_ref[i, c] = (others_ref[i, c] + extra).astype(BF16)
    decays = []
    for part in range(per + with_c):
        here = slice(part * CHUNK, (part + 1) * CHUNK)
        if part < per:
            lanes = pl.ds(pl.multiple_of(at + part * CHUNK, CHUNK), CHUNK)
            taps = [taps_x_ref[j : j + 1, lanes] for j in range(taps_len)]
        else:
            lanes = slice(channels + gn, channels + 2 * gn)
            taps = [taps_c_ref[j : j + 1, :] for j in range(taps_len)]
        ext_ref[4:8, :] = tail_ref[:, lanes].astype(F32)
        ext_ref[8:, :] = (x_ref[:, lanes] if part < per else c_ref[...]).astype(F32)

        def emit(low, total):
            value = silu(total).astype(BF16)
            if part < per:
                xc_ref[0, low : low + ROWS, here] = value
            else:
                cc_ref[low : low + ROWS, :] = value

        convolve(ext_ref, mask_ref, taps, emit)
        if part < per:

            def h_put(c, value):
                h_ref[0, c, :, here] = value.astype(BF16)

            state, decay, _ = state_of(
                at + part * CHUNK,
                heads,
                head_dim,
                bt_ref,
                tab_ref,
                d_ref,
                lambda c: xc_ref[0, c * SUB : (c + 1) * SUB, here].astype(F32),
                h_put,
            )
            put_piece(send_ref, part * (CHUNK // LANES), state)
            decays.append(decay)
    put_decay(send_ref, jnp.concatenate(decays, 1))


def late(k, tail, age, tab, d, bc, taps_x, x, with_c=()):
    tok, channels = x.shape
    owned = channels // CLUSTER
    gn = bc.shape[1]
    subs = tok // SUB - 1
    shape = jax.ShapeDtypeStruct
    extra_out = (shape((tok, gn), BF16), shape((EARLY, subs, STATE, owned), BF16)) if with_c else ()
    return pl.pallas_call(
        functools.partial(late_kernel, k, bool(with_c)),
        out_shape=(
            *extra_out,
            shape((1, tok, owned), BF16),
            shape((1, subs, STATE, owned), BF16),
            piece_shape(owned),
        ),
        in_specs=[VMEM] * (7 + len(with_c)),
        out_specs=(VMEM,) * (3 + len(extra_out)),
        scratch_shapes=[
            pltpu.VMEM((STATE, tok), BF16),
            pltpu.VMEM((tok + 8, CHUNK), F32),
            pltpu.VMEM((taps_x.shape[0] - 1, tok, LANES), F32),
        ],
        compiler_params=params(16),
        cost_estimate=cost(tok * owned * 16 + tok * STATE * owned * 4, tok * owned * 8, tok * owned),
        name="own" if with_c else "late",
    )(tail, age, tab, d, bc, taps_x, x, *with_c)


def collect_kernel(*refs):
    *pieces, out_ref = refs
    for k, ref in enumerate(pieces):
        out_ref[k] = ref[...]


def collect(pieces):
    return pl.pallas_call(
        collect_kernel,
        out_shape=jax.ShapeDtypeStruct((len(pieces), *pieces[0].shape), BF16),
        in_specs=[VMEM] * len(pieces),
        out_specs=VMEM,
        compiler_params=params(16),
        cost_estimate=cost(0, 4 * len(pieces) * pieces[0].size),
        name="collect",
    )(*pieces)


def scan_kernel(*refs):
    first_ref, *last, local_ref, pre_ref, total_ref = refs
    pieces = [first_ref.at[k] for k in range(first_ref.shape[0])] + last
    mine = lax.axis_index("seq") % CLUSTER

    def in_order(values):
        bit = 1
        while bit < CLUSTER:
            odd = (mine & bit) != 0
            values = [jnp.where(odd, values[i ^ bit], values[i]) for i in range(CLUSTER)]
            bit *= 2
        return values

    owned = total_ref.shape[1]
    tiles = owned // LANES
    rows = [ref[tiles * STATE :, :].astype(F32) for ref in pieces]
    decays = in_order(
        [jnp.concatenate([row[2 * t : 2 * t + 1] + row[2 * t + 1 : 2 * t + 2] for t in range(tiles)], 1) for row in rows]
    )
    pre = jnp.ones((1, owned), F32)
    for i in range(CLUSTER):
        pre_ref[i] = jnp.broadcast_to(pre, (8, owned))
        pre = pre * decays[i]
    pre_ref[CLUSTER] = jnp.broadcast_to(pre, (8, owned))
    for at in range(0, owned, LANES):
        lanes = slice(at, at + LANES)
        for low in range(0, STATE, 64):
            rows = slice(low, low + 64)
            at_rows = slice(at + low, at + low + 64)
            values = in_order([ref[at_rows, :].astype(F32) for ref in pieces])
            local_ref[0, rows, lanes] = jnp.zeros((64, LANES), F32)
            state = values[0]
            for i in range(1, CLUSTER):
                local_ref[i, rows, lanes] = state
                state = decays[i][:, lanes] * state + values[i]
            total_ref[rows, lanes] = state.astype(BF16)


def scan_blocks(pieces):
    operands = (collect(pieces[: 1 + EARLY]), *pieces[1 + EARLY :])
    owned = pieces[0].shape[0] // (STATE + 2) * LANES
    return pl.pallas_call(
        scan_kernel,
        out_shape=(
            jax.ShapeDtypeStruct((CLUSTER, STATE, owned), F32),
            jax.ShapeDtypeStruct((CLUSTER + 1, 8, owned), F32),
            jax.ShapeDtypeStruct((STATE, owned), BF16),
        ),
        in_specs=[VMEM] * len(operands),
        out_specs=(VMEM,) * 3,
        compiler_params=params(),
        cost_estimate=cost(CLUSTER * STATE * owned * 2, CLUSTER * STATE * owned * 6),
        name="cluster_scan",
    )(*operands)


def join_kernel(before_ref, local_ref, pre_ref, *outs):
    index = lax.axis_index("seq")
    mine = index % CLUSTER
    before = jnp.where(index >= CLUSTER, before_ref[...].astype(F32), 0.0)
    for k in range(CLUSTER):
        block = mine ^ k
        outs[k][...] = (local_ref[block] + pre_ref[block][0:1] * before).astype(BF16)


def join(before, local, pre):
    owned = local.shape[2]
    return pl.pallas_call(
        join_kernel,
        out_shape=(jax.ShapeDtypeStruct((STATE, owned), BF16),) * CLUSTER,
        in_specs=[VMEM] * 3,
        out_specs=(VMEM,) * CLUSTER,
        compiler_params=params(),
        cost_estimate=cost(CLUSTER * STATE * owned * 2, CLUSTER * STATE * owned * 6),
        name="join",
    )(before, local, pre)


def group_at(turn, groups):
    return (lax.axis_index("seq") % CLUSTER) // (CLUSTER // groups) ^ turn


def intra_kernel(pieces, heads, head_dim, *refs):
    bc_ref, cc_ref, tab_ref, tab0_ref, col_ref, row_ref, age_ref = refs[:7]
    count = len(pieces)
    xs, hs, gates = refs[7 : 7 + count], refs[7 + count : 7 + 2 * count], refs[7 + 2 * count : 7 + 3 * count]
    parts, scales = refs[7 + 3 * count : 7 + 4 * count], refs[7 + 4 * count : 7 + 5 * count]
    hot_ref, hot0_ref = refs[7 + 5 * count :]
    owned = parts[0].shape[1]
    per_piece = owned // head_dim
    mine = lax.axis_index("seq") % CLUSTER

    @pl.when(pl.program_id(0) == 0)
    def _():
        for p, k in enumerate(pieces):
            hot_ref[p] = spread(2 * heads, 4 * heads, (mine ^ k) * per_piece, heads, owned, head_dim)
            hot0_ref[p] = spread(0, 2 * heads, (mine ^ k) * per_piece, heads, owned, head_dim)

    back = lax.broadcasted_iota(jnp.int32, (SUB, SUB), 0) - lax.broadcasted_iota(jnp.int32, (SUB, SUB), 1)
    keep = (back >= 0) & (back <= age_ref[...])
    c_blk = cc_ref[...]
    scores = lax.dot_general(c_blk, bc_ref[...], (((1,), (1,)), ((), ())), preferred_element_type=F32)
    scores = jnp.where(keep, scores, 0.0)
    lane = lax.broadcasted_iota(jnp.int32, (SUB, LANES), 1)
    per_tile = LANES // head_dim
    for p, k in enumerate(pieces):
        first = (mine ^ k) * per_piece
        col = pltpu.roll(col_ref[...], LANES - (2 * heads + first), 1)
        row = row_ref[pl.ds(pl.multiple_of(first, per_piece), per_piece), :]
        for tile in range(owned // LANES):
            lanes = slice(tile * LANES, (tile + 1) * LANES)
            x_tile = xs[p][0, :, lanes].astype(F32)
            left, right = [], []
            for i in range(per_tile):
                head = tile * per_tile + i
                gap = col[:, head : head + 1] + row[head : head + 1, :]
                left.append((jnp.exp2(jnp.minimum(gap, 80.0)) * scores).astype(BF16))
                here = (lane >= i * head_dim) & (lane < (i + 1) * head_dim)
                right.append(jnp.where(here, x_tile, 0.0).astype(BF16))
            inner = mm(jnp.concatenate(left, 1), jnp.concatenate(right, 0))
            inner = inner + mm(c_blk, hs[p][0, 0, :, lanes]) * mm(tab_ref[...], hot_ref[p, :, lanes])
            gate = silu(gates[p][:, lanes].astype(F32))
            parts[p][:, lanes] = inner * gate
            scales[p][:, lanes] = mm(tab0_ref[...], hot0_ref[p, :, lanes]) * gate


def early_index(k):
    return k - 1 if 1 <= k <= EARLY else 0


def intra(turn, pieces, bc, cc, tab, tab0, col, row, age, xs, hs, gate):
    tok, gn = bc.shape
    heads = row.shape[0]
    channels = gate.shape[1]
    head_dim = channels // heads
    groups = gn // STATE
    owned = channels // CLUSTER
    count = len(pieces)
    out = jax.ShapeDtypeStruct((tok, owned), F32)

    def piece_spec(block, index):
        return [pl.BlockSpec(block, functools.partial(index, k)) for k in pieces]

    return pl.pallas_call(
        functools.partial(intra_kernel, pieces, heads, head_dim),
        out_shape=(out,) * (2 * count),
        grid=(tok // SUB,),
        in_specs=[
            pl.BlockSpec((SUB, STATE), lambda i: (i, group_at(turn, groups))),
            pl.BlockSpec((SUB, STATE), lambda i: (i, group_at(turn, groups))),
            pl.BlockSpec((SUB, tab.shape[1]), lambda i: (i, 0)),
            pl.BlockSpec((SUB, tab0.shape[1]), lambda i: (i, 0)),
            pl.BlockSpec((SUB, LANES), lambda i: (i, 0)),
            pl.BlockSpec((heads, SUB), lambda i: (0, i)),
            pl.BlockSpec((SUB, LANES), lambda i: (i, 0)),
        ]
        + piece_spec((1, SUB, owned), lambda k, i: (early_index(k), i, 0))
        + piece_spec((1, 1, STATE, owned), lambda k, i: (early_index(k), jnp.maximum(i - 1, 0), 0, 0))
        + piece_spec((SUB, owned), lambda k, i: (i, lax.axis_index("seq") % CLUSTER ^ k)),
        out_specs=(pl.BlockSpec((SUB, owned), lambda i: (i, 0)),) * (2 * count),
        scratch_shapes=[pltpu.VMEM((count, 4 * heads, owned), BF16), pltpu.VMEM((count, 2 * heads, owned), BF16)],
        compiler_params=params(16),
        cost_estimate=cost(tok * SUB * owned * count * 4, tok * owned * count * 12, tok * SUB * owned * count // head_dim),
        name="intra",
    )(bc, cc, tab, tab0, col, row, age, *xs, *hs, *([gate] * count))


def final_kernel(turn, groups, *refs):
    cc_ref, gain_ref = refs[:2]
    share = CLUSTER // groups
    parts, scales, pieces = (refs[2 + i * share : 2 + (i + 1) * share] for i in range(3))
    out_hbm, y_ref, put_ref, sem = refs[-4:]
    tok, owned = parts[0].shape
    rows = y_ref.shape[1]
    copies = []
    c_lanes = pl.ds(pl.multiple_of(group_at(turn, groups) * STATE, STATE), STATE)
    columns = [pl.ds(place_of(turn * share + i, owned), owned) for i in range(share)]
    for low in range(0, tok, rows):
        span = slice(low, low + rows)
        c_blk = cc_ref[span, c_lanes]
        squares = None
        for i in range(share):
            for at in range(0, owned, CHUNK):
                lanes = slice(at, at + CHUNK)
                value = parts[i][span, lanes] + mm(c_blk, pieces[i][:, lanes]) * scales[i][span, lanes]
                y_ref[i, :, lanes] = value
                square = value * value
                for j in range(0, CHUNK, LANES):
                    piece = square[:, j : j + LANES]
                    squares = piece if squares is None else squares + piece
        factor = lax.rsqrt(jnp.sum(squares, axis=1, keepdims=True) * (1.0 / (share * owned)) + norm_eps)
        for i in range(share):
            put_ref[i, span, :] = (y_ref[i] * factor * gain_ref[:, columns[i]]).astype(BF16)
            copies.append(
                pltpu.make_async_copy(put_ref.at[i, span, :], out_hbm.at[span, columns[i]], sem.at[i, low // rows])
            )
            copies[-1].start()
    wait_all(copies)


def final(turn, cc, gain, parts, scales, pieces, so_far):
    tok, owned = parts[0].shape
    groups = cc.shape[1] // STATE
    share = CLUSTER // groups
    rows = 64
    operands = (cc, gain, *parts, *scales, *pieces) + (() if so_far is None else (so_far,))
    return pl.pallas_call(
        functools.partial(final_kernel, turn, groups),
        out_shape=jax.ShapeDtypeStruct((tok, owned * CLUSTER), BF16),
        in_specs=[VMEM] * (2 + 3 * share) + ([] if so_far is None else [ANY]),
        out_specs=ANY,
        scratch_shapes=[
            pltpu.VMEM((share, rows, owned), F32),
            pltpu.VMEM((share, tok, owned), BF16),
            pltpu.SemaphoreType.DMA((share, tok // rows)),
        ],
        input_output_aliases={} if so_far is None else {len(operands) - 1: 0},
        compiler_params=params(16),
        cost_estimate=cost(tok * STATE * owned * share * 2, tok * owned * share * 8),
        name="final",
    )(*operands)


def moved(value, hop):
    count = lax.axis_size("seq")
    return lax.ppermute(value, "seq", [(i, hop(i)) for i in range(count) if 0 <= hop(i) < count])


def exchanged(pieces, order):
    arrived = {0: pieces[0]}
    for k in order:
        arrived[k] = moved(pieces[k], lambda i, k=k: i ^ k)
    return [arrived[k] for k in range(CLUSTER)]


def before_cluster(total, pre):
    clusters = lax.axis_size("seq") // CLUSTER
    if clusters == 1:
        return jnp.zeros_like(total)
    if clusters == 2:
        return moved(total, lambda i: i ^ CLUSTER)
    shift = lambda value, steps: moved(value, lambda i: i + steps * CLUSTER)
    state, decay = shift((total.astype(F32), pre[CLUSTER, 0]), 1)
    step = 1
    while step < clusters - 1:
        earlier, fell = shift((state, decay), step)
        state, decay = state + decay[None, :] * earlier, decay * fell
        step *= 2
    return state


def tied(values, other):
    *values, _ = lax.optimization_barrier((*values, other))
    return values


def on_device(
    x_input,
    b_input,
    c_input,
    dt_input,
    decay_rate,
    gate_input,
    taps_x,
    taps_b,
    taps_c,
    norm_gain,
    doc_lengths,
):
    groups = b_input.shape[1] // STATE
    count = lax.axis_size("seq")
    pin = lambda value: pltpu.with_memory_space_constraint(value, pltpu.HBM)
    ends = pack(pin(x_input), pin(b_input), pin(c_input))
    tail = lax.ppermute(ends, "seq", [(i, (i + 1) % count) for i in range(count)])
    tab, tab0, col, row, d, age, part_x, part_b, xc, bc = conv(
        doc_lengths, dt_input.T, decay_rate[None, :], x_input, b_input, taps_x, taps_b
    )
    state, others, decay, weight = states(tab, d, xc, bc)
    xc, bc, extra, *sends = with_head(tail, part_x, part_b, taps_x, taps_b, age, state, decay, weight, xc, bc)
    known = (tail, age, tab, d, bc, taps_x, x_input)
    xs, hs = [None] + [xc] * EARLY, [None] * (1 + EARLY)
    for k in range(1 + EARLY, CLUSTER):
        late_x, late_h, late_send = late(k, *known)
        xs.append(late_x)
        hs.append(late_h)
        sends.append(late_send)
    cc, early_h, xs[0], hs[0], own_send = late(0, *known, (c_input, taps_c, others, extra, decay))
    hs[1 : 1 + EARLY] = [early_h] * EARLY
    shared = (bc, cc, tab, tab0, col, row)
    share = CLUSTER // groups

    def inner(turn, age):
        pieces = tuple(range(turn * share, (turn + 1) * share))
        return intra(turn, pieces, *shared, age, [xs[k] for k in pieces], [hs[k] for k in pieces], gate_input)

    local, pre, total = scan_blocks(exchanged([own_send, *sends], (1, 2, 3)))
    first = inner(0, *tied([age], total))
    joined = join(*tied([before_cluster(total, pre)], first[0]), local, pre)
    later = [inner(turn, *tied([age], joined[0])) for turn in range(1, groups)]
    entering = exchanged(joined, (1, 2, 3))
    output = None
    for turn, found in enumerate((first, *later)):
        mine = entering[turn * share : (turn + 1) * share]
        output = final(turn, cc, norm_gain[None, :], found[:share], found[share:], mine, output)
    return output


def solution(mesh):
    rows = P(("groups", "seq"), "dp")
    placed = (rows, rows, rows, rows, P("dp"), rows, P(None, "dp"), P(None, "dp"), P(None, "dp"), P("dp"), P("groups"))
    return jax.shard_map(on_device, mesh=mesh, in_specs=placed, out_specs=rows, check_vma=False)
```

```python
import functools

import jax
import jax.numpy as jnp
from jax import lax
from jax.experimental import pallas as pl
from jax.experimental.pallas import tpu as pltpu
from jax.sharding import PartitionSpec as P

STATE = 128
SUB = 128
CHUNK = 256
LANES = 128
ROWS = 32
CLUSTER = 4
EARLY = 2
LOG2E = 1.4426950408889634
norm_eps = 1e-05

F32 = jnp.float32
BF16 = jnp.bfloat16
VMEM = pl.BlockSpec(memory_space=pltpu.VMEM)
ANY = pl.BlockSpec(memory_space=pl.ANY)
HBM = pl.BlockSpec(memory_space=pltpu.HBM)


def params(mib=24):
    return pltpu.CompilerParams(vmem_limit_bytes=mib << 20)


def cost(flops, moved, transcendentals=0):
    return pl.CostEstimate(flops=flops, bytes_accessed=moved, transcendentals=transcendentals)


def doc_edges(dl_ref):
    edges = [0]
    for i in range(dl_ref.shape[0] - 1):
        edges.append(edges[-1] + dl_ref[i])
    return edges


def doc_start(token, edges):
    start = jnp.zeros_like(token)
    for edge in edges[1:]:
        start = jnp.where(token >= edge, jnp.maximum(start, edge), start)
    return start


def split2(value):
    high = value.astype(BF16)
    return high, (value - high.astype(F32)).astype(BF16)


def split3(value):
    high = value.astype(BF16)
    rest = value - high.astype(F32)
    mid = rest.astype(BF16)
    return high, mid, (rest - mid.astype(F32)).astype(BF16)


def mm(a, b):
    return jnp.dot(a, b, preferred_element_type=F32)


def silu(value):
    half = 0.5 * value
    return half + half * jnp.tanh(half)


def spread(base, rows, first_head, heads, width, head_dim):
    row = lax.broadcasted_iota(jnp.int32, (rows, width), 0) - (base + first_head)
    head = lax.broadcasted_iota(jnp.int32, (rows, width), 1) // head_dim
    return jnp.where((row == head) | (row == head + heads), 1.0, 0.0).astype(BF16)


def start_all(copies):
    for copy in copies:
        copy.start()


def wait_all(copies):
    for copy in copies:
        copy.wait()


def steps_of(row0, edges, dt_ref, rate_ref):
    heads, tok = dt_ref.shape
    upto = jnp.where(
        lax.broadcasted_iota(jnp.int32, (SUB, SUB), 0) <= lax.broadcasted_iota(jnp.int32, (SUB, SUB), 1), 1.0, 0.0
    ).astype(BF16)
    rate = jnp.concatenate([rate_ref[...], jnp.zeros((1, LANES - heads), F32)], 1)
    rate = jnp.broadcast_to(rate, (LANES, LANES)).T[:heads]
    found = []
    for c in range(tok // SUB):
        span = slice(c * SUB, (c + 1) * SUB)
        dt = dt_ref[:, span]
        step = jnp.maximum(dt, 0.0) + jnp.log1p(jnp.exp(-jnp.abs(dt)))
        parts = split3(-(step * rate))
        cum = mm(parts[0], upto) + (mm(parts[1], upto) + mm(parts[2], upto))
        token = row0 + c * SUB + lax.broadcasted_iota(jnp.int32, (heads, SUB), 1)
        found.append((span, row0 + c * SUB, step, cum, token))
    return found


def end_tables(row0, edges, dt_ref, rate_ref, tab_ref, d_ref):
    heads, tok = dt_ref.shape
    total = jnp.zeros((heads, 1), F32)
    decays = []
    for span, first, step, cum, token in steps_of(row0, edges, dt_ref, rate_ref):
        last = cum[:, SUB - 1 :]
        last_start = doc_start(jnp.int32(first + SUB - 1), edges)
        to_end = jnp.exp(last - cum) * step * jnp.where(token >= last_start, 1.0, 0.0)
        pair = [part.astype(F32) for part in split2(to_end)] + [jnp.zeros((LANES - 2 * heads, SUB), F32)]
        tab_ref[span, :] = jnp.concatenate(pair, 0).T[:, : 2 * heads].astype(BF16)
        decays.append(jnp.exp(last) * jnp.where(last_start < first, 1.0, 0.0))
        total = total + last
    end_start = doc_start(jnp.int32(row0 + tok - 1), edges)
    whole = jnp.exp(total) * jnp.where(end_start < row0, 1.0, 0.0)
    columns = [part.astype(F32) for part in split3(whole)] + decays[1:]
    columns.append(jnp.zeros((heads, LANES - len(columns)), F32))
    columns = jnp.concatenate([jnp.concatenate(columns, 1), jnp.zeros((LANES - heads, LANES), F32)], 0)
    halves = [part.astype(F32)[:, :heads] for part in split2(columns.T[:8])]
    d_ref[...] = jnp.concatenate(halves, 1).astype(BF16)


def inner_tables(row0, edges, dt_ref, rate_ref, tab_ref, col_ref, row_ref):
    heads = dt_ref.shape[0]
    total = jnp.zeros((heads, 1), F32)
    for span, first, step, cum, token in steps_of(row0, edges, dt_ref, rate_ref):
        start = doc_start(token, edges)
        since_sub = jnp.exp(cum) * jnp.where((start < first) & (first > row0), 1.0, 0.0)
        since_block = jnp.exp(cum + total) * jnp.where(start < row0, 1.0, 0.0)
        pairs = [part.astype(F32) for part in (*split2(since_block), *split2(since_sub))]
        tab_ref[span, :] = jnp.concatenate(pairs, 0).T.astype(BF16)
        zero = jnp.zeros_like(cum)
        col_ref[span, :] = jnp.concatenate([zero, zero, cum * LOG2E, zero], 0).T
        row_ref[:, span] = (jnp.log(step) - cum) * LOG2E
        total = total + cum[:, SUB - 1 :]


def pack_kernel(x_ref, b_ref, c_ref, out_ref):
    rows = [ref[...].astype(F32)[4:] for ref in (x_ref, b_ref, c_ref)]
    out_ref[...] = jnp.concatenate(rows, 1).astype(BF16)


def pack(x, b, c):
    tiles = x.shape[0] // 8
    widths = [value.shape[1] for value in (x, b, c)]
    return pl.pallas_call(
        pack_kernel,
        out_shape=jax.ShapeDtypeStruct((4, sum(widths)), BF16),
        grid=(1,),
        in_specs=[pl.BlockSpec((8, width), lambda i: (tiles - 1, 0)) for width in widths],
        out_specs=pl.BlockSpec((4, sum(widths)), lambda i: (0, 0)),
        compiler_params=params(16),
        name="pack",
    )(x, b, c)


def place_of(k, owned):
    return pl.multiple_of((lax.axis_index("seq") % CLUSTER ^ k) * owned, owned)


def fill_masks(age_ref, mask_ref):
    for back in range(1, mask_ref.shape[0] + 1):
        mask_ref[back - 1] = jnp.where(age_ref[...] >= back, 1.0, 0.0)


def convolve(ext_ref, mask_ref, taps, emit):
    tok = ext_ref.shape[0] - 8
    repeats = ext_ref.shape[1] // LANES
    for low in range(0, tok, ROWS):
        total = ext_ref[8 + low : 8 + low + ROWS, :] * taps[-1]
        for back in range(1, len(taps)):
            mask = jnp.concatenate([mask_ref[back - 1, low : low + ROWS, :]] * repeats, 1)
            window = ext_ref[8 + low - back : 8 + low - back + ROWS, :]
            total = total + (window * taps[-1 - back]) * mask
        emit(low, total)


def state_of(at, heads, head_dim, bt_ref, tab_ref, d_ref, x_rows, h_put):
    one_hot = spread(0, 2 * heads, at // head_dim, heads, CHUNK, head_dim)
    decay = mm(d_ref[...], one_hot)
    tok = tab_ref.shape[0]
    state = None
    for c in range(tok // SUB):
        rows = slice(c * SUB, (c + 1) * SUB)
        weight = mm(tab_ref[rows, :], one_hot)
        if c == 0:
            head_weight = weight[:8]
        local = mm(bt_ref[:, rows], (x_rows(c) * weight).astype(BF16))
        if state is None:
            state = local
        else:
            h_put(c - 1, state)
            state = local + decay[2 + c : 3 + c, :] * state
    return state, decay, head_weight


def put_piece(send_ref, low, state):
    for tile in range(state.shape[1] // LANES):
        at = low * STATE + tile * STATE
        send_ref[at : at + STATE, :] = state[:, tile * LANES : (tile + 1) * LANES].astype(BF16)


def put_decay(send_ref, decay):
    tiles = decay.shape[1] // LANES
    rows = [decay[:2, tile * LANES : (tile + 1) * LANES] for tile in range(tiles)]
    send_ref[tiles * STATE :, :] = jnp.concatenate(rows, 0).astype(BF16)


def piece_shape(owned):
    return jax.ShapeDtypeStruct((owned // LANES * (STATE + 2), LANES), BF16)


def conv_kernel(
    dl_ref,
    dt_ref,
    rate_ref,
    x_ref,
    b_ref,
    taps_x_ref,
    taps_b_ref,
    tab_ref,
    d_ref,
    age_ref,
    part_x_ref,
    part_b_ref,
    xc_ref,
    bc_ref,
    ext_ref,
    mask_ref,
):
    tok, channels = x_ref.shape
    owned = channels // CLUSTER
    per = owned // CHUNK
    row0 = lax.axis_index("seq") * tok
    edges = doc_edges(dl_ref)
    end_tables(row0, edges, dt_ref, rate_ref, tab_ref, d_ref)
    token = row0 + lax.broadcasted_iota(jnp.int32, (tok, LANES), 0)
    age_ref[...] = token - doc_start(token, edges)
    fill_masks(age_ref, mask_ref)
    ext_ref[:8, :] = jnp.zeros((8, CHUNK), F32)
    taps_len = taps_x_ref.shape[0]

    def body(i, carry):
        k = i // per
        lanes = pl.ds(pl.multiple_of(place_of(k + 1, owned) + (i % per) * CHUNK, CHUNK), CHUNK)
        inner = pl.ds(pl.multiple_of((i % per) * CHUNK, CHUNK), CHUNK)
        ext_ref[8:, :] = x_ref[:, lanes].astype(F32)

        def emit(low, total):
            if low == 0:
                part_x_ref[k, :, inner] = total[:8]
            xc_ref[k, low : low + ROWS, inner] = silu(total).astype(BF16)

        convolve(ext_ref, mask_ref, [taps_x_ref[j : j + 1, lanes] for j in range(taps_len)], emit)
        return carry

    lax.fori_loop(0, EARLY * per, body, 0)
    ext_ref[8:, :] = b_ref[...].astype(F32)

    def emit_b(low, total):
        if low == 0:
            part_b_ref[...] = total[:8]
        bc_ref[low : low + ROWS, :] = silu(total).astype(BF16)

    convolve(ext_ref, mask_ref, [taps_b_ref[j : j + 1, :] for j in range(taps_len)], emit_b)


def conv(doc_lengths, dt_t, rate, x, b, taps_x, taps_b):
    heads = dt_t.shape[0]
    tok, channels = x.shape
    gn = b.shape[1]
    owned = channels // CLUSTER
    shape = jax.ShapeDtypeStruct
    return pl.pallas_call(
        conv_kernel,
        out_shape=(
            shape((tok, 2 * heads), BF16),
            shape((8, 2 * heads), BF16),
            shape((tok, LANES), jnp.int32),
            shape((EARLY, 8, owned), F32),
            shape((8, gn), F32),
            shape((EARLY, tok, owned), BF16),
            shape((tok, gn), BF16),
        ),
        in_specs=[pl.BlockSpec(memory_space=pltpu.SMEM)] + [VMEM] * 6,
        out_specs=(VMEM,) * 7,
        scratch_shapes=[
            pltpu.VMEM((tok + 8, CHUNK), F32),
            pltpu.VMEM((taps_x.shape[0] - 1, tok, LANES), F32),
        ],
        compiler_params=params(16),
        cost_estimate=cost(tok * channels * 16, tok * channels * 4, tok * channels),
        name="conv",
    )(doc_lengths, dt_t, rate, x, b, taps_x, taps_b)


def state_kernel(tab_ref, d_ref, xc_ref, bc_ref, s_ref, h_ref, decay_ref, weight_ref, bt_ref):
    pieces, tok, owned = xc_ref.shape
    gn = bc_ref.shape[1]
    channels = owned * CLUSTER
    heads = d_ref.shape[1] // 2
    for group in range(gn // STATE):
        b_blk = bc_ref[:, group * STATE : (group + 1) * STATE].astype(F32)[8:]
        bt_ref[group] = jnp.concatenate([jnp.zeros((8, STATE), F32), b_blk], 0).T.astype(BF16)
    for k in range(pieces):
        at = place_of(k + 1, owned)
        group = at // (channels // (gn // STATE))
        for part in range(owned // CHUNK):
            here = slice(part * CHUNK, (part + 1) * CHUNK)

            def h_put(c, value):
                h_ref[k, c, :, here] = value

            state, decay, weight = state_of(
                at + part * CHUNK,
                heads,
                channels // heads,
                bt_ref.at[group],
                tab_ref,
                d_ref,
                lambda c: xc_ref[k, c * SUB : (c + 1) * SUB, here].astype(F32),
                h_put,
            )
            s_ref[k, :, here] = state
            decay_ref[k, :, here] = decay
            weight_ref[k, :, here] = weight


def states(tab, d, xc, bc):
    pieces, tok, owned = xc.shape
    gn = bc.shape[1]
    row = jax.ShapeDtypeStruct((pieces, 8, owned), F32)
    return pl.pallas_call(
        state_kernel,
        out_shape=(
            jax.ShapeDtypeStruct((pieces, STATE, owned), F32),
            jax.ShapeDtypeStruct((pieces, tok // SUB - 1, STATE, owned), F32),
            row,
            row,
        ),
        in_specs=[VMEM] * 4,
        out_specs=(VMEM,) * 4,
        scratch_shapes=[pltpu.VMEM((gn // STATE, STATE, tok), BF16)],
        compiler_params=params(16),
        cost_estimate=cost(tok * STATE * owned * pieces * 4, tok * owned * pieces * 4),
        name="state",
    )(tab, d, xc, bc)


def head_kernel(
    tail_ref,
    part_x_ref,
    part_b_ref,
    taps_x_ref,
    taps_b_ref,
    age_ref,
    s_ref,
    decay_ref,
    weight_ref,
    xc_in,
    bc_in,
    xc_ref,
    bc_ref,
    extra_ref,
    *rest,
):
    pieces, _, owned = s_ref.shape
    sends = rest[:pieces]
    ext_ref, bt_ref, xw_ref = rest[pieces:]
    gn = bc_in.shape[1]
    channels = owned * CLUSTER
    taps_len = taps_x_ref.shape[0]
    ext_ref[4:8, :] = tail_ref[...].astype(F32)
    ext_ref[8:, :] = jnp.zeros_like(ext_ref[8:, :])

    def head_of(part, lanes, taps, width):
        total = part
        age = jnp.concatenate([age_ref[:8, :]] * (width // LANES), 1)
        for back in range(1, taps_len):
            total = total + jnp.where(age >= back, ext_ref[8 - back : 16 - back, lanes] * taps[-1 - back], 0.0)
        return silu(total).astype(BF16)

    head = head_of(
        part_b_ref[...], slice(channels, channels + gn), [taps_b_ref[j : j + 1, :] for j in range(taps_len)], gn
    )
    bc_ref[:8, :] = head
    for group in range(gn // STATE):
        rows = head[:, group * STATE : (group + 1) * STATE].astype(F32)
        bt_ref[group] = jnp.concatenate([rows, jnp.zeros((LANES - 8, STATE), F32)], 0).T.astype(BF16)
    xw_ref[...] = jnp.zeros_like(xw_ref)
    for k in range(pieces):
        at = place_of(k + 1, owned)
        lanes = pl.ds(at, owned)
        head = head_of(part_x_ref[k], lanes, [taps_x_ref[j : j + 1, lanes] for j in range(taps_len)], owned)
        xc_ref[k, :8, :] = head
        xw_ref[:8, :] = head.astype(F32) * weight_ref[k]
        extra = mm(bt_ref[at // (channels // (gn // STATE))], xw_ref[...].astype(BF16))
        extra_ref[k] = extra
        decay = decay_ref[k]
        rest_of_block = decay[3:4, :]
        for c in range(4, 3 + xc_in.shape[1] // SUB - 1):
            rest_of_block = rest_of_block * decay[c : c + 1, :]
        put_piece(sends[k], 0, s_ref[k] + rest_of_block * extra)
        put_decay(sends[k], decay)


def with_head(tail, part_x, part_b, taps_x, taps_b, age, state, decay, weight, xc, bc):
    pieces, _, owned = xc.shape
    gn = bc.shape[1]
    shape = jax.ShapeDtypeStruct
    return pl.pallas_call(
        head_kernel,
        out_shape=(shape(xc.shape, BF16), shape(bc.shape, BF16), shape(state.shape, F32))
        + (piece_shape(owned),) * pieces,
        in_specs=[VMEM] * 11,
        out_specs=(VMEM,) * (3 + pieces),
        scratch_shapes=[
            pltpu.VMEM((16, tail.shape[1]), F32),
            pltpu.VMEM((gn // STATE, STATE, LANES), BF16),
            pltpu.VMEM((LANES, owned), F32),
        ],
        input_output_aliases={9: 0, 10: 1},
        compiler_params=params(16),
        cost_estimate=cost(STATE * LANES * owned * pieces * 2, STATE * owned * pieces * 10),
        name="head",
    )(tail, part_x, part_b, taps_x, taps_b, age, state, decay, weight, xc, bc)


def late_kernel(k, with_c, *refs):
    tail_ref, age_ref, tab_ref, d_ref, bc_ref, taps_x_ref, x_ref = refs[:7]
    refs = refs[7:]
    if with_c:
        c_ref, taps_c_ref, others_ref, extra_ref, decay_ref, dt_ref, rate_ref, dl_ref = refs[:8]
        cc_ref, early_ref, inner_ref, col_ref, row_ref = refs[8:13]
        refs = refs[13:]
    xc_ref, h_ref, send_ref, bt_ref, ext_ref, mask_ref = refs
    tok, channels = x_ref.shape
    owned = channels // CLUSTER
    gn = bc_ref.shape[1]
    per = owned // CHUNK
    heads = d_ref.shape[1] // 2
    head_dim = channels // heads
    taps_len = taps_x_ref.shape[0]
    at = place_of(k, owned)
    fill_masks(age_ref, mask_ref)
    group = at // (channels // (gn // STATE))
    b_blk = bc_ref[:, pl.ds(pl.multiple_of(group * STATE, STATE), STATE)]
    bt_ref[...] = b_blk.astype(F32).T.astype(BF16)
    if with_c:
        row0 = lax.axis_index("seq") * tok
        inner_tables(row0, doc_edges(dl_ref), dt_ref, rate_ref, inner_ref, col_ref, row_ref)
        for i in range(EARLY):
            extra = extra_ref[i]
            for c in range(tok // SUB - 1):
                if c > 0:
                    extra = extra * decay_ref[i, 2 + c : 3 + c, :]
                early_ref[i, c] = (others_ref[i, c] + extra).astype(BF16)
    decays = []
    for part in range(per + with_c):
        here = slice(part * CHUNK, (part + 1) * CHUNK)
        if part < per:
            lanes = pl.ds(pl.multiple_of(at + part * CHUNK, CHUNK), CHUNK)
            taps = [taps_x_ref[j : j + 1, lanes] for j in range(taps_len)]
        else:
            lanes = slice(channels + gn, channels + 2 * gn)
            taps = [taps_c_ref[j : j + 1, :] for j in range(taps_len)]
        ext_ref[4:8, :] = tail_ref[:, lanes].astype(F32)
        ext_ref[8:, :] = (x_ref[:, lanes] if part < per else c_ref[...]).astype(F32)

        def emit(low, total):
            value = silu(total).astype(BF16)
            if part < per:
                xc_ref[0, low : low + ROWS, here] = value
            else:
                cc_ref[low : low + ROWS, :] = value

        convolve(ext_ref, mask_ref, taps, emit)
        if part < per:

            def h_put(c, value):
                h_ref[0, c, :, here] = value.astype(BF16)

            state, decay, _ = state_of(
                at + part * CHUNK,
                heads,
                head_dim,
                bt_ref,
                tab_ref,
                d_ref,
                lambda c: xc_ref[0, c * SUB : (c + 1) * SUB, here].astype(F32),
                h_put,
            )
            put_piece(send_ref, part * (CHUNK // LANES), state)
            decays.append(decay)
    put_decay(send_ref, jnp.concatenate(decays, 1))


def late(k, tail, age, tab, d, bc, taps_x, x, with_c=()):
    tok, channels = x.shape
    owned = channels // CLUSTER
    gn = bc.shape[1]
    subs = tok // SUB - 1
    shape = jax.ShapeDtypeStruct
    heads = d.shape[1] // 2
    extra_out = (
        shape((tok, gn), BF16),
        shape((EARLY, subs, STATE, owned), BF16),
        shape((tok, LANES), BF16),
        shape((tok, LANES), F32),
        shape((heads, tok), F32),
    )
    if not with_c:
        extra_out = ()
    return pl.pallas_call(
        functools.partial(late_kernel, k, bool(with_c)),
        out_shape=(
            *extra_out,
            shape((1, tok, owned), BF16),
            shape((1, subs, STATE, owned), BF16),
            piece_shape(owned),
        ),
        in_specs=[VMEM] * 7 + ([VMEM] * (len(with_c) - 1) + [pl.BlockSpec(memory_space=pltpu.SMEM)] if with_c else []),
        out_specs=(VMEM,) * (3 + len(extra_out)),
        scratch_shapes=[
            pltpu.VMEM((STATE, tok), BF16),
            pltpu.VMEM((tok + 8, CHUNK), F32),
            pltpu.VMEM((taps_x.shape[0] - 1, tok, LANES), F32),
        ],
        compiler_params=params(16),
        cost_estimate=cost(tok * owned * 16 + tok * STATE * owned * 4, tok * owned * 8, tok * owned),
        name="own" if with_c else "late",
    )(tail, age, tab, d, bc, taps_x, x, *with_c)


def collect_kernel(*refs):
    *pieces, out_ref = refs
    for k, ref in enumerate(pieces):
        out_ref[k] = ref[...]


def collect(pieces):
    return pl.pallas_call(
        collect_kernel,
        out_shape=jax.ShapeDtypeStruct((len(pieces), *pieces[0].shape), BF16),
        in_specs=[VMEM] * len(pieces),
        out_specs=VMEM,
        compiler_params=params(16),
        cost_estimate=cost(0, 4 * len(pieces) * pieces[0].size),
        name="collect",
    )(*pieces)


def scan_kernel(*refs):
    first_ref, *last, local_ref, pre_ref, total_ref = refs
    pieces = [first_ref.at[k] for k in range(first_ref.shape[0])] + last
    mine = lax.axis_index("seq") % CLUSTER

    def in_order(values):
        bit = 1
        while bit < CLUSTER:
            odd = (mine & bit) != 0
            values = [jnp.where(odd, values[i ^ bit], values[i]) for i in range(CLUSTER)]
            bit *= 2
        return values

    owned = total_ref.shape[1]
    tiles = owned // LANES
    rows = [ref[tiles * STATE :, :].astype(F32) for ref in pieces]
    decays = in_order(
        [jnp.concatenate([row[2 * t : 2 * t + 1] + row[2 * t + 1 : 2 * t + 2] for t in range(tiles)], 1) for row in rows]
    )
    pre = jnp.ones((1, owned), F32)
    for i in range(CLUSTER):
        pre_ref[i] = jnp.broadcast_to(pre, (8, owned))
        pre = pre * decays[i]
    pre_ref[CLUSTER] = jnp.broadcast_to(pre, (8, owned))
    for at in range(0, owned, LANES):
        lanes = slice(at, at + LANES)
        for low in range(0, STATE, 64):
            rows = slice(low, low + 64)
            at_rows = slice(at + low, at + low + 64)
            values = in_order([ref[at_rows, :].astype(F32) for ref in pieces])
            local_ref[0, rows, lanes] = jnp.zeros((64, LANES), F32)
            state = values[0]
            for i in range(1, CLUSTER):
                local_ref[i, rows, lanes] = state
                state = decays[i][:, lanes] * state + values[i]
            total_ref[rows, lanes] = state.astype(BF16)


def scan_blocks(pieces):
    operands = (collect(pieces[: 1 + EARLY]), *pieces[1 + EARLY :])
    owned = pieces[0].shape[0] // (STATE + 2) * LANES
    return pl.pallas_call(
        scan_kernel,
        out_shape=(
            jax.ShapeDtypeStruct((CLUSTER, STATE, owned), F32),
            jax.ShapeDtypeStruct((CLUSTER + 1, 8, owned), F32),
            jax.ShapeDtypeStruct((STATE, owned), BF16),
        ),
        in_specs=[VMEM] * len(operands),
        out_specs=(VMEM,) * 3,
        compiler_params=params(),
        cost_estimate=cost(CLUSTER * STATE * owned * 2, CLUSTER * STATE * owned * 6),
        name="cluster_scan",
    )(*operands)


def join_kernel(before_ref, local_ref, pre_ref, *outs):
    index = lax.axis_index("seq")
    mine = index % CLUSTER
    before = jnp.where(index >= CLUSTER, before_ref[...].astype(F32), 0.0)
    for k in range(CLUSTER):
        block = mine ^ k
        outs[k][...] = (local_ref[block] + pre_ref[block][0:1] * before).astype(BF16)


def join(before, local, pre):
    owned = local.shape[2]
    return pl.pallas_call(
        join_kernel,
        out_shape=(jax.ShapeDtypeStruct((STATE, owned), BF16),) * CLUSTER,
        in_specs=[VMEM] * 3,
        out_specs=(VMEM,) * CLUSTER,
        compiler_params=params(),
        cost_estimate=cost(CLUSTER * STATE * owned * 2, CLUSTER * STATE * owned * 6),
        name="join",
    )(before, local, pre)


def group_at(turn, groups):
    return (lax.axis_index("seq") % CLUSTER) // (CLUSTER // groups) ^ turn


def intra_kernel(pieces, heads, head_dim, *refs):
    bc_ref, cc_ref, tab_ref, col_ref, row_ref, age_ref = refs[:6]
    refs = refs[6:]
    count = len(pieces)
    xs, hs, gates, parts, scales = (refs[i * count : (i + 1) * count] for i in range(5))
    hot_ref, hot0_ref = refs[5 * count :]
    owned = parts[0].shape[1]
    per_piece = owned // head_dim
    mine = lax.axis_index("seq") % CLUSTER

    @pl.when(pl.program_id(0) == 0)
    def _():
        for p, k in enumerate(pieces):
            hot_ref[p] = spread(2 * heads, 4 * heads, (mine ^ k) * per_piece, heads, owned, head_dim)
            hot0_ref[p] = spread(0, 2 * heads, (mine ^ k) * per_piece, heads, owned, head_dim)

    back = lax.broadcasted_iota(jnp.int32, (SUB, SUB), 0) - lax.broadcasted_iota(jnp.int32, (SUB, SUB), 1)
    keep = (back >= 0) & (back <= age_ref[...])
    c_blk = cc_ref[...]
    scores = lax.dot_general(c_blk, bc_ref[...], (((1,), (1,)), ((), ())), preferred_element_type=F32)
    scores = jnp.where(keep, scores, 0.0)
    lane = lax.broadcasted_iota(jnp.int32, (SUB, LANES), 1)
    per_tile = LANES // head_dim
    for p, k in enumerate(pieces):
        first = (mine ^ k) * per_piece
        col = pltpu.roll(col_ref[...], LANES - (2 * heads + first), 1)
        row = row_ref[pl.ds(pl.multiple_of(first, per_piece), per_piece), :]
        for tile in range(owned // LANES):
            lanes = slice(tile * LANES, (tile + 1) * LANES)
            x_tile = xs[p][0, :, lanes].astype(F32)
            left, right = [], []
            for i in range(per_tile):
                head = tile * per_tile + i
                gap = col[:, head : head + 1] + row[head : head + 1, :]
                left.append((jnp.exp2(jnp.minimum(gap, 80.0)) * scores).astype(BF16))
                here = (lane >= i * head_dim) & (lane < (i + 1) * head_dim)
                right.append(jnp.where(here, x_tile, 0.0).astype(BF16))
            inner = mm(jnp.concatenate(left, 1), jnp.concatenate(right, 0))
            inner = inner + mm(c_blk, hs[p][0, 0, :, lanes]) * mm(tab_ref[...], hot_ref[p, :, lanes])
            gate = silu(gates[p][:, lanes].astype(F32))
            parts[p][:, lanes] = inner * gate
            scales[p][:, lanes] = mm(tab_ref[:, : 2 * heads], hot0_ref[p, :, lanes]) * gate


def early_index(k):
    return k - 1 if 1 <= k <= EARLY else 0


def intra(turn, pieces, bc, cc, tab, col, row, age, xs, hs, gate):
    tok, gn = bc.shape
    heads = row.shape[0]
    channels = gate.shape[1]
    head_dim = channels // heads
    groups = gn // STATE
    owned = channels // CLUSTER
    count = len(pieces)
    out = jax.ShapeDtypeStruct((tok, owned), F32)

    def piece_spec(block, index):
        return [pl.BlockSpec(block, functools.partial(index, k)) for k in pieces]

    return pl.pallas_call(
        functools.partial(intra_kernel, pieces, heads, head_dim),
        out_shape=(out,) * (2 * count),
        grid=(tok // SUB,),
        in_specs=[
            pl.BlockSpec((SUB, STATE), lambda i: (i, group_at(turn, groups))),
            pl.BlockSpec((SUB, STATE), lambda i: (i, group_at(turn, groups))),
            pl.BlockSpec((SUB, tab.shape[1]), lambda i: (i, 0)),
            pl.BlockSpec((SUB, LANES), lambda i: (i, 0)),
            pl.BlockSpec((heads, SUB), lambda i: (0, i)),
            pl.BlockSpec((SUB, LANES), lambda i: (i, 0)),
        ]
        + piece_spec((1, SUB, owned), lambda k, i: (early_index(k), i, 0))
        + piece_spec((1, 1, STATE, owned), lambda k, i: (early_index(k), jnp.maximum(i - 1, 0), 0, 0))
        + piece_spec((SUB, owned), lambda k, i: (i, lax.axis_index("seq") % CLUSTER ^ k)),
        out_specs=(pl.BlockSpec((SUB, owned), lambda i: (i, 0)),) * (2 * count),
        scratch_shapes=[pltpu.VMEM((count, 4 * heads, owned), BF16), pltpu.VMEM((count, 2 * heads, owned), BF16)],
        compiler_params=params(16),
        cost_estimate=cost(tok * SUB * owned * count * 4, tok * owned * count * 12, tok * SUB * owned * count // head_dim),
        name="intra",
    )(bc, cc, tab, col, row, age, *xs, *hs, *([gate] * count))


def final_kernel(turn, groups, *refs):
    cc_ref, gain_ref = refs[:2]
    share = CLUSTER // groups
    parts, scales, pieces = (refs[2 + i * share : 2 + (i + 1) * share] for i in range(3))
    out_hbm, y_ref, put_ref, sem = refs[-4:]
    tok, owned = parts[0].shape
    rows = y_ref.shape[1]
    copies = []
    c_lanes = pl.ds(pl.multiple_of(group_at(turn, groups) * STATE, STATE), STATE)
    columns = [pl.ds(place_of(turn * share + i, owned), owned) for i in range(share)]
    for low in range(0, tok, rows):
        span = slice(low, low + rows)
        c_blk = cc_ref[span, c_lanes]
        squares = None
        for i in range(share):
            for at in range(0, owned, CHUNK):
                lanes = slice(at, at + CHUNK)
                value = parts[i][span, lanes] + mm(c_blk, pieces[i][:, lanes]) * scales[i][span, lanes]
                y_ref[i, :, lanes] = value
                square = value * value
                for j in range(0, CHUNK, LANES):
                    piece = square[:, j : j + LANES]
                    squares = piece if squares is None else squares + piece
        factor = lax.rsqrt(jnp.sum(squares, axis=1, keepdims=True) * (1.0 / (share * owned)) + norm_eps)
        for i in range(share):
            put_ref[i, span, :] = (y_ref[i] * factor * gain_ref[:, columns[i]]).astype(BF16)
            copies.append(
                pltpu.make_async_copy(put_ref.at[i, span, :], out_hbm.at[span, columns[i]], sem.at[i, low // rows])
            )
            copies[-1].start()
    wait_all(copies)


def final(turn, cc, gain, parts, scales, pieces, so_far):
    tok, owned = parts[0].shape
    groups = cc.shape[1] // STATE
    share = CLUSTER // groups
    rows = 64
    operands = (cc, gain, *parts, *scales, *pieces) + (() if so_far is None else (so_far,))
    return pl.pallas_call(
        functools.partial(final_kernel, turn, groups),
        out_shape=jax.ShapeDtypeStruct((tok, owned * CLUSTER), BF16),
        in_specs=[VMEM] * (2 + 3 * share) + ([] if so_far is None else [ANY]),
        out_specs=ANY,
        scratch_shapes=[
            pltpu.VMEM((share, rows, owned), F32),
            pltpu.VMEM((share, tok, owned), BF16),
            pltpu.SemaphoreType.DMA((share, tok // rows)),
        ],
        input_output_aliases={} if so_far is None else {len(operands) - 1: 0},
        compiler_params=params(16),
        cost_estimate=cost(tok * STATE * owned * share * 2, tok * owned * share * 8),
        name="final",
    )(*operands)


def moved(value, hop):
    count = lax.axis_size("seq")
    return lax.ppermute(value, "seq", [(i, hop(i)) for i in range(count) if 0 <= hop(i) < count])


def exchanged(pieces, order):
    arrived = {0: pieces[0]}
    for k in order:
        arrived[k] = moved(pieces[k], lambda i, k=k: i ^ k)
    return [arrived[k] for k in range(CLUSTER)]


def before_cluster(total, pre):
    clusters = lax.axis_size("seq") // CLUSTER
    if clusters == 1:
        return jnp.zeros_like(total)
    if clusters == 2:
        return moved(total, lambda i: i ^ CLUSTER)
    shift = lambda value, steps: moved(value, lambda i: i + steps * CLUSTER)
    state, decay = shift((total.astype(F32), pre[CLUSTER, 0]), 1)
    step = 1
    while step < clusters - 1:
        earlier, fell = shift((state, decay), step)
        state, decay = state + decay[None, :] * earlier, decay * fell
        step *= 2
    return state


def tied(values, other):
    *values, _ = lax.optimization_barrier((*values, other))
    return values


def on_device(
    x_input,
    b_input,
    c_input,
    dt_input,
    decay_rate,
    gate_input,
    taps_x,
    taps_b,
    taps_c,
    norm_gain,
    doc_lengths,
):
    groups = b_input.shape[1] // STATE
    count = lax.axis_size("seq")
    pin = lambda value: pltpu.with_memory_space_constraint(value, pltpu.HBM)
    ends = pack(pin(x_input), pin(b_input), pin(c_input))
    tail = lax.ppermute(ends, "seq", [(i, (i + 1) % count) for i in range(count)])
    rates = (dt_input.T, decay_rate[None, :])
    tab, d, age, part_x, part_b, xc, bc = conv(doc_lengths, *rates, x_input, b_input, taps_x, taps_b)
    state, others, decay, weight = states(tab, d, xc, bc)
    xc, bc, extra, *sends = with_head(tail, part_x, part_b, taps_x, taps_b, age, state, decay, weight, xc, bc)
    known = (tail, age, tab, d, bc, taps_x, x_input)
    xs, hs = [None] + [xc] * EARLY, [None] * (1 + EARLY)
    for k in range(1 + EARLY, CLUSTER):
        late_x, late_h, late_send = late(k, *known)
        xs.append(late_x)
        hs.append(late_h)
        sends.append(late_send)
    cc, early_h, inner_tab, col, row, xs[0], hs[0], own_send = late(
        0, *known, (c_input, taps_c, others, extra, decay, *rates, doc_lengths)
    )
    hs[1 : 1 + EARLY] = [early_h] * EARLY
    shared = (bc, cc, inner_tab, col, row)
    share = CLUSTER // groups

    def inner(turn, age):
        pieces = tuple(range(turn * share, (turn + 1) * share))
        return intra(turn, pieces, *shared, age, [xs[k] for k in pieces], [hs[k] for k in pieces], gate_input)

    local, pre, total = scan_blocks(exchanged([own_send, *sends], (1, 2, 3)))
    first = inner(0, *tied([age], total))
    joined = join(*tied([before_cluster(total, pre)], first[0]), local, pre)
    later = [inner(turn, *tied([age], joined[0])) for turn in range(1, groups)]
    entering = exchanged(joined, (1, 2, 3))
    output = None
    for turn, found in enumerate((first, *later)):
        mine = entering[turn * share : (turn + 1) * share]
        output = final(turn, cc, norm_gain[None, :], found[:share], found[share:], mine, output)
    return output


def solution(mesh):
    rows = P(("groups", "seq"), "dp")
    placed = (rows, rows, rows, rows, P("dp"), rows, P(None, "dp"), P(None, "dp"), P(None, "dp"), P("dp"), P("groups"))
    return jax.shard_map(on_device, mesh=mesh, in_specs=placed, out_specs=rows, check_vma=False)
```

```python
import functools

import jax
import jax.numpy as jnp
from jax import lax
from jax.experimental import pallas as pl
from jax.experimental.pallas import tpu as pltpu
from jax.sharding import PartitionSpec as P

STATE = 128
SUB = 128
CHUNK = 256
LANES = 128
ROWS = 32
CLUSTER = 4
EARLY = 3
LOG2E = 1.4426950408889634
norm_eps = 1e-05

F32 = jnp.float32
BF16 = jnp.bfloat16
VMEM = pl.BlockSpec(memory_space=pltpu.VMEM)
ANY = pl.BlockSpec(memory_space=pl.ANY)
HBM = pl.BlockSpec(memory_space=pltpu.HBM)


def params(mib=24):
    return pltpu.CompilerParams(vmem_limit_bytes=mib << 20)


def cost(flops, moved, transcendentals=0):
    return pl.CostEstimate(flops=flops, bytes_accessed=moved, transcendentals=transcendentals)


def doc_edges(dl_ref):
    lengths = dl_ref[...]
    edges = [lengths[:, :1]]
    for i in range(1, lengths.shape[1] - 1):
        edges.append(edges[-1] + lengths[:, i : i + 1])
    return edges


def doc_start(token, edges):
    start = jnp.zeros_like(token)
    for edge in edges:
        start = jnp.where(token >= edge, jnp.maximum(start, edge), start)
    return start


def one(value):
    return jnp.full((1, 1), value, jnp.int32)


def split2(value):
    high = value.astype(BF16)
    return high, (value - high.astype(F32)).astype(BF16)


def split3(value):
    high = value.astype(BF16)
    rest = value - high.astype(F32)
    mid = rest.astype(BF16)
    return high, mid, (rest - mid.astype(F32)).astype(BF16)


def mm(a, b):
    return jnp.dot(a, b, preferred_element_type=F32)


def silu(value):
    half = 0.5 * value
    return half + half * jnp.tanh(half)


def spread(base, rows, first_head, heads, width, head_dim):
    row = lax.broadcasted_iota(jnp.int32, (rows, width), 0) - (base + first_head)
    head = lax.broadcasted_iota(jnp.int32, (rows, width), 1) // head_dim
    return jnp.where((row == head) | (row == head + heads), 1.0, 0.0).astype(BF16)


def start_all(copies):
    for copy in copies:
        copy.start()


def wait_all(copies):
    for copy in copies:
        copy.wait()


def steps_of(row0, edges, dt_ref, rate_ref):
    heads, tok = dt_ref.shape
    upto = jnp.where(
        lax.broadcasted_iota(jnp.int32, (SUB, SUB), 0) <= lax.broadcasted_iota(jnp.int32, (SUB, SUB), 1), 1.0, 0.0
    ).astype(BF16)
    rate = jnp.concatenate([rate_ref[...], jnp.zeros((1, LANES - heads), F32)], 1)
    rate = jnp.broadcast_to(rate, (LANES, LANES)).T[:heads]
    found = []
    for c in range(tok // SUB):
        span = slice(c * SUB, (c + 1) * SUB)
        dt = dt_ref[:, span]
        step = jnp.maximum(dt, 0.0) + jnp.log1p(jnp.exp(-jnp.abs(dt)))
        parts = split3(-(step * rate))
        cum = mm(parts[0], upto) + (mm(parts[1], upto) + mm(parts[2], upto))
        token = row0 + c * SUB + lax.broadcasted_iota(jnp.int32, (heads, SUB), 1)
        found.append((span, row0 + c * SUB, step, cum, token))
    return found


def end_tables(row0, edges, dt_ref, rate_ref, tab_ref, d_ref):
    heads, tok = dt_ref.shape
    total = jnp.zeros((heads, 1), F32)
    decays = []
    for span, first, step, cum, token in steps_of(row0, edges, dt_ref, rate_ref):
        last = cum[:, SUB - 1 :]
        last_start = doc_start(one(first + SUB - 1), edges)
        to_end = jnp.exp(last - cum) * step * jnp.where(token >= last_start, 1.0, 0.0)
        pair = [part.astype(F32) for part in split2(to_end)] + [jnp.zeros((LANES - 2 * heads, SUB), F32)]
        tab_ref[span, :] = jnp.concatenate(pair, 0).T[:, : 2 * heads].astype(BF16)
        decays.append(jnp.exp(last) * jnp.where(last_start < first, 1.0, 0.0))
        total = total + last
    end_start = doc_start(one(row0 + tok - 1), edges)
    whole = jnp.exp(total) * jnp.where(end_start < row0, 1.0, 0.0)
    columns = [part.astype(F32) for part in split3(whole)] + decays[1:]
    columns.append(jnp.zeros((heads, LANES - len(columns)), F32))
    columns = jnp.concatenate([jnp.concatenate(columns, 1), jnp.zeros((LANES - heads, LANES), F32)], 0)
    halves = [part.astype(F32)[:, :heads] for part in split2(columns.T[:8])]
    d_ref[...] = jnp.concatenate(halves, 1).astype(BF16)


def inner_tables(row0, edges, dt_ref, rate_ref, tab_ref, col_ref, row_ref):
    heads = dt_ref.shape[0]
    total = jnp.zeros((heads, 1), F32)
    for span, first, step, cum, token in steps_of(row0, edges, dt_ref, rate_ref):
        start = doc_start(token, edges)
        since_sub = jnp.exp(cum) * jnp.where((start < first) & (first > row0), 1.0, 0.0)
        since_block = jnp.exp(cum + total) * jnp.where(start < row0, 1.0, 0.0)
        pairs = [part.astype(F32) for part in (*split2(since_block), *split2(since_sub))]
        tab_ref[span, :] = jnp.concatenate(pairs, 0).T.astype(BF16)
        zero = jnp.zeros_like(cum)
        col_ref[span, :] = jnp.concatenate([zero, zero, cum * LOG2E, zero], 0).T
        row_ref[:, span] = (jnp.log(step) - cum) * LOG2E
        total = total + cum[:, SUB - 1 :]


def pack_kernel(x_ref, b_ref, c_ref, out_ref):
    rows = [ref[...].astype(F32)[4:] for ref in (x_ref, b_ref, c_ref)]
    out_ref[...] = jnp.concatenate(rows, 1).astype(BF16)


def pack(x, b, c):
    tiles = x.shape[0] // 8
    widths = [value.shape[1] for value in (x, b, c)]
    return pl.pallas_call(
        pack_kernel,
        out_shape=jax.ShapeDtypeStruct((4, sum(widths)), BF16),
        grid=(1,),
        in_specs=[pl.BlockSpec((8, width), lambda i: (tiles - 1, 0)) for width in widths],
        out_specs=pl.BlockSpec((4, sum(widths)), lambda i: (0, 0)),
        compiler_params=params(16),
        name="pack",
    )(x, b, c)


def place_of(k, owned):
    return pl.multiple_of((lax.axis_index("seq") % CLUSTER ^ k) * owned, owned)


def fill_masks(age_ref, mask_ref):
    for back in range(1, mask_ref.shape[0] + 1):
        mask_ref[back - 1] = jnp.where(age_ref[...] >= back, 1.0, 0.0)


def convolve(ext_ref, mask_ref, taps, emit):
    tok = ext_ref.shape[0] - 8
    repeats = ext_ref.shape[1] // LANES
    for low in range(0, tok, ROWS):
        total = ext_ref[8 + low : 8 + low + ROWS, :] * taps[-1]
        for back in range(1, len(taps)):
            mask = jnp.concatenate([mask_ref[back - 1, low : low + ROWS, :]] * repeats, 1)
            window = ext_ref[8 + low - back : 8 + low - back + ROWS, :]
            total = total + (window * taps[-1 - back]) * mask
        emit(low, total)


def state_of(at, heads, head_dim, bt_ref, tab_ref, d_ref, x_rows, h_put):
    one_hot = spread(0, 2 * heads, at // head_dim, heads, CHUNK, head_dim)
    decay = mm(d_ref[...], one_hot)
    tok = tab_ref.shape[0]
    state = None
    for c in range(tok // SUB):
        rows = slice(c * SUB, (c + 1) * SUB)
        weight = mm(tab_ref[rows, :], one_hot)
        if c == 0:
            head_weight = weight[:8]
        local = mm(bt_ref[:, rows], (x_rows(c) * weight).astype(BF16))
        if state is None:
            state = local
        else:
            h_put(c - 1, state)
            state = local + decay[2 + c : 3 + c, :] * state
    return state, decay, head_weight


def put_piece(send_ref, low, state):
    for tile in range(state.shape[1] // LANES):
        at = low * STATE + tile * STATE
        send_ref[at : at + STATE, :] = state[:, tile * LANES : (tile + 1) * LANES].astype(BF16)


def put_decay(send_ref, decay):
    tiles = decay.shape[1] // LANES
    rows = [decay[:2, tile * LANES : (tile + 1) * LANES] for tile in range(tiles)]
    send_ref[tiles * STATE :, :] = jnp.concatenate(rows, 0).astype(BF16)


def piece_shape(owned):
    return jax.ShapeDtypeStruct((owned // LANES * (STATE + 2), LANES), BF16)


def conv_kernel(
    dl_ref,
    dt_ref,
    rate_ref,
    x_ref,
    b_ref,
    taps_x_ref,
    taps_b_ref,
    tab_ref,
    d_ref,
    age_ref,
    part_x_ref,
    part_b_ref,
    xc_ref,
    bc_ref,
    ext_ref,
    mask_ref,
):
    tok, channels = x_ref.shape
    owned = channels // CLUSTER
    per = owned // CHUNK
    row0 = lax.axis_index("seq") * tok
    edges = doc_edges(dl_ref)
    end_tables(row0, edges, dt_ref, rate_ref, tab_ref, d_ref)
    token = row0 + lax.broadcasted_iota(jnp.int32, (tok, LANES), 0)
    age_ref[...] = token - doc_start(token, edges)
    fill_masks(age_ref, mask_ref)
    ext_ref[:8, :] = jnp.zeros((8, CHUNK), F32)
    taps_len = taps_x_ref.shape[0]

    def body(i, carry):
        k = i // per
        lanes = pl.ds(pl.multiple_of(place_of(k + 1, owned) + (i % per) * CHUNK, CHUNK), CHUNK)
        inner = pl.ds(pl.multiple_of((i % per) * CHUNK, CHUNK), CHUNK)
        ext_ref[8:, :] = x_ref[:, lanes].astype(F32)

        def emit(low, total):
            if low == 0:
                part_x_ref[k, :, inner] = total[:8]
            xc_ref[k, low : low + ROWS, inner] = silu(total).astype(BF16)

        convolve(ext_ref, mask_ref, [taps_x_ref[j : j + 1, lanes] for j in range(taps_len)], emit)
        return carry

    lax.fori_loop(0, EARLY * per, body, 0)
    ext_ref[8:, :] = b_ref[...].astype(F32)

    def emit_b(low, total):
        if low == 0:
            part_b_ref[...] = total[:8]
        bc_ref[low : low + ROWS, :] = silu(total).astype(BF16)

    convolve(ext_ref, mask_ref, [taps_b_ref[j : j + 1, :] for j in range(taps_len)], emit_b)


def conv(doc_lengths, dt_t, rate, x, b, taps_x, taps_b):
    heads = dt_t.shape[0]
    tok, channels = x.shape
    gn = b.shape[1]
    owned = channels // CLUSTER
    shape = jax.ShapeDtypeStruct
    return pl.pallas_call(
        conv_kernel,
        out_shape=(
            shape((tok, 2 * heads), BF16),
            shape((8, 2 * heads), BF16),
            shape((tok, LANES), jnp.int32),
            shape((EARLY, 8, owned), F32),
            shape((8, gn), F32),
            shape((EARLY, tok, owned), BF16),
            shape((tok, gn), BF16),
        ),
        in_specs=[VMEM] * 7,
        out_specs=(VMEM,) * 7,
        scratch_shapes=[
            pltpu.VMEM((tok + 8, CHUNK), F32),
            pltpu.VMEM((taps_x.shape[0] - 1, tok, LANES), F32),
        ],
        compiler_params=params(16),
        cost_estimate=cost(tok * channels * 16, tok * channels * 4, tok * channels),
        name="conv",
    )(doc_lengths, dt_t, rate, x, b, taps_x, taps_b)


def state_kernel(tab_ref, d_ref, xc_ref, bc_ref, s_ref, h_ref, decay_ref, weight_ref, bt_ref):
    pieces, tok, owned = xc_ref.shape
    gn = bc_ref.shape[1]
    channels = owned * CLUSTER
    heads = d_ref.shape[1] // 2
    for group in range(gn // STATE):
        b_blk = bc_ref[:, group * STATE : (group + 1) * STATE].astype(F32)[8:]
        bt_ref[group] = jnp.concatenate([jnp.zeros((8, STATE), F32), b_blk], 0).T.astype(BF16)
    for k in range(pieces):
        at = place_of(k + 1, owned)
        group = at // (channels // (gn // STATE))
        for part in range(owned // CHUNK):
            here = slice(part * CHUNK, (part + 1) * CHUNK)

            def h_put(c, value):
                h_ref[k, c, :, here] = value

            state, decay, weight = state_of(
                at + part * CHUNK,
                heads,
                channels // heads,
                bt_ref.at[group],
                tab_ref,
                d_ref,
                lambda c: xc_ref[k, c * SUB : (c + 1) * SUB, here].astype(F32),
                h_put,
            )
            s_ref[k, :, here] = state
            decay_ref[k, :, here] = decay
            weight_ref[k, :, here] = weight


def states(tab, d, xc, bc):
    pieces, tok, owned = xc.shape
    gn = bc.shape[1]
    row = jax.ShapeDtypeStruct((pieces, 8, owned), F32)
    return pl.pallas_call(
        state_kernel,
        out_shape=(
            jax.ShapeDtypeStruct((pieces, STATE, owned), F32),
            jax.ShapeDtypeStruct((pieces, tok // SUB - 1, STATE, owned), F32),
            row,
            row,
        ),
        in_specs=[VMEM] * 4,
        out_specs=(VMEM,) * 4,
        scratch_shapes=[pltpu.VMEM((gn // STATE, STATE, tok), BF16)],
        compiler_params=params(16),
        cost_estimate=cost(tok * STATE * owned * pieces * 4, tok * owned * pieces * 4),
        name="state",
    )(tab, d, xc, bc)


def head_kernel(
    tail_ref,
    part_x_ref,
    part_b_ref,
    taps_x_ref,
    taps_b_ref,
    age_ref,
    s_ref,
    decay_ref,
    weight_ref,
    xc_in,
    bc_in,
    xc_ref,
    bc_ref,
    extra_ref,
    *rest,
):
    pieces, _, owned = s_ref.shape
    sends = rest[:pieces]
    ext_ref, bt_ref, xw_ref = rest[pieces:]
    gn = bc_in.shape[1]
    channels = owned * CLUSTER
    taps_len = taps_x_ref.shape[0]
    ext_ref[4:8, :] = tail_ref[...].astype(F32)
    ext_ref[8:, :] = jnp.zeros_like(ext_ref[8:, :])

    def head_of(part, lanes, taps, width):
        total = part
        age = jnp.concatenate([age_ref[:8, :]] * (width // LANES), 1)
        for back in range(1, taps_len):
            total = total + jnp.where(age >= back, ext_ref[8 - back : 16 - back, lanes] * taps[-1 - back], 0.0)
        return silu(total).astype(BF16)

    head = head_of(
        part_b_ref[...], slice(channels, channels + gn), [taps_b_ref[j : j + 1, :] for j in range(taps_len)], gn
    )
    bc_ref[:8, :] = head
    for group in range(gn // STATE):
        rows = head[:, group * STATE : (group + 1) * STATE].astype(F32)
        bt_ref[group] = jnp.concatenate([rows, jnp.zeros((LANES - 8, STATE), F32)], 0).T.astype(BF16)
    xw_ref[...] = jnp.zeros_like(xw_ref)
    for k in range(pieces):
        at = place_of(k + 1, owned)
        lanes = pl.ds(at, owned)
        head = head_of(part_x_ref[k], lanes, [taps_x_ref[j : j + 1, lanes] for j in range(taps_len)], owned)
        xc_ref[k, :8, :] = head
        xw_ref[:8, :] = head.astype(F32) * weight_ref[k]
        extra = mm(bt_ref[at // (channels // (gn // STATE))], xw_ref[...].astype(BF16))
        extra_ref[k] = extra
        decay = decay_ref[k]
        rest_of_block = decay[3:4, :]
        for c in range(4, 3 + xc_in.shape[1] // SUB - 1):
            rest_of_block = rest_of_block * decay[c : c + 1, :]
        put_piece(sends[k], 0, s_ref[k] + rest_of_block * extra)
        put_decay(sends[k], decay)


def with_head(tail, part_x, part_b, taps_x, taps_b, age, state, decay, weight, xc, bc):
    pieces, _, owned = xc.shape
    gn = bc.shape[1]
    shape = jax.ShapeDtypeStruct
    return pl.pallas_call(
        head_kernel,
        out_shape=(shape(xc.shape, BF16), shape(bc.shape, BF16), shape(state.shape, F32))
        + (piece_shape(owned),) * pieces,
        in_specs=[VMEM] * 11,
        out_specs=(VMEM,) * (3 + pieces),
        scratch_shapes=[
            pltpu.VMEM((16, tail.shape[1]), F32),
            pltpu.VMEM((gn // STATE, STATE, LANES), BF16),
            pltpu.VMEM((LANES, owned), F32),
        ],
        input_output_aliases={9: 0, 10: 1},
        compiler_params=params(16),
        cost_estimate=cost(STATE * LANES * owned * pieces * 2, STATE * owned * pieces * 10),
        name="head",
    )(tail, part_x, part_b, taps_x, taps_b, age, state, decay, weight, xc, bc)


def late_kernel(k, with_c, *refs):
    tail_ref, age_ref, tab_ref, d_ref, bc_ref, taps_x_ref, x_ref = refs[:7]
    refs = refs[7:]
    if with_c:
        c_ref, taps_c_ref, others_ref, extra_ref, decay_ref, dt_ref, rate_ref, dl_ref = refs[:8]
        cc_ref, early_ref, inner_ref, col_ref, row_ref = refs[8:13]
        refs = refs[13:]
    xc_ref, h_ref, send_ref, bt_ref, ext_ref, mask_ref = refs
    tok, channels = x_ref.shape
    owned = channels // CLUSTER
    gn = bc_ref.shape[1]
    per = owned // CHUNK
    heads = d_ref.shape[1] // 2
    head_dim = channels // heads
    taps_len = taps_x_ref.shape[0]
    at = place_of(k, owned)
    fill_masks(age_ref, mask_ref)
    group = at // (channels // (gn // STATE))
    b_blk = bc_ref[:, pl.ds(pl.multiple_of(group * STATE, STATE), STATE)]
    bt_ref[...] = b_blk.astype(F32).T.astype(BF16)
    if with_c:
        row0 = lax.axis_index("seq") * tok
        inner_tables(row0, doc_edges(dl_ref), dt_ref, rate_ref, inner_ref, col_ref, row_ref)
        for i in range(EARLY):
            extra = extra_ref[i]
            for c in range(tok // SUB - 1):
                if c > 0:
                    extra = extra * decay_ref[i, 2 + c : 3 + c, :]
                early_ref[i, c] = (others_ref[i, c] + extra).astype(BF16)
    decays = []
    for part in range(per + with_c):
        here = slice(part * CHUNK, (part + 1) * CHUNK)
        if part < per:
            lanes = pl.ds(pl.multiple_of(at + part * CHUNK, CHUNK), CHUNK)
            taps = [taps_x_ref[j : j + 1, lanes] for j in range(taps_len)]
        else:
            lanes = slice(channels + gn, channels + 2 * gn)
            taps = [taps_c_ref[j : j + 1, :] for j in range(taps_len)]
        ext_ref[4:8, :] = tail_ref[:, lanes].astype(F32)
        ext_ref[8:, :] = (x_ref[:, lanes] if part < per else c_ref[...]).astype(F32)

        def emit(low, total):
            value = silu(total).astype(BF16)
            if part < per:
                xc_ref[0, low : low + ROWS, here] = value
            else:
                cc_ref[low : low + ROWS, :] = value

        convolve(ext_ref, mask_ref, taps, emit)
        if part < per:

            def h_put(c, value):
                h_ref[0, c, :, here] = value.astype(BF16)

            state, decay, _ = state_of(
                at + part * CHUNK,
                heads,
                head_dim,
                bt_ref,
                tab_ref,
                d_ref,
                lambda c: xc_ref[0, c * SUB : (c + 1) * SUB, here].astype(F32),
                h_put,
            )
            put_piece(send_ref, part * (CHUNK // LANES), state)
            decays.append(decay)
    put_decay(send_ref, jnp.concatenate(decays, 1))


def late(k, tail, age, tab, d, bc, taps_x, x, with_c=()):
    tok, channels = x.shape
    owned = channels // CLUSTER
    gn = bc.shape[1]
    subs = tok // SUB - 1
    shape = jax.ShapeDtypeStruct
    heads = d.shape[1] // 2
    extra_out = (
        shape((tok, gn), BF16),
        shape((EARLY, subs, STATE, owned), BF16),
        shape((tok, LANES), BF16),
        shape((tok, LANES), F32),
        shape((heads, tok), F32),
    )
    if not with_c:
        extra_out = ()
    return pl.pallas_call(
        functools.partial(late_kernel, k, bool(with_c)),
        out_shape=(
            *extra_out,
            shape((1, tok, owned), BF16),
            shape((1, subs, STATE, owned), BF16),
            piece_shape(owned),
        ),
        in_specs=[VMEM] * (7 + len(with_c)),
        out_specs=(VMEM,) * (3 + len(extra_out)),
        scratch_shapes=[
            pltpu.VMEM((STATE, tok), BF16),
            pltpu.VMEM((tok + 8, CHUNK), F32),
            pltpu.VMEM((taps_x.shape[0] - 1, tok, LANES), F32),
        ],
        compiler_params=params(16),
        cost_estimate=cost(tok * owned * 16 + tok * STATE * owned * 4, tok * owned * 8, tok * owned),
        name="own" if with_c else "late",
    )(tail, age, tab, d, bc, taps_x, x, *with_c)


def collect_kernel(*refs):
    *pieces, out_ref = refs
    for k, ref in enumerate(pieces):
        out_ref[k] = ref[...]


def collect(pieces):
    return pl.pallas_call(
        collect_kernel,
        out_shape=jax.ShapeDtypeStruct((len(pieces), *pieces[0].shape), BF16),
        in_specs=[VMEM] * len(pieces),
        out_specs=VMEM,
        compiler_params=params(16),
        cost_estimate=cost(0, 4 * len(pieces) * pieces[0].size),
        name="collect",
    )(*pieces)


def scan_kernel(*refs):
    first_ref, *last, local_ref, pre_ref, total_ref = refs
    pieces = [first_ref.at[k] for k in range(first_ref.shape[0])] + last
    mine = lax.axis_index("seq") % CLUSTER

    def in_order(values):
        bit = 1
        while bit < CLUSTER:
            odd = (mine & bit) != 0
            values = [jnp.where(odd, values[i ^ bit], values[i]) for i in range(CLUSTER)]
            bit *= 2
        return values

    owned = total_ref.shape[1]
    tiles = owned // LANES
    rows = [ref[tiles * STATE :, :].astype(F32) for ref in pieces]
    decays = in_order(
        [jnp.concatenate([row[2 * t : 2 * t + 1] + row[2 * t + 1 : 2 * t + 2] for t in range(tiles)], 1) for row in rows]
    )
    pre = jnp.ones((1, owned), F32)
    for i in range(CLUSTER):
        pre_ref[i] = jnp.broadcast_to(pre, (8, owned))
        pre = pre * decays[i]
    pre_ref[CLUSTER] = jnp.broadcast_to(pre, (8, owned))
    for at in range(0, owned, LANES):
        lanes = slice(at, at + LANES)
        for low in range(0, STATE, 64):
            rows = slice(low, low + 64)
            at_rows = slice(at + low, at + low + 64)
            values = in_order([ref[at_rows, :].astype(F32) for ref in pieces])
            local_ref[0, rows, lanes] = jnp.zeros((64, LANES), F32)
            state = values[0]
            for i in range(1, CLUSTER):
                local_ref[i, rows, lanes] = state
                state = decays[i][:, lanes] * state + values[i]
            total_ref[rows, lanes] = state.astype(BF16)


def scan_blocks(pieces):
    operands = (collect(pieces[: 1 + EARLY]), *pieces[1 + EARLY :])
    owned = pieces[0].shape[0] // (STATE + 2) * LANES
    return pl.pallas_call(
        scan_kernel,
        out_shape=(
            jax.ShapeDtypeStruct((CLUSTER, STATE, owned), F32),
            jax.ShapeDtypeStruct((CLUSTER + 1, 8, owned), F32),
            jax.ShapeDtypeStruct((STATE, owned), BF16),
        ),
        in_specs=[VMEM] * len(operands),
        out_specs=(VMEM,) * 3,
        compiler_params=params(),
        cost_estimate=cost(CLUSTER * STATE * owned * 2, CLUSTER * STATE * owned * 6),
        name="cluster_scan",
    )(*operands)


def join_kernel(before_ref, local_ref, pre_ref, *outs):
    index = lax.axis_index("seq")
    mine = index % CLUSTER
    before = jnp.where(index >= CLUSTER, before_ref[...].astype(F32), 0.0)
    for k in range(CLUSTER):
        block = mine ^ k
        outs[k][...] = (local_ref[block] + pre_ref[block][0:1] * before).astype(BF16)


def join(before, local, pre):
    owned = local.shape[2]
    return pl.pallas_call(
        join_kernel,
        out_shape=(jax.ShapeDtypeStruct((STATE, owned), BF16),) * CLUSTER,
        in_specs=[VMEM] * 3,
        out_specs=(VMEM,) * CLUSTER,
        compiler_params=params(),
        cost_estimate=cost(CLUSTER * STATE * owned * 2, CLUSTER * STATE * owned * 6),
        name="join",
    )(before, local, pre)


def group_at(turn, groups):
    return (lax.axis_index("seq") % CLUSTER) // (CLUSTER // groups) ^ turn


def intra_kernel(pieces, heads, head_dim, *refs):
    bc_ref, cc_ref, tab_ref, col_ref, row_ref, age_ref = refs[:6]
    refs = refs[6:]
    count = len(pieces)
    xs, hs, gates, parts, scales = (refs[i * count : (i + 1) * count] for i in range(5))
    hot_ref, hot0_ref = refs[5 * count :]
    owned = parts[0].shape[1]
    per_piece = owned // head_dim
    mine = lax.axis_index("seq") % CLUSTER

    @pl.when(pl.program_id(0) == 0)
    def _():
        for p, k in enumerate(pieces):
            hot_ref[p] = spread(2 * heads, 4 * heads, (mine ^ k) * per_piece, heads, owned, head_dim)
            hot0_ref[p] = spread(0, 2 * heads, (mine ^ k) * per_piece, heads, owned, head_dim)

    back = lax.broadcasted_iota(jnp.int32, (SUB, SUB), 0) - lax.broadcasted_iota(jnp.int32, (SUB, SUB), 1)
    keep = (back >= 0) & (back <= age_ref[...])
    c_blk = cc_ref[...]
    scores = lax.dot_general(c_blk, bc_ref[...], (((1,), (1,)), ((), ())), preferred_element_type=F32)
    scores = jnp.where(keep, scores, 0.0)
    lane = lax.broadcasted_iota(jnp.int32, (SUB, LANES), 1)
    per_tile = LANES // head_dim
    for p, k in enumerate(pieces):
        first = (mine ^ k) * per_piece
        col = pltpu.roll(col_ref[...], LANES - (2 * heads + first), 1)
        row = row_ref[pl.ds(pl.multiple_of(first, per_piece), per_piece), :]
        for tile in range(owned // LANES):
            lanes = slice(tile * LANES, (tile + 1) * LANES)
            x_tile = xs[p][0, :, lanes].astype(F32)
            left, right = [], []
            for i in range(per_tile):
                head = tile * per_tile + i
                gap = col[:, head : head + 1] + row[head : head + 1, :]
                left.append((jnp.exp2(jnp.minimum(gap, 80.0)) * scores).astype(BF16))
                here = (lane >= i * head_dim) & (lane < (i + 1) * head_dim)
                right.append(jnp.where(here, x_tile, 0.0).astype(BF16))
            inner = mm(jnp.concatenate(left, 1), jnp.concatenate(right, 0))
            inner = inner + mm(c_blk, hs[p][0, 0, :, lanes]) * mm(tab_ref[...], hot_ref[p, :, lanes])
            gate = silu(gates[p][:, lanes].astype(F32))
            parts[p][:, lanes] = inner * gate
            scales[p][:, lanes] = mm(tab_ref[:, : 2 * heads], hot0_ref[p, :, lanes]) * gate


def early_index(k):
    return k - 1 if 1 <= k <= EARLY else 0


def intra(turn, pieces, bc, cc, tab, col, row, age, xs, hs, gate):
    tok, gn = bc.shape
    heads = row.shape[0]
    channels = gate.shape[1]
    head_dim = channels // heads
    groups = gn // STATE
    owned = channels // CLUSTER
    count = len(pieces)
    out = jax.ShapeDtypeStruct((tok, owned), F32)

    def piece_spec(block, index):
        return [pl.BlockSpec(block, functools.partial(index, k)) for k in pieces]

    return pl.pallas_call(
        functools.partial(intra_kernel, pieces, heads, head_dim),
        out_shape=(out,) * (2 * count),
        grid=(tok // SUB,),
        in_specs=[
            pl.BlockSpec((SUB, STATE), lambda i: (i, group_at(turn, groups))),
            pl.BlockSpec((SUB, STATE), lambda i: (i, group_at(turn, groups))),
            pl.BlockSpec((SUB, tab.shape[1]), lambda i: (i, 0)),
            pl.BlockSpec((SUB, LANES), lambda i: (i, 0)),
            pl.BlockSpec((heads, SUB), lambda i: (0, i)),
            pl.BlockSpec((SUB, LANES), lambda i: (i, 0)),
        ]
        + piece_spec((1, SUB, owned), lambda k, i: (early_index(k), i, 0))
        + piece_spec((1, 1, STATE, owned), lambda k, i: (early_index(k), jnp.maximum(i - 1, 0), 0, 0))
        + piece_spec((SUB, owned), lambda k, i: (i, lax.axis_index("seq") % CLUSTER ^ k)),
        out_specs=(pl.BlockSpec((SUB, owned), lambda i: (i, 0)),) * (2 * count),
        scratch_shapes=[pltpu.VMEM((count, 4 * heads, owned), BF16), pltpu.VMEM((count, 2 * heads, owned), BF16)],
        compiler_params=params(16),
        cost_estimate=cost(tok * SUB * owned * count * 4, tok * owned * count * 12, tok * SUB * owned * count // head_dim),
        name="intra",
    )(bc, cc, tab, col, row, age, *xs, *hs, *([gate] * count))


def final_kernel(turn, groups, *refs):
    cc_ref, gain_ref = refs[:2]
    share = CLUSTER // groups
    parts, scales, pieces = (refs[2 + i * share : 2 + (i + 1) * share] for i in range(3))
    out_hbm, y_ref, put_ref, sem = refs[-4:]
    tok, owned = parts[0].shape
    rows = y_ref.shape[1]
    copies = []
    c_lanes = pl.ds(pl.multiple_of(group_at(turn, groups) * STATE, STATE), STATE)
    columns = [pl.ds(place_of(turn * share + i, owned), owned) for i in range(share)]
    for low in range(0, tok, rows):
        span = slice(low, low + rows)
        c_blk = cc_ref[span, c_lanes]
        squares = None
        for i in range(share):
            for at in range(0, owned, CHUNK):
                lanes = slice(at, at + CHUNK)
                value = parts[i][span, lanes] + mm(c_blk, pieces[i][:, lanes]) * scales[i][span, lanes]
                y_ref[i, :, lanes] = value
                square = value * value
                for j in range(0, CHUNK, LANES):
                    piece = square[:, j : j + LANES]
                    squares = piece if squares is None else squares + piece
        factor = lax.rsqrt(jnp.sum(squares, axis=1, keepdims=True) * (1.0 / (share * owned)) + norm_eps)
        for i in range(share):
            put_ref[i, span, :] = (y_ref[i] * factor * gain_ref[:, columns[i]]).astype(BF16)
            copies.append(
                pltpu.make_async_copy(put_ref.at[i, span, :], out_hbm.at[span, columns[i]], sem.at[i, low // rows])
            )
            copies[-1].start()
    wait_all(copies)


def final(turn, cc, gain, parts, scales, pieces, so_far):
    tok, owned = parts[0].shape
    groups = cc.shape[1] // STATE
    share = CLUSTER // groups
    rows = 64
    operands = (cc, gain, *parts, *scales, *pieces) + (() if so_far is None else (so_far,))
    return pl.pallas_call(
        functools.partial(final_kernel, turn, groups),
        out_shape=jax.ShapeDtypeStruct((tok, owned * CLUSTER), BF16),
        in_specs=[VMEM] * (2 + 3 * share) + ([] if so_far is None else [ANY]),
        out_specs=ANY,
        scratch_shapes=[
            pltpu.VMEM((share, rows, owned), F32),
            pltpu.VMEM((share, tok, owned), BF16),
            pltpu.SemaphoreType.DMA((share, tok // rows)),
        ],
        input_output_aliases={} if so_far is None else {len(operands) - 1: 0},
        compiler_params=params(16),
        cost_estimate=cost(tok * STATE * owned * share * 2, tok * owned * share * 8),
        name="final",
    )(*operands)


def moved(value, hop):
    count = lax.axis_size("seq")
    return lax.ppermute(value, "seq", [(i, hop(i)) for i in range(count) if 0 <= hop(i) < count])


def exchanged(pieces, order):
    arrived = {0: pieces[0]}
    for k in order:
        arrived[k] = moved(pieces[k], lambda i, k=k: i ^ k)
    return [arrived[k] for k in range(CLUSTER)]


def before_cluster(total, pre):
    clusters = lax.axis_size("seq") // CLUSTER
    if clusters == 1:
        return jnp.zeros_like(total)
    if clusters == 2:
        return moved(total, lambda i: i ^ CLUSTER)
    shift = lambda value, steps: moved(value, lambda i: i + steps * CLUSTER)
    state, decay = shift((total.astype(F32), pre[CLUSTER, 0]), 1)
    step = 1
    while step < clusters - 1:
        earlier, fell = shift((state, decay), step)
        state, decay = state + decay[None, :] * earlier, decay * fell
        step *= 2
    return state


def tied(values, other):
    *values, _ = lax.optimization_barrier((*values, other))
    return values


def on_device(
    x_input,
    b_input,
    c_input,
    dt_input,
    decay_rate,
    gate_input,
    taps_x,
    taps_b,
    taps_c,
    norm_gain,
    doc_lengths,
):
    groups = b_input.shape[1] // STATE
    count = lax.axis_size("seq")
    pin = lambda value: pltpu.with_memory_space_constraint(value, pltpu.HBM)
    ends = pack(pin(x_input), pin(b_input), pin(c_input))
    tail = lax.ppermute(ends, "seq", [(i, (i + 1) % count) for i in range(count)])
    rates = (dt_input.T, decay_rate[None, :])
    lengths = doc_lengths[None, :]
    tab, d, age, part_x, part_b, xc, bc = conv(lengths, *rates, x_input, b_input, taps_x, taps_b)
    state, others, decay, weight = states(tab, d, xc, bc)
    xc, bc, extra, *sends = with_head(tail, part_x, part_b, taps_x, taps_b, age, state, decay, weight, xc, bc)
    known = (tail, age, tab, d, bc, taps_x, x_input)
    xs, hs = [None] + [xc] * EARLY, [None] * (1 + EARLY)
    for k in range(1 + EARLY, CLUSTER):
        late_x, late_h, late_send = late(k, *known)
        xs.append(late_x)
        hs.append(late_h)
        sends.append(late_send)
    cc, early_h, inner_tab, col, row, xs[0], hs[0], own_send = late(
        0, *known, (c_input, taps_c, others, extra, decay, *rates, lengths)
    )
    hs[1 : 1 + EARLY] = [early_h] * EARLY
    shared = (bc, cc, inner_tab, col, row)
    share = CLUSTER // groups

    def inner(turn, age):
        pieces = tuple(range(turn * share, (turn + 1) * share))
        return intra(turn, pieces, *shared, age, [xs[k] for k in pieces], [hs[k] for k in pieces], gate_input)

    local, pre, total = scan_blocks(exchanged([own_send, *sends], (1, 2, 3)))
    first = inner(0, *tied([age], total))
    joined = join(*tied([before_cluster(total, pre)], first[0]), local, pre)
    later = [inner(turn, *tied([age], joined[0])) for turn in range(1, groups)]
    entering = exchanged(joined, (1, 2, 3))
    output = None
    for turn, found in enumerate((first, *later)):
        mine = entering[turn * share : (turn + 1) * share]
        output = final(turn, cc, norm_gain[None, :], found[:share], found[share:], mine, output)
    return output


def solution(mesh):
    rows = P(("groups", "seq"), "dp")
    placed = (rows, rows, rows, rows, P("dp"), rows, P(None, "dp"), P(None, "dp"), P(None, "dp"), P("dp"), P("groups"))
    return jax.shard_map(on_device, mesh=mesh, in_specs=placed, out_specs=rows, check_vma=False)
```

```python
import functools

import jax
import jax.numpy as jnp
from jax import lax
from jax.experimental import pallas as pl
from jax.experimental.pallas import tpu as pltpu
from jax.sharding import PartitionSpec as P

STATE = 128
SUB = 128
CHUNK = 256
LANES = 128
ROWS = 32
CLUSTER = 4
EARLY = 2
LOG2E = 1.4426950408889634
norm_eps = 1e-05

F32 = jnp.float32
BF16 = jnp.bfloat16
VMEM = pl.BlockSpec(memory_space=pltpu.VMEM)
ANY = pl.BlockSpec(memory_space=pl.ANY)
HBM = pl.BlockSpec(memory_space=pltpu.HBM)


def params(mib=24):
    return pltpu.CompilerParams(vmem_limit_bytes=mib << 20)


def cost(flops, moved, transcendentals=0):
    return pl.CostEstimate(flops=flops, bytes_accessed=moved, transcendentals=transcendentals)


def doc_edges(dl_ref):
    edges = [0]
    for i in range(dl_ref.shape[0] - 1):
        edges.append(edges[-1] + dl_ref[i])
    return edges


def doc_start(token, edges):
    start = jnp.zeros_like(token)
    for edge in edges[1:]:
        start = jnp.where(token >= edge, jnp.maximum(start, edge), start)
    return start


def split2(value):
    high = value.astype(BF16)
    return high, (value - high.astype(F32)).astype(BF16)


def split3(value):
    high = value.astype(BF16)
    rest = value - high.astype(F32)
    mid = rest.astype(BF16)
    return high, mid, (rest - mid.astype(F32)).astype(BF16)


def mm(a, b):
    return jnp.dot(a, b, preferred_element_type=F32)


def silu(value):
    half = 0.5 * value
    return half + half * jnp.tanh(half)


def spread(base, rows, first_head, heads, width, head_dim):
    row = lax.broadcasted_iota(jnp.int32, (rows, width), 0) - (base + first_head)
    head = lax.broadcasted_iota(jnp.int32, (rows, width), 1) // head_dim
    return jnp.where((row == head) | (row == head + heads), 1.0, 0.0).astype(BF16)


def start_all(copies):
    for copy in copies:
        copy.start()


def wait_all(copies):
    for copy in copies:
        copy.wait()


def steps_of(row0, edges, dt_ref, rate_ref):
    heads, tok = dt_ref.shape
    upto = jnp.where(
        lax.broadcasted_iota(jnp.int32, (SUB, SUB), 0) <= lax.broadcasted_iota(jnp.int32, (SUB, SUB), 1), 1.0, 0.0
    ).astype(BF16)
    rate = jnp.concatenate([rate_ref[...], jnp.zeros((1, LANES - heads), F32)], 1)
    rate = jnp.broadcast_to(rate, (LANES, LANES)).T[:heads]
    found = []
    for c in range(tok // SUB):
        span = slice(c * SUB, (c + 1) * SUB)
        dt = dt_ref[:, span]
        step = jnp.maximum(dt, 0.0) + jnp.log1p(jnp.exp(-jnp.abs(dt)))
        parts = split3(-(step * rate))
        cum = mm(parts[0], upto) + (mm(parts[1], upto) + mm(parts[2], upto))
        token = row0 + c * SUB + lax.broadcasted_iota(jnp.int32, (heads, SUB), 1)
        found.append((span, row0 + c * SUB, step, cum, token))
    return found


def end_tables(row0, edges, dt_ref, rate_ref, tab_ref, d_ref):
    heads, tok = dt_ref.shape
    total = jnp.zeros((heads, 1), F32)
    decays = []
    for span, first, step, cum, token in steps_of(row0, edges, dt_ref, rate_ref):
        last = cum[:, SUB - 1 :]
        last_start = doc_start(jnp.int32(first + SUB - 1), edges)
        to_end = jnp.exp(last - cum) * step * jnp.where(token >= last_start, 1.0, 0.0)
        pair = [part.astype(F32) for part in split2(to_end)] + [jnp.zeros((LANES - 2 * heads, SUB), F32)]
        tab_ref[span, :] = jnp.concatenate(pair, 0).T[:, : 2 * heads].astype(BF16)
        decays.append(jnp.exp(last) * jnp.where(last_start < first, 1.0, 0.0))
        total = total + last
    end_start = doc_start(jnp.int32(row0 + tok - 1), edges)
    whole = jnp.exp(total) * jnp.where(end_start < row0, 1.0, 0.0)
    columns = [part.astype(F32) for part in split3(whole)] + decays[1:]
    columns.append(jnp.zeros((heads, LANES - len(columns)), F32))
    columns = jnp.concatenate([jnp.concatenate(columns, 1), jnp.zeros((LANES - heads, LANES), F32)], 0)
    halves = [part.astype(F32)[:, :heads] for part in split2(columns.T[:8])]
    d_ref[...] = jnp.concatenate(halves, 1).astype(BF16)


def inner_tables(row0, edges, dt_ref, rate_ref, tab_ref, col_ref, row_ref):
    heads = dt_ref.shape[0]
    total = jnp.zeros((heads, 1), F32)
    for span, first, step, cum, token in steps_of(row0, edges, dt_ref, rate_ref):
        start = doc_start(token, edges)
        since_sub = jnp.exp(cum) * jnp.where((start < first) & (first > row0), 1.0, 0.0)
        since_block = jnp.exp(cum + total) * jnp.where(start < row0, 1.0, 0.0)
        pairs = [part.astype(F32) for part in (*split2(since_block), *split2(since_sub))]
        tab_ref[span, :] = jnp.concatenate(pairs, 0).T.astype(BF16)
        zero = jnp.zeros_like(cum)
        col_ref[span, :] = jnp.concatenate([zero, zero, cum * LOG2E, zero], 0).T
        row_ref[:, span] = (jnp.log(step) - cum) * LOG2E
        total = total + cum[:, SUB - 1 :]


def pack_kernel(x_ref, b_ref, c_ref, out_ref):
    rows = [ref[...].astype(F32)[4:] for ref in (x_ref, b_ref, c_ref)]
    out_ref[...] = jnp.concatenate(rows, 1).astype(BF16)


def pack(x, b, c):
    tiles = x.shape[0] // 8
    widths = [value.shape[1] for value in (x, b, c)]
    return pl.pallas_call(
        pack_kernel,
        out_shape=jax.ShapeDtypeStruct((4, sum(widths)), BF16),
        grid=(1,),
        in_specs=[pl.BlockSpec((8, width), lambda i: (tiles - 1, 0)) for width in widths],
        out_specs=pl.BlockSpec((4, sum(widths)), lambda i: (0, 0)),
        compiler_params=params(16),
        name="pack",
    )(x, b, c)


def place_of(k, owned):
    return pl.multiple_of((lax.axis_index("seq") % CLUSTER ^ k) * owned, owned)


def fill_masks(age_ref, mask_ref):
    for back in range(1, mask_ref.shape[0] + 1):
        mask_ref[back - 1] = jnp.where(age_ref[...] >= back, 1.0, 0.0)


def convolve(ext_ref, mask_ref, taps, emit):
    tok = ext_ref.shape[0] - 8
    repeats = ext_ref.shape[1] // LANES
    for low in range(0, tok, ROWS):
        total = ext_ref[8 + low : 8 + low + ROWS, :] * taps[-1]
        for back in range(1, len(taps)):
            mask = jnp.concatenate([mask_ref[back - 1, low : low + ROWS, :]] * repeats, 1)
            window = ext_ref[8 + low - back : 8 + low - back + ROWS, :]
            total = total + (window * taps[-1 - back]) * mask
        emit(low, total)


def state_of(at, heads, head_dim, bt_ref, tab_ref, d_ref, x_rows, h_put):
    one_hot = spread(0, 2 * heads, at // head_dim, heads, CHUNK, head_dim)
    decay = mm(d_ref[...], one_hot)
    tok = tab_ref.shape[0]
    state = None
    for c in range(tok // SUB):
        rows = slice(c * SUB, (c + 1) * SUB)
        weight = mm(tab_ref[rows, :], one_hot)
        if c == 0:
            head_weight = weight[:8]
        local = mm(bt_ref[:, rows], (x_rows(c) * weight).astype(BF16))
        if state is None:
            state = local
        else:
            h_put(c - 1, state)
            state = local + decay[2 + c : 3 + c, :] * state
    return state, decay, head_weight


def put_piece(send_ref, low, state):
    for tile in range(state.shape[1] // LANES):
        at = low * STATE + tile * STATE
        send_ref[at : at + STATE, :] = state[:, tile * LANES : (tile + 1) * LANES].astype(BF16)


def put_decay(send_ref, decay):
    tiles = decay.shape[1] // LANES
    rows = [decay[:2, tile * LANES : (tile + 1) * LANES] for tile in range(tiles)]
    send_ref[tiles * STATE :, :] = jnp.concatenate(rows, 0).astype(BF16)


def piece_shape(owned):
    return jax.ShapeDtypeStruct((owned // LANES * (STATE + 2), LANES), BF16)


def conv_kernel(
    dl_ref,
    dt_ref,
    rate_ref,
    x_ref,
    b_ref,
    taps_x_ref,
    taps_b_ref,
    tab_ref,
    d_ref,
    age_ref,
    part_x_ref,
    part_b_ref,
    xc_ref,
    bc_ref,
    ext_ref,
    mask_ref,
):
    tok, channels = x_ref.shape
    owned = channels // CLUSTER
    per = owned // CHUNK
    row0 = lax.axis_index("seq") * tok
    edges = doc_edges(dl_ref)
    end_tables(row0, edges, dt_ref, rate_ref, tab_ref, d_ref)
    token = row0 + lax.broadcasted_iota(jnp.int32, (tok, LANES), 0)
    age_ref[...] = token - doc_start(token, edges)
    fill_masks(age_ref, mask_ref)
    ext_ref[:8, :] = jnp.zeros((8, CHUNK), F32)
    taps_len = taps_x_ref.shape[0]

    def body(i, carry):
        k = i // per
        lanes = pl.ds(pl.multiple_of(place_of(k + 1, owned) + (i % per) * CHUNK, CHUNK), CHUNK)
        inner = pl.ds(pl.multiple_of((i % per) * CHUNK, CHUNK), CHUNK)
        ext_ref[8:, :] = x_ref[:, lanes].astype(F32)

        def emit(low, total):
            if low == 0:
                part_x_ref[k, :, inner] = total[:8]
            xc_ref[k, low : low + ROWS, inner] = silu(total).astype(BF16)

        convolve(ext_ref, mask_ref, [taps_x_ref[j : j + 1, lanes] for j in range(taps_len)], emit)
        return carry

    lax.fori_loop(0, EARLY * per, body, 0)
    ext_ref[8:, :] = b_ref[...].astype(F32)

    def emit_b(low, total):
        if low == 0:
            part_b_ref[...] = total[:8]
        bc_ref[low : low + ROWS, :] = silu(total).astype(BF16)

    convolve(ext_ref, mask_ref, [taps_b_ref[j : j + 1, :] for j in range(taps_len)], emit_b)


def conv(doc_lengths, dt_t, rate, x, b, taps_x, taps_b):
    heads = dt_t.shape[0]
    tok, channels = x.shape
    gn = b.shape[1]
    owned = channels // CLUSTER
    shape = jax.ShapeDtypeStruct
    return pl.pallas_call(
        conv_kernel,
        out_shape=(
            shape((tok, 2 * heads), BF16),
            shape((8, 2 * heads), BF16),
            shape((tok, LANES), jnp.int32),
            shape((EARLY, 8, owned), F32),
            shape((8, gn), F32),
            shape((EARLY, tok, owned), BF16),
            shape((tok, gn), BF16),
        ),
        in_specs=[pl.BlockSpec(memory_space=pltpu.SMEM)] + [VMEM] * 6,
        out_specs=(VMEM,) * 7,
        scratch_shapes=[
            pltpu.VMEM((tok + 8, CHUNK), F32),
            pltpu.VMEM((taps_x.shape[0] - 1, tok, LANES), F32),
        ],
        compiler_params=params(16),
        cost_estimate=cost(tok * channels * 16, tok * channels * 4, tok * channels),
        name="conv",
    )(doc_lengths, dt_t, rate, x, b, taps_x, taps_b)


def state_kernel(tab_ref, d_ref, xc_ref, bc_ref, s_ref, h_ref, decay_ref, weight_ref, bt_ref):
    pieces, tok, owned = xc_ref.shape
    gn = bc_ref.shape[1]
    channels = owned * CLUSTER
    heads = d_ref.shape[1] // 2
    for group in range(gn // STATE):
        b_blk = bc_ref[:, group * STATE : (group + 1) * STATE].astype(F32)[8:]
        bt_ref[group] = jnp.concatenate([jnp.zeros((8, STATE), F32), b_blk], 0).T.astype(BF16)
    for k in range(pieces):
        at = place_of(k + 1, owned)
        group = at // (channels // (gn // STATE))
        for part in range(owned // CHUNK):
            here = slice(part * CHUNK, (part + 1) * CHUNK)

            def h_put(c, value):
                h_ref[k, c, :, here] = value

            state, decay, weight = state_of(
                at + part * CHUNK,
                heads,
                channels // heads,
                bt_ref.at[group],
                tab_ref,
                d_ref,
                lambda c: xc_ref[k, c * SUB : (c + 1) * SUB, here].astype(F32),
                h_put,
            )
            s_ref[k, :, here] = state
            decay_ref[k, :, here] = decay
            weight_ref[k, :, here] = weight


def states(tab, d, xc, bc):
    pieces, tok, owned = xc.shape
    gn = bc.shape[1]
    row = jax.ShapeDtypeStruct((pieces, 8, owned), F32)
    return pl.pallas_call(
        state_kernel,
        out_shape=(
            jax.ShapeDtypeStruct((pieces, STATE, owned), F32),
            jax.ShapeDtypeStruct((pieces, tok // SUB - 1, STATE, owned), F32),
            row,
            row,
        ),
        in_specs=[VMEM] * 4,
        out_specs=(VMEM,) * 4,
        scratch_shapes=[pltpu.VMEM((gn // STATE, STATE, tok), BF16)],
        compiler_params=params(16),
        cost_estimate=cost(tok * STATE * owned * pieces * 4, tok * owned * pieces * 4),
        name="state",
    )(tab, d, xc, bc)


def head_kernel(
    tail_ref,
    part_x_ref,
    part_b_ref,
    taps_x_ref,
    taps_b_ref,
    age_ref,
    s_ref,
    decay_ref,
    weight_ref,
    xc_in,
    bc_in,
    xc_ref,
    bc_ref,
    extra_ref,
    *rest,
):
    pieces, _, owned = s_ref.shape
    sends = rest[:pieces]
    ext_ref, bt_ref, xw_ref = rest[pieces:]
    gn = bc_in.shape[1]
    channels = owned * CLUSTER
    taps_len = taps_x_ref.shape[0]
    ext_ref[4:8, :] = tail_ref[...].astype(F32)
    ext_ref[8:, :] = jnp.zeros_like(ext_ref[8:, :])

    def head_of(part, lanes, taps, width):
        total = part
        age = jnp.concatenate([age_ref[:8, :]] * (width // LANES), 1)
        for back in range(1, taps_len):
            total = total + jnp.where(age >= back, ext_ref[8 - back : 16 - back, lanes] * taps[-1 - back], 0.0)
        return silu(total).astype(BF16)

    head = head_of(
        part_b_ref[...], slice(channels, channels + gn), [taps_b_ref[j : j + 1, :] for j in range(taps_len)], gn
    )
    bc_ref[:8, :] = head
    for group in range(gn // STATE):
        rows = head[:, group * STATE : (group + 1) * STATE].astype(F32)
        bt_ref[group] = jnp.concatenate([rows, jnp.zeros((LANES - 8, STATE), F32)], 0).T.astype(BF16)
    xw_ref[...] = jnp.zeros_like(xw_ref)
    for k in range(pieces):
        at = place_of(k + 1, owned)
        lanes = pl.ds(at, owned)
        head = head_of(part_x_ref[k], lanes, [taps_x_ref[j : j + 1, lanes] for j in range(taps_len)], owned)
        xc_ref[k, :8, :] = head
        xw_ref[:8, :] = head.astype(F32) * weight_ref[k]
        extra = mm(bt_ref[at // (channels // (gn // STATE))], xw_ref[...].astype(BF16))
        extra_ref[k] = extra
        decay = decay_ref[k]
        rest_of_block = decay[3:4, :]
        for c in range(4, 3 + xc_in.shape[1] // SUB - 1):
            rest_of_block = rest_of_block * decay[c : c + 1, :]
        put_piece(sends[k], 0, s_ref[k] + rest_of_block * extra)
        put_decay(sends[k], decay)


def with_head(tail, part_x, part_b, taps_x, taps_b, age, state, decay, weight, xc, bc):
    pieces, _, owned = xc.shape
    gn = bc.shape[1]
    shape = jax.ShapeDtypeStruct
    return pl.pallas_call(
        head_kernel,
        out_shape=(shape(xc.shape, BF16), shape(bc.shape, BF16), shape(state.shape, F32))
        + (piece_shape(owned),) * pieces,
        in_specs=[VMEM] * 11,
        out_specs=(VMEM,) * (3 + pieces),
        scratch_shapes=[
            pltpu.VMEM((16, tail.shape[1]), F32),
            pltpu.VMEM((gn // STATE, STATE, LANES), BF16),
            pltpu.VMEM((LANES, owned), F32),
        ],
        input_output_aliases={9: 0, 10: 1},
        compiler_params=params(16),
        cost_estimate=cost(STATE * LANES * owned * pieces * 2, STATE * owned * pieces * 10),
        name="head",
    )(tail, part_x, part_b, taps_x, taps_b, age, state, decay, weight, xc, bc)


def late_kernel(k, with_c, *refs):
    tail_ref, age_ref, tab_ref, d_ref, bc_ref, taps_x_ref, x_ref = refs[:7]
    refs = refs[7:]
    if with_c:
        c_ref, taps_c_ref, others_ref, extra_ref, decay_ref, dt_ref, rate_ref, dl_ref = refs[:8]
        cc_ref, early_ref, inner_ref, col_ref, row_ref = refs[8:13]
        refs = refs[13:]
    xc_ref, h_ref, send_ref, bt_ref, ext_ref, mask_ref = refs
    tok, channels = x_ref.shape
    owned = channels // CLUSTER
    gn = bc_ref.shape[1]
    per = owned // CHUNK
    heads = d_ref.shape[1] // 2
    head_dim = channels // heads
    taps_len = taps_x_ref.shape[0]
    at = place_of(k, owned)
    fill_masks(age_ref, mask_ref)
    group = at // (channels // (gn // STATE))
    b_blk = bc_ref[:, pl.ds(pl.multiple_of(group * STATE, STATE), STATE)]
    bt_ref[...] = b_blk.astype(F32).T.astype(BF16)
    if with_c:
        row0 = lax.axis_index("seq") * tok
        inner_tables(row0, doc_edges(dl_ref), dt_ref, rate_ref, inner_ref, col_ref, row_ref)
        for i in range(EARLY):
            extra = extra_ref[i]
            for c in range(tok // SUB - 1):
                if c > 0:
                    extra = extra * decay_ref[i, 2 + c : 3 + c, :]
                early_ref[i, c] = (others_ref[i, c] + extra).astype(BF16)
    decays = []
    for part in range(per + with_c):
        here = slice(part * CHUNK, (part + 1) * CHUNK)
        if part < per:
            lanes = pl.ds(pl.multiple_of(at + part * CHUNK, CHUNK), CHUNK)
            taps = [taps_x_ref[j : j + 1, lanes] for j in range(taps_len)]
        else:
            lanes = slice(channels + gn, channels + 2 * gn)
            taps = [taps_c_ref[j : j + 1, :] for j in range(taps_len)]
        ext_ref[4:8, :] = tail_ref[:, lanes].astype(F32)
        ext_ref[8:, :] = (x_ref[:, lanes] if part < per else c_ref[...]).astype(F32)

        def emit(low, total):
            value = silu(total).astype(BF16)
            if part < per:
                xc_ref[0, low : low + ROWS, here] = value
            else:
                cc_ref[low : low + ROWS, :] = value

        convolve(ext_ref, mask_ref, taps, emit)
        if part < per:

            def h_put(c, value):
                h_ref[0, c, :, here] = value.astype(BF16)

            state, decay, _ = state_of(
                at + part * CHUNK,
                heads,
                head_dim,
                bt_ref,
                tab_ref,
                d_ref,
                lambda c: xc_ref[0, c * SUB : (c + 1) * SUB, here].astype(F32),
                h_put,
            )
            put_piece(send_ref, part * (CHUNK // LANES), state)
            decays.append(decay)
    put_decay(send_ref, jnp.concatenate(decays, 1))


def late(k, tail, age, tab, d, bc, taps_x, x, with_c=()):
    tok, channels = x.shape
    owned = channels // CLUSTER
    gn = bc.shape[1]
    subs = tok // SUB - 1
    shape = jax.ShapeDtypeStruct
    heads = d.shape[1] // 2
    extra_out = (
        shape((tok, gn), BF16),
        shape((EARLY, subs, STATE, owned), BF16),
        shape((tok, LANES), BF16),
        shape((tok, LANES), F32),
        shape((heads, tok), F32),
    )
    if not with_c:
        extra_out = ()
    return pl.pallas_call(
        functools.partial(late_kernel, k, bool(with_c)),
        out_shape=(
            *extra_out,
            shape((1, tok, owned), BF16),
            shape((1, subs, STATE, owned), BF16),
            piece_shape(owned),
        ),
        in_specs=[VMEM] * 7 + ([VMEM] * (len(with_c) - 1) + [pl.BlockSpec(memory_space=pltpu.SMEM)] if with_c else []),
        out_specs=(VMEM,) * (3 + len(extra_out)),
        scratch_shapes=[
            pltpu.VMEM((STATE, tok), BF16),
            pltpu.VMEM((tok + 8, CHUNK), F32),
            pltpu.VMEM((taps_x.shape[0] - 1, tok, LANES), F32),
        ],
        compiler_params=params(16),
        cost_estimate=cost(tok * owned * 16 + tok * STATE * owned * 4, tok * owned * 8, tok * owned),
        name="own" if with_c else "late",
    )(tail, age, tab, d, bc, taps_x, x, *with_c)


def collect_kernel(*refs):
    *pieces, out_ref = refs
    for k, ref in enumerate(pieces):
        out_ref[k] = ref[...]


def collect(pieces):
    return pl.pallas_call(
        collect_kernel,
        out_shape=jax.ShapeDtypeStruct((len(pieces), *pieces[0].shape), BF16),
        in_specs=[VMEM] * len(pieces),
        out_specs=VMEM,
        compiler_params=params(16),
        cost_estimate=cost(0, 4 * len(pieces) * pieces[0].size),
        name="collect",
    )(*pieces)


def scan_kernel(*refs):
    first_ref, *last, local_ref, pre_ref, total_ref = refs
    pieces = [first_ref.at[k] for k in range(first_ref.shape[0])] + last
    mine = lax.axis_index("seq") % CLUSTER

    def in_order(values):
        bit = 1
        while bit < CLUSTER:
            odd = (mine & bit) != 0
            values = [jnp.where(odd, values[i ^ bit], values[i]) for i in range(CLUSTER)]
            bit *= 2
        return values

    owned = total_ref.shape[1]
    tiles = owned // LANES
    rows = [ref[tiles * STATE :, :].astype(F32) for ref in pieces]
    decays = in_order(
        [jnp.concatenate([row[2 * t : 2 * t + 1] + row[2 * t + 1 : 2 * t + 2] for t in range(tiles)], 1) for row in rows]
    )
    pre = jnp.ones((1, owned), F32)
    for i in range(CLUSTER):
        pre_ref[i] = jnp.broadcast_to(pre, (8, owned))
        pre = pre * decays[i]
    pre_ref[CLUSTER] = jnp.broadcast_to(pre, (8, owned))
    for at in range(0, owned, LANES):
        lanes = slice(at, at + LANES)
        for low in range(0, STATE, 64):
            rows = slice(low, low + 64)
            at_rows = slice(at + low, at + low + 64)
            values = in_order([ref[at_rows, :].astype(F32) for ref in pieces])
            local_ref[0, rows, lanes] = jnp.zeros((64, LANES), F32)
            state = values[0]
            for i in range(1, CLUSTER):
                local_ref[i, rows, lanes] = state
                state = decays[i][:, lanes] * state + values[i]
            total_ref[rows, lanes] = state.astype(BF16)


def scan_blocks(pieces):
    operands = (collect(pieces[: 1 + EARLY]), *pieces[1 + EARLY :])
    owned = pieces[0].shape[0] // (STATE + 2) * LANES
    return pl.pallas_call(
        scan_kernel,
        out_shape=(
            jax.ShapeDtypeStruct((CLUSTER, STATE, owned), F32),
            jax.ShapeDtypeStruct((CLUSTER + 1, 8, owned), F32),
            jax.ShapeDtypeStruct((STATE, owned), BF16),
        ),
        in_specs=[VMEM] * len(operands),
        out_specs=(VMEM,) * 3,
        compiler_params=params(),
        cost_estimate=cost(CLUSTER * STATE * owned * 2, CLUSTER * STATE * owned * 6),
        name="cluster_scan",
    )(*operands)


def join_kernel(before_ref, local_ref, pre_ref, *outs):
    index = lax.axis_index("seq")
    mine = index % CLUSTER
    before = jnp.where(index >= CLUSTER, before_ref[...].astype(F32), 0.0)
    for k in range(CLUSTER):
        block = mine ^ k
        outs[k][...] = (local_ref[block] + pre_ref[block][0:1] * before).astype(BF16)


def join(before, local, pre):
    owned = local.shape[2]
    return pl.pallas_call(
        join_kernel,
        out_shape=(jax.ShapeDtypeStruct((STATE, owned), BF16),) * CLUSTER,
        in_specs=[VMEM] * 3,
        out_specs=(VMEM,) * CLUSTER,
        compiler_params=params(),
        cost_estimate=cost(CLUSTER * STATE * owned * 2, CLUSTER * STATE * owned * 6),
        name="join",
    )(before, local, pre)


def group_at(turn, groups):
    return (lax.axis_index("seq") % CLUSTER) // (CLUSTER // groups) ^ turn


def intra_kernel(pieces, heads, head_dim, *refs):
    bc_ref, cc_ref, tab_ref, col_ref, row_ref, age_ref = refs[:6]
    refs = refs[6:]
    count = len(pieces)
    xs, hs, gates, parts, scales = (refs[i * count : (i + 1) * count] for i in range(5))
    hot_ref, hot0_ref = refs[5 * count :]
    owned = parts[0].shape[1]
    per_piece = owned // head_dim
    mine = lax.axis_index("seq") % CLUSTER

    @pl.when(pl.program_id(0) == 0)
    def _():
        for p, k in enumerate(pieces):
            hot_ref[p] = spread(2 * heads, 4 * heads, (mine ^ k) * per_piece, heads, owned, head_dim)
            hot0_ref[p] = spread(0, 2 * heads, (mine ^ k) * per_piece, heads, owned, head_dim)

    back = lax.broadcasted_iota(jnp.int32, (SUB, SUB), 0) - lax.broadcasted_iota(jnp.int32, (SUB, SUB), 1)
    keep = (back >= 0) & (back <= age_ref[...])
    c_blk = cc_ref[...]
    scores = lax.dot_general(c_blk, bc_ref[...], (((1,), (1,)), ((), ())), preferred_element_type=F32)
    scores = jnp.where(keep, scores, 0.0)
    lane = lax.broadcasted_iota(jnp.int32, (SUB, LANES), 1)
    per_tile = LANES // head_dim
    for p, k in enumerate(pieces):
        first = (mine ^ k) * per_piece
        col = pltpu.roll(col_ref[...], LANES - (2 * heads + first), 1)
        row = row_ref[pl.ds(pl.multiple_of(first, per_piece), per_piece), :]
        for tile in range(owned // LANES):
            lanes = slice(tile * LANES, (tile + 1) * LANES)
            x_tile = xs[p][0, :, lanes].astype(F32)
            left, right = [], []
            for i in range(per_tile):
                head = tile * per_tile + i
                gap = col[:, head : head + 1] + row[head : head + 1, :]
                left.append((jnp.exp2(jnp.minimum(gap, 80.0)) * scores).astype(BF16))
                here = (lane >= i * head_dim) & (lane < (i + 1) * head_dim)
                right.append(jnp.where(here, x_tile, 0.0).astype(BF16))
            inner = mm(jnp.concatenate(left, 1), jnp.concatenate(right, 0))
            inner = inner + mm(c_blk, hs[p][0, 0, :, lanes]) * mm(tab_ref[...], hot_ref[p, :, lanes])
            gate = silu(gates[p][:, lanes].astype(F32))
            parts[p][:, lanes] = inner * gate
            scales[p][:, lanes] = mm(tab_ref[:, : 2 * heads], hot0_ref[p, :, lanes]) * gate


def early_index(k):
    return k - 1 if 1 <= k <= EARLY else 0


def intra(turn, pieces, bc, cc, tab, col, row, age, xs, hs, gate):
    tok, gn = bc.shape
    heads = row.shape[0]
    channels = gate.shape[1]
    head_dim = channels // heads
    groups = gn // STATE
    owned = channels // CLUSTER
    count = len(pieces)
    out = jax.ShapeDtypeStruct((tok, owned), F32)

    def piece_spec(block, index):
        return [pl.BlockSpec(block, functools.partial(index, k)) for k in pieces]

    return pl.pallas_call(
        functools.partial(intra_kernel, pieces, heads, head_dim),
        out_shape=(out,) * (2 * count),
        grid=(tok // SUB,),
        in_specs=[
            pl.BlockSpec((SUB, STATE), lambda i: (i, group_at(turn, groups))),
            pl.BlockSpec((SUB, STATE), lambda i: (i, group_at(turn, groups))),
            pl.BlockSpec((SUB, tab.shape[1]), lambda i: (i, 0)),
            pl.BlockSpec((SUB, LANES), lambda i: (i, 0)),
            pl.BlockSpec((heads, SUB), lambda i: (0, i)),
            pl.BlockSpec((SUB, LANES), lambda i: (i, 0)),
        ]
        + piece_spec((1, SUB, owned), lambda k, i: (early_index(k), i, 0))
        + piece_spec((1, 1, STATE, owned), lambda k, i: (early_index(k), jnp.maximum(i - 1, 0), 0, 0))
        + piece_spec((SUB, owned), lambda k, i: (i, lax.axis_index("seq") % CLUSTER ^ k)),
        out_specs=(pl.BlockSpec((SUB, owned), lambda i: (i, 0)),) * (2 * count),
        scratch_shapes=[pltpu.VMEM((count, 4 * heads, owned), BF16), pltpu.VMEM((count, 2 * heads, owned), BF16)],
        compiler_params=params(16),
        cost_estimate=cost(tok * SUB * owned * count * 4, tok * owned * count * 12, tok * SUB * owned * count // head_dim),
        name="intra",
    )(bc, cc, tab, col, row, age, *xs, *hs, *([gate] * count))


def final_kernel(turn, groups, *refs):
    cc_ref, gain_ref = refs[:2]
    share = CLUSTER // groups
    parts, scales, pieces = (refs[2 + i * share : 2 + (i + 1) * share] for i in range(3))
    out_hbm, y_ref, put_ref, sem = refs[-4:]
    tok, owned = parts[0].shape
    rows = y_ref.shape[1]
    copies = []
    c_lanes = pl.ds(pl.multiple_of(group_at(turn, groups) * STATE, STATE), STATE)
    columns = [pl.ds(place_of(turn * share + i, owned), owned) for i in range(share)]
    for low in range(0, tok, rows):
        span = slice(low, low + rows)
        c_blk = cc_ref[span, c_lanes]
        squares = None
        for i in range(share):
            for at in range(0, owned, CHUNK):
                lanes = slice(at, at + CHUNK)
                value = parts[i][span, lanes] + mm(c_blk, pieces[i][:, lanes]) * scales[i][span, lanes]
                y_ref[i, :, lanes] = value
                square = value * value
                for j in range(0, CHUNK, LANES):
                    piece = square[:, j : j + LANES]
                    squares = piece if squares is None else squares + piece
        factor = lax.rsqrt(jnp.sum(squares, axis=1, keepdims=True) * (1.0 / (share * owned)) + norm_eps)
        for i in range(share):
            put_ref[i, span, :] = (y_ref[i] * factor * gain_ref[:, columns[i]]).astype(BF16)
            copies.append(
                pltpu.make_async_copy(put_ref.at[i, span, :], out_hbm.at[span, columns[i]], sem.at[i, low // rows])
            )
            copies[-1].start()
    wait_all(copies)


def final(turn, cc, gain, parts, scales, pieces, so_far):
    tok, owned = parts[0].shape
    groups = cc.shape[1] // STATE
    share = CLUSTER // groups
    rows = 64
    operands = (cc, gain, *parts, *scales, *pieces) + (() if so_far is None else (so_far,))
    return pl.pallas_call(
        functools.partial(final_kernel, turn, groups),
        out_shape=jax.ShapeDtypeStruct((tok, owned * CLUSTER), BF16),
        in_specs=[VMEM] * (2 + 3 * share) + ([] if so_far is None else [ANY]),
        out_specs=ANY,
        scratch_shapes=[
            pltpu.VMEM((share, rows, owned), F32),
            pltpu.VMEM((share, tok, owned), BF16),
            pltpu.SemaphoreType.DMA((share, tok // rows)),
        ],
        input_output_aliases={} if so_far is None else {len(operands) - 1: 0},
        compiler_params=params(16),
        cost_estimate=cost(tok * STATE * owned * share * 2, tok * owned * share * 8),
        name="final",
    )(*operands)


def moved(value, hop):
    count = lax.axis_size("seq")
    return lax.ppermute(value, "seq", [(i, hop(i)) for i in range(count) if 0 <= hop(i) < count])


def exchanged(pieces, order):
    arrived = {0: pieces[0]}
    for k in order:
        arrived[k] = moved(pieces[k], lambda i, k=k: i ^ k)
    return [arrived[k] for k in range(CLUSTER)]


def before_cluster(total, pre):
    clusters = lax.axis_size("seq") // CLUSTER
    if clusters == 1:
        return jnp.zeros_like(total)
    if clusters == 2:
        return moved(total, lambda i: i ^ CLUSTER)
    shift = lambda value, steps: moved(value, lambda i: i + steps * CLUSTER)
    state, decay = shift((total.astype(F32), pre[CLUSTER, 0]), 1)
    step = 1
    while step < clusters - 1:
        earlier, fell = shift((state, decay), step)
        state, decay = state + decay[None, :] * earlier, decay * fell
        step *= 2
    return state


def tied(values, other):
    *values, _ = lax.optimization_barrier((*values, other))
    return values


def on_device(
    x_input,
    b_input,
    c_input,
    dt_input,
    decay_rate,
    gate_input,
    taps_x,
    taps_b,
    taps_c,
    norm_gain,
    doc_lengths,
):
    groups = b_input.shape[1] // STATE
    count = lax.axis_size("seq")
    pin = lambda value: pltpu.with_memory_space_constraint(value, pltpu.HBM)
    ends = pack(pin(x_input), pin(b_input), pin(c_input))
    tail = lax.ppermute(ends, "seq", [(i, (i + 1) % count) for i in range(count)])
    rates = (dt_input.T, decay_rate[None, :])
    tab, d, age, part_x, part_b, xc, bc = conv(doc_lengths, *rates, x_input, b_input, taps_x, taps_b)
    state, others, decay, weight = states(tab, d, xc, bc)
    xc, bc, extra, *sends = with_head(tail, part_x, part_b, taps_x, taps_b, age, state, decay, weight, xc, bc)
    known = (tail, age, tab, d, bc, taps_x, x_input)
    xs, hs = [None] + [xc] * EARLY, [None] * (1 + EARLY)
    for k in range(1 + EARLY, CLUSTER):
        late_x, late_h, late_send = late(k, *known)
        xs.append(late_x)
        hs.append(late_h)
        sends.append(late_send)
    cc, early_h, inner_tab, col, row, xs[0], hs[0], own_send = late(
        0, *known, (c_input, taps_c, others, extra, decay, *rates, doc_lengths)
    )
    hs[1 : 1 + EARLY] = [early_h] * EARLY
    shared = (bc, cc, inner_tab, col, row)
    share = CLUSTER // groups

    def inner(turn, age):
        pieces = tuple(range(turn * share, (turn + 1) * share))
        return intra(turn, pieces, *shared, age, [xs[k] for k in pieces], [hs[k] for k in pieces], gate_input)

    local, pre, total = scan_blocks(exchanged([own_send, *sends], (1, 2, 3)))
    first = inner(0, *tied([age], total))
    joined = join(*tied([before_cluster(total, pre)], first[0]), local, pre)
    later = [inner(turn, *tied([age], joined[0])) for turn in range(1, groups)]
    entering = exchanged(joined, (2, 1, 3))
    (entering[1],) = tied(entering[1:2], entering[2])
    output = None
    for turn, found in enumerate((first, *later)):
        mine = entering[turn * share : (turn + 1) * share]
        output = final(turn, cc, norm_gain[None, :], found[:share], found[share:], mine, output)
    return output


def solution(mesh):
    rows = P(("groups", "seq"), "dp")
    placed = (rows, rows, rows, rows, P("dp"), rows, P(None, "dp"), P(None, "dp"), P(None, "dp"), P("dp"), P("groups"))
    return jax.shard_map(on_device, mesh=mesh, in_specs=placed, out_specs=rows, check_vma=False)
```
